256 devices in a mesh: row: 16 (over y_hi, x, core), tensor: 16 (over y_lo, z).
Axes of the slice: x: 4, y: 4 (y_hi: 2, y_lo: 2; y = y_hi * 2 + y_lo), z: 8, core: 2. Of those that a mesh axis runs over, the one named last changes fastest.
Arguments:
- latents: bfloat16 [4, 32, 64, 2240], P(None, 'row', None, 'tensor'), may hold values from -6 to 6
- clip_height: int32 [4], replicated, may hold values from 16 to 32, as said below
- clip_width: int32 [4], replicated, may hold values from 32 to 64, as said below
- expand_weight: bfloat16 [2, 2240, 5600], P(None, None, 'tensor'), may hold values from -0.125 to 0.125
- expand_bias: float32 [2, 5600], P(None, 'tensor'), may hold values from -3 to 3
- depth_weight: float32 [3, 3, 2, 5600], P(None, None, None, 'tensor'), may hold values from -2 to 2
- depth_bias: float32 [2, 5600], P(None, 'tensor'), may hold values from -3 to 3
- project_weight: bfloat16 [5600, 2240], P('tensor'), may hold values from -0.109375 to 0.109375
Outputs:
- block_output: bfloat16 [4, 32, 64, 2240], P(None, 'row', None, 'tensor')
The draws below stay inside these ranges and needn't reach their ends.
Inputs may be any that keep to these rules, and one draw needn't show every extreme that they name: `clip_height`: one clip spans all 32 rows and another exactly 16 of them. `clip_width`: one clip spans all 64 columns and another exactly 32 of them.
All inputs are finite; a program needn't handle non-finite values.
Results may differ from the reference program's by a relative error of at most 0.0062.
Values may be sent and summed in bfloat16 or wider, within the bound.
A program may use at most 128 MiB of HBM per device.

```python
import jax
import jax.numpy as jnp
from jax import lax

D = 2240
FF = 5600
BATCH = 4
CW = 64
NH = 32


def bucket_draw(key, upper_bound, item_count):
    levels = jax.random.randint(key, (item_count,), upper_bound // 2, upper_bound + 1)
    ranking = jax.random.permutation(jax.random.fold_in(key, 7), item_count)
    levels = jnp.where(ranking == 0, upper_bound, levels)
    levels = jnp.where(ranking == 1, upper_bound // 2, levels)
    return levels.astype(jnp.int32)


def draw_clip_height(key, part):
    return bucket_draw(jax.random.fold_in(key, 11), NH, BATCH)


def draw_clip_width(key, part):
    return bucket_draw(jax.random.fold_in(key, 13), CW, BATCH)


def with_spikes(result, key, source, target, shards_of, factor):
    def block_of(dim):
        return (jnp.arange(result.shape[dim]) // (result.shape[dim] // shards_of)).reshape((-1,) + (1,) * (result.ndim - 1 - dim))

    near = jax.random.permutation(key, shards_of)[block_of(target)]
    far = (block_of(target) + shards_of // 2) % shards_of
    return jnp.where((block_of(source) == near) | (block_of(source) == far), factor * result, result)


def steps_of(key, extent, shards, least, top_value):
    gain, own = 1.0, jax.random.fold_in(key, 6)
    for dim, shards_of in shards:
        steps = jnp.exp(jax.random.uniform(jax.random.fold_in(own, dim), (shards_of,), jnp.float32, least / len(shards), top_value / len(shards)))
        gain = gain * jnp.repeat(steps, extent[dim] // shards_of).reshape([-1 if axis == dim else 1 for axis in range(len(extent))])
    return gain


def noise(rng, dims, width, limit, pieces=(), kind=jnp.bfloat16):
    level = steps_of(rng, dims, pieces, -0.22, 0.18) if pieces else 1.0
    array = jax.random.normal(rng, dims, jnp.float32) * width * level
    return jnp.minimum(jnp.maximum(array, -limit), limit).astype(kind)


def noise_with(rng, extent, width, bound, split, heavy, kind=jnp.bfloat16):
    result = width * jax.random.normal(rng, extent, jnp.float32)
    if split:
        result = result * steps_of(rng, extent, split, -0.22, 0.18)
    return jnp.clip(with_spikes(result, jax.random.fold_in(rng, 3), *heavy), -bound, bound).astype(kind)


def setup_inputs(seed: int = 0) -> dict:
    splits = jax.random.split(jax.random.key(seed), 9)
    return {
        "latents": noise(splits[0], (BATCH, NH, CW, D), 1.0, 6.0, ((1, 16), (3, 16))),
        "clip_height": draw_clip_height(jax.random.fold_in(splits[8], 71), 0),
        "clip_width": draw_clip_width(jax.random.fold_in(splits[8], 71), 0),
        "expand_weight": noise(splits[3], (2, D, FF), D ** -0.5, 0.125, ((2, 16),)),
        "expand_bias": noise(splits[4], (2, FF), 0.5, 3.0, ((1, 16),), jnp.float32),
        "depth_weight": noise(splits[5], (3, 3, 2, FF), 9 ** -0.5, 2.0, ((3, 16),), jnp.float32),
        "depth_bias": noise(splits[6], (2, FF), 0.5, 3.0, ((1, 16),), jnp.float32),
        "project_weight": noise_with(splits[7], (FF, D), FF ** -0.5, 0.109375, ((0, 16),), (0, 1, 16, 2.0)),
    }


def reference(latents, clip_height, clip_width, expand_weight, expand_bias, depth_weight, depth_bias, project_weight):
    def per_sample(inputs):
        sample, height_limit, width_limit = inputs
        row_ids = jnp.arange(NH, dtype=jnp.int32)
        col_ids = jnp.arange(CW, dtype=jnp.int32)
        valid_mask = ((row_ids[:, None] < height_limit) & (col_ids[None, :] < width_limit)).astype(jnp.float32)[..., None]
        flat = sample.reshape(NH * CW, D)
        halves = [jnp.dot(flat, expand_weight[half], preferred_element_type=jnp.float32).reshape(NH, CW, FF) for half in range(2)]
        pre_act = jnp.stack(halves, axis=2) + expand_bias
        expanded = (jax.nn.silu(pre_act) * valid_mask[..., None]).astype(jnp.bfloat16)
        padded = jnp.pad(expanded, ((1, 1), (1, 1), (0, 0), (0, 0)))
        depth_out = jnp.zeros((NH, CW, 2, FF), jnp.float32) + depth_bias
        for tap_row in range(3):
            for tap_col in range(3):
                depth_out = depth_out + depth_weight[tap_row, tap_col] * padded[tap_row:tap_row + NH, tap_col:tap_col + CW]
        hidden = (depth_out[:, :, 0] * jax.nn.silu(depth_out[:, :, 1])).astype(jnp.bfloat16)
        projected = jnp.dot(hidden.reshape(NH * CW, FF), project_weight, preferred_element_type=jnp.float32).reshape(NH, CW, D)
        return (projected * valid_mask).astype(jnp.bfloat16)

    return lax.map(per_sample, (latents, clip_height, clip_width))
```

```python
import functools

import jax
import jax.numpy as jnp
from jax import lax
from jax.experimental import pallas as pl
from jax.experimental.pallas import tpu as pltpu
from jax.sharding import PartitionSpec as P

MESH = pl.DeviceIdType.MESH
NY, NZ = 2, 8
LANES = 128
BF16 = jnp.bfloat16
F32 = jnp.float32


def ceil_to(n, m):
    return -(-n // m) * m


def silu(v):
    return v / (1.0 + jnp.exp(-v))


def kernel(
    rows,
    ch,
    x_ref,
    height_ref,
    width_ref,
    w_ref,
    cols_ref,
    p_ref,
    out_ref,
    xg,
    ex,
    dn_out,
    up_out,
    dn_in,
    up_in,
    hid,
    zc_out,
    zc_in,
    zw_out,
    zw_in,
    qc_out,
    qc_in,
    qw_out,
    qw_in,
    qy_out,
    qy_in,
    py_out,
    py_in,
    send,
    recv,
):
    r = lax.axis_index("row")
    t = lax.axis_index("tensor")
    y, z = t // NZ, t % NZ
    chp = xg.shape[3]
    ffp = ex.shape[2]
    width = xg.shape[4]
    per_half = width // LANES

    def tz(step):
        return (z + NZ + step) % NZ

    cw = {"tensor": y * NZ + tz(1)}
    ccw = {"tensor": y * NZ + tz(-1)}
    other = {"tensor": (1 - y) * NZ + z}
    above = {"row": (r + rows - 1) % rows}
    below = {"row": (r + 1) % rows}

    barrier = pltpu.get_barrier_semaphore()
    for target in (cw, ccw, other, above, below):
        pl.semaphore_signal(barrier, inc=1, device_id=target, device_id_type=MESH)

    ids = {}

    def copy(key, src, dst, target):
        n = ids.setdefault(key, len(ids))
        return pltpu.make_async_remote_copy(
            src_ref=src,
            dst_ref=dst,
            send_sem=send.at[n],
            recv_sem=recv.at[n],
            device_id=target,
            device_id_type=MESH,
        )

    pending = []

    def start(key, src, dst, target):
        c = copy(key, src, dst, target)
        c.start()
        pending.append(c)
        return c

    def block(half, zz, yy):
        return xg.at[half, zz, yy]

    for half in range(2):
        for b in range(per_half):
            tok = x_ref[half * per_half + b].reshape(LANES, ch)
            xg[half, z, y, 0:ch, b * LANES : (b + 1) * LANES] = tok.T
        xg[half, z, y, ch:chp, :] = jnp.zeros((chp - ch, width), BF16)

    pl.semaphore_wait(barrier, 5)

    y0 = start("y0", block(0, z, y), block(0, z, y), other)
    yq = {0: start("yq0", block(1, z, y), block(1, z, y), other)}
    pc, pw, qc, qw = {}, {}, {}, {}
    pc[0] = [start("pc0a", block(0, z, y), block(0, z, y), cw)]
    pw[0] = [start("pw0a", block(0, z, y), block(0, z, y), ccw)]
    qc[0] = start("qc0", block(1, z, y), block(1, z, y), cw)
    qw[0] = start("qw0", block(1, z, y), block(1, z, y), ccw)
    y0.wait_recv()
    pc[0].append(start("pc0b", block(0, z, 1 - y), block(0, z, 1 - y), cw))
    pw[0].append(start("pw0b", block(0, z, 1 - y), block(0, z, 1 - y), ccw))
    far_c, far_w = NZ // 2, NZ - 1 - NZ // 2
    for s in range(1, far_c + 1):
        for c in pc[s - 1]:
            c.wait_recv()
        if s < far_c:
            zz = tz(-s)
            pc[s] = [start(f"pc{s}", xg.at[0, zz], xg.at[0, zz], cw)]
        if s <= far_w:
            for c in pw[s - 1]:
                c.wait_recv()
            if s < far_w:
                zz = tz(s)
                pw[s] = [start(f"pw{s}", xg.at[0, zz], xg.at[0, zz], ccw)]
        qc[s - 1].wait_recv()
        zz = tz(-s)
        if s < far_c:
            qc[s] = start(f"qc{s}", block(1, zz, y), block(1, zz, y), cw)
        yq[-s] = start(f"yqc{s}", block(1, zz, y), block(1, zz, y), other)
        if s <= far_w:
            qw[s - 1].wait_recv()
            zz = tz(s)
            if s < far_w:
                qw[s] = start(f"qw{s}", block(1, zz, y), block(1, zz, y), ccw)
            yq[s] = start(f"yqw{s}", block(1, zz, y), block(1, zz, y), other)

    lane = lax.broadcasted_iota(jnp.int32, (1, LANES), 1)
    first = lane < LANES // 2
    col = lane % (LANES // 2)
    left_ok = col > 0
    right_ok = col < LANES // 2 - 1

    def valid(clip):
        h = 2 * r + lane // (LANES // 2)
        return (h < height_ref[clip]) & (col < width_ref[clip])

    top_ok = r > 0
    bottom_ok = r < rows - 1
    halo = {}

    def expand(half):
        gathered = xg[half].reshape(NZ * NY * chp, width)
        mask = jnp.concatenate(
            [valid(half * per_half + b).astype(F32) for b in range(per_half)], axis=1
        )
        for k in range(2):
            acc = jnp.dot(w_ref[k], gathered, preferred_element_type=F32)
            acc = silu(acc + cols_ref[:, k : k + 1]) * mask
            ex[half, k] = acc.astype(BF16)

        for b in range(per_half):
            sl = slice(b * LANES, (b + 1) * LANES)
            e0, e1 = ex[half, 0, :, sl].astype(F32), ex[half, 1, :, sl].astype(F32)
            dn_out[half, :, sl] = jnp.where(first, pltpu.roll(e0, LANES // 2, 1), e1).astype(BF16)
            up_out[half, :, sl] = jnp.where(first, e0, pltpu.roll(e1, LANES // 2, 1)).astype(BF16)
        halo[half] = (
            start(f"dn{half}", dn_out.at[half], dn_in.at[half], below),
            start(f"up{half}", up_out.at[half], up_in.at[half], above),
        )

    def conv(half):
        for c in halo[half]:
            c.wait_recv()
        for b in range(per_half):
            sl = slice(b * LANES, (b + 1) * LANES)
            up = jnp.where(top_ok, dn_in[half, :, sl].astype(F32), 0.0)
            dn = jnp.where(bottom_ok, up_in[half, :, sl].astype(F32), 0.0)
            outs = []
            for k in range(2):
                mid = ex[half, k, :, sl].astype(F32)
                turned = pltpu.roll(mid, LANES // 2, 1)
                a = up if k == 0 else pltpu.roll(up, LANES // 2, 1)
                d = pltpu.roll(dn, LANES // 2, 1) if k == 0 else dn
                taps = [jnp.where(first, a, turned), mid, jnp.where(first, turned, d)]
                sums = []
                for j in range(3):
                    total = None
                    for i in range(3):
                        n = 4 + (i * 3 + j) * 2 + k
                        term = cols_ref[:, n : n + 1] * taps[i]
                        total = term if total is None else total + term
                    sums.append(total)
                res = sums[1] + cols_ref[:, 2 + k : 3 + k]
                res = res + jnp.where(left_ok, pltpu.roll(sums[0], 1, 1), 0.0)
                res = res + jnp.where(right_ok, pltpu.roll(sums[2], LANES - 1, 1), 0.0)
                outs.append(res)
            hid[half, :, sl] = (outs[0] * silu(outs[1])).astype(BF16)

    def share(half, zz, yy=None):
        if yy is None:
            w = p_ref[zz].reshape(NY * chp, ffp)
        else:
            w = p_ref[zz, yy]
        return jnp.dot(w, hid[half], preferred_element_type=F32)

    pc[far_c - 1][0]
    expand(0)
    for c in yq.values():
        c.wait_recv()
    expand(1)
    conv(0)

    rc, rw, sc, sw = {}, {}, {}, {}

    def p_step(s):
        if s < far_c:
            total = share(0, tz(far_c - s))
            if s > 0:
                rc[s - 1].wait_recv()
                total = total + zc_in[s - 1].astype(F32)
            zc_out[s] = total.astype(BF16)
            rc[s] = start(f"rc{s}", zc_out.at[s], zc_in.at[s], cw)
        if s < far_w:
            total = share(0, tz(s - far_w))
            if s > 0:
                rw[s - 1].wait_recv()
                total = total + zw_in[s - 1].astype(F32)
            zw_out[s] = total.astype(BF16)
            rw[s] = start(f"rw{s}", zw_out.at[s], zw_in.at[s], ccw)

    p_step(0)
    conv(1)
    order = []
    for s in range(far_c):
        order.append(far_c - s)
        if s < far_w:
            order.append(s - far_w)
    order.append(0)
    qy = {}
    for n, d in enumerate(order):
        qy_out[n] = share(1, tz(d), 1 - y).astype(BF16)
        qy[d] = (n, start(f"qy{n}", qy_out.at[n], qy_in.at[n], other))

    def q_block(d):
        n, c = qy[d]
        total = share(1, tz(d), y)
        c.wait_recv()
        return total + qy_in[n].astype(F32)

    def q_step(s):
        if s < far_c:
            total = q_block(far_c - s)
            if s > 0:
                sc[s - 1].wait_recv()
                total = total + qc_in[s - 1].astype(F32)
            qc_out[s] = total.astype(BF16)
            sc[s] = start(f"sc{s}", qc_out.at[s], qc_in.at[s], cw)
        if s < far_w:
            total = q_block(s - far_w)
            if s > 0:
                sw[s - 1].wait_recv()
                total = total + qw_in[s - 1].astype(F32)
            qw_out[s] = total.astype(BF16)
            sw[s] = start(f"sw{s}", qw_out.at[s], qw_in.at[s], ccw)

    for s in range(far_c):
        q_step(s)
        p_step(s + 1)

    def emit(half, total):
        for b in range(per_half):
            clip = half * per_half + b
            part = total[:, b * LANES : (b + 1) * LANES]
            part = jnp.where(valid(clip), part, 0.0)
            tok = part.T[:, :ch].astype(BF16)
            out_ref[clip] = tok.reshape(out_ref.shape[1:])

    rc[far_c - 1].wait_recv()
    rw[far_w - 1].wait_recv()
    whole = share(0, z, 1 - y)
    py_out[...] = (
        whole
        + zc_in[far_c - 1, pl.ds((1 - y) * chp, chp)].astype(F32)
        + zw_in[far_w - 1, pl.ds((1 - y) * chp, chp)].astype(F32)
    ).astype(BF16)
    last = start("py", py_out, py_in, other)
    mine = (
        share(0, z, y)
        + zc_in[far_c - 1, pl.ds(y * chp, chp)].astype(F32)
        + zw_in[far_w - 1, pl.ds(y * chp, chp)].astype(F32)
    )
    total = q_block(0)
    sc[far_c - 1].wait_recv()
    sw[far_w - 1].wait_recv()
    total = total + qc_in[far_c - 1].astype(F32) + qw_in[far_w - 1].astype(F32)
    emit(1, total)
    last.wait_recv()
    emit(0, mine + py_in[...].astype(F32))
    for c in pending:
        c.wait_send()


def on_device(
    row_devices,
    latents,
    clip_height,
    clip_width,
    expand_weight,
    expand_bias,
    depth_weight,
    depth_bias,
    project_weight,
):
    batch, row_count, col_count, ch = latents.shape
    ff = expand_bias.shape[1]
    assert row_count * col_count == LANES and batch % 2 == 0
    chp, ffp = ceil_to(ch, 16), ceil_to(ff, 16)
    width = batch // 2 * LANES

    w = expand_weight.transpose(0, 2, 1).reshape(2, ff, NY, NZ, ch).transpose(0, 1, 3, 2, 4)
    w = jnp.pad(w, ((0, 0), (0, ffp - ff), (0, 0), (0, 0), (0, chp - ch)))
    w = w.reshape(2, ffp, NZ * NY * chp)
    p = project_weight.reshape(ff, NY, NZ, ch).transpose(2, 1, 3, 0)
    p = jnp.pad(p, ((0, 0), (0, 0), (0, chp - ch), (0, ffp - ff)))
    cols = jnp.concatenate([expand_bias, depth_bias, depth_weight.reshape(18, ff)], axis=0)
    cols = jnp.pad(cols.T, ((0, ffp - ff), (0, 0)))

    far_c, far_w = NZ // 2, NZ - 1 - NZ // 2
    vmem = pl.BlockSpec(memory_space=pltpu.VMEM)
    smem = pl.BlockSpec(memory_space=pltpu.SMEM)
    return pl.pallas_call(
        functools.partial(kernel, row_devices, ch),
        out_shape=jax.ShapeDtypeStruct(latents.shape, BF16),
        in_specs=[vmem, smem, smem, vmem, vmem, vmem],
        out_specs=vmem,
        scratch_shapes=[
            pltpu.VMEM((2, NZ, NY, chp, width), BF16),
            pltpu.VMEM((2, 2, ffp, width), BF16),
        ]
        + [pltpu.VMEM((2, ffp, width), BF16)] * 5
        + [pltpu.VMEM((far_c, NY * chp, width), BF16)] * 2
        + [pltpu.VMEM((far_w, NY * chp, width), BF16)] * 2
        + [pltpu.VMEM((far_c, chp, width), BF16)] * 2
        + [pltpu.VMEM((far_w, chp, width), BF16)] * 2
        + [pltpu.VMEM((NZ, chp, width), BF16)] * 2
        + [pltpu.VMEM((chp, width), BF16)] * 2
        + [pltpu.SemaphoreType.DMA((64,)), pltpu.SemaphoreType.DMA((64,))],
        compiler_params=pltpu.CompilerParams(
            collective_id=0, has_side_effects=True, vmem_limit_bytes=60 * 1024 * 1024
        ),
    )(latents, clip_height, clip_width, w, cols, p)


def solution(mesh):
    in_specs = (
        P(None, "row", None, "tensor"),
        P(),
        P(),
        P(None, None, "tensor"),
        P(None, "tensor"),
        P(None, None, None, "tensor"),
        P(None, "tensor"),
        P("tensor", None),
    )
    return jax.shard_map(
        functools.partial(on_device, mesh.shape["row"]),
        mesh=mesh,
        in_specs=in_specs,
        out_specs=P(None, "row", None, "tensor"),
        check_vma=False,
    )
```

```python
import functools

import jax
import jax.numpy as jnp
from jax import lax
from jax.experimental import pallas as pl
from jax.experimental.pallas import tpu as pltpu
from jax.sharding import PartitionSpec as P

MESH = pl.DeviceIdType.MESH
NY, NZ = 2, 8
LANES = 128
BF16 = jnp.bfloat16
F32 = jnp.float32


def ceil_to(n, m):
    return -(-n // m) * m


def silu(v):
    return v / (1.0 + jnp.exp(-v))


def kernel(
    rows,
    ch,
    x_ref,
    height_ref,
    width_ref,
    w_hbm,
    bias_ref,
    taps_ref,
    shift_ref,
    p_hbm,
    out_ref,
    w_raw,
    w_flat,
    w_ref,
    p_raw,
    p_ref,
    rows_s,
    cols_ref,
    xg,
    ex,
    dn_out,
    up_out,
    dn_in,
    up_in,
    hid,
    zc_out,
    zc_in,
    zw_out,
    zw_in,
    qc_out,
    qc_in,
    qw_out,
    qw_in,
    qy_out,
    qy_in,
    py_out,
    py_in,
    load,
    send,
    recv,
):
    r = lax.axis_index("row")
    t = lax.axis_index("tensor")
    y, z = t // NZ, t % NZ
    ff = bias_ref.shape[1]
    chp = xg.shape[3]
    ffp = ex.shape[2]
    width = xg.shape[4]
    wide = NY * NZ * ch
    per_half = width // LANES

    def tz(step):
        return (z + NZ + step) % NZ

    cw = {"tensor": y * NZ + tz(1)}
    ccw = {"tensor": y * NZ + tz(-1)}
    other = {"tensor": (1 - y) * NZ + z}
    above = {"row": (r + rows - 1) % rows}
    below = {"row": (r + 1) % rows}

    w_load = pltpu.make_async_copy(w_hbm, w_raw.at[pl.ds(0, ff)], load.at[0])
    p_load = pltpu.make_async_copy(p_hbm, p_raw, load.at[1])
    w_load.start()
    p_load.start()

    barrier = pltpu.get_barrier_semaphore()
    for target in (cw, ccw, other, above, below):
        pl.semaphore_signal(barrier, inc=1, device_id=target, device_id_type=MESH)

    ids = {}

    def copy(key, src, dst, target):
        n = ids.setdefault(key, len(ids))
        return pltpu.make_async_remote_copy(
            src_ref=src,
            dst_ref=dst,
            send_sem=send.at[n],
            recv_sem=recv.at[n],
            device_id=target,
            device_id_type=MESH,
        )

    pending = []

    def start(key, src, dst, target):
        c = copy(key, src, dst, target)
        c.start()
        pending.append(c)
        return c

    def block(half, zz, yy):
        return xg.at[half, yy, zz]

    for half in range(2):
        for b in range(per_half):
            tok = x_ref[half * per_half + b].reshape(LANES, ch)
            xg[half, y, z, 0:ch, b * LANES : (b + 1) * LANES] = tok.T
        xg[half, y, z, ch:chp, :] = jnp.zeros((chp - ch, width), BF16)

    pl.semaphore_wait(barrier, 5)

    def flatten_w():
        w_flat[:, wide:] = jnp.zeros((2 * ffp, w_flat.shape[1] - wide), BF16)
        w_load.wait()
        w_raw[ff:ffp] = jnp.zeros((ffp - ff, 2, wide), BF16)

        def body(i, _):
            dst = pl.ds(pl.multiple_of(i * 32, 32), 32)
            w_flat[dst, 0:wide] = w_raw[pl.ds(i * 16, 16)].reshape(32, wide)
            return 0

        lax.fori_loop(0, ffp // 16, body, 0)

    def spread_w():
        for j in range(NY * NZ * chp // LANES):
            c = LANES * j + lax.broadcasted_iota(jnp.int32, (2 * LANES, LANES), 1)
            begin = LANES * j - (chp - ch) * (LANES * j // chp)
            base = begin // LANES * LANES
            p = base + lax.broadcasted_iota(jnp.int32, (2 * LANES, LANES), 0)
            owner = c // chp
            pick = (p == c - (chp - ch) * owner) & (c - chp * owner < ch)
            part = jnp.dot(
                w_flat[:, base : base + 2 * LANES],
                pick.astype(F32).astype(BF16),
                preferred_element_type=F32,
            )
            w_ref[:, LANES * j : LANES * (j + 1)] = part.astype(BF16)

    def split_w():
        to = lax.broadcasted_iota(jnp.int32, (2 * ffp, 2 * ffp), 0)
        at = lax.broadcasted_iota(jnp.int32, (2 * ffp, 2 * ffp), 1)
        pick = at == jnp.where(to < ffp, 2 * to, 2 * (to - ffp) + 1)
        pick = pick.astype(F32).astype(BF16)
        for n in range(NY * NZ * chp // (2 * LANES)):
            sl = slice(2 * LANES * n, 2 * LANES * (n + 1))
            part = jnp.dot(pick, w_ref[:, sl], preferred_element_type=F32)
            w_ref[:, sl] = part.astype(BF16)

    def turn_p():
        p_ref[...] = jnp.zeros_like(p_ref)
        p_load.wait()
        for zz in range(NZ):
            for yy in range(NY):
                o = yy * NZ + zz
                p_ref[zz, yy, 0:ch, 0:ff] = p_raw[:, ch * o : ch * (o + 1)].T

    def turn_columns():
        rows_s[...] = jnp.zeros_like(rows_s)
        rows_s[0:2, 0:ff] = bias_ref[...]
        rows_s[2:4, 0:ff] = shift_ref[...]
        for i in range(3):
            for j in range(3):
                n = 4 + 2 * (3 * i + j)
                rows_s[n : n + 2, 0:ff] = taps_ref[i, j]
        cols_ref[...] = rows_s[...].T[:ffp]

    work = {1: spread_w, 2: split_w, 3: turn_p}

    y0 = start("y0", block(0, z, y), block(0, z, y), other)
    yq = {0: start("yq0", block(1, z, y), block(1, z, y), other)}
    pc, pw, qc, qw = {}, {}, {}, {}
    pc[0] = [start("pc0a", block(0, z, y), block(0, z, y), cw)]
    pw[0] = [start("pw0a", block(0, z, y), block(0, z, y), ccw)]
    qc[0] = start("qc0", block(1, z, y), block(1, z, y), cw)
    qw[0] = start("qw0", block(1, z, y), block(1, z, y), ccw)
    turn_columns()
    flatten_w()
    y0.wait_recv()
    pc[0].append(start("pc0b", block(0, z, 1 - y), block(0, z, 1 - y), cw))
    pw[0].append(start("pw0b", block(0, z, 1 - y), block(0, z, 1 - y), ccw))
    far_c, far_w = NZ // 2, NZ - 1 - NZ // 2
    for s in range(1, far_c + 1):
        for c in pc[s - 1]:
            c.wait_recv()
        if s < far_c:
            zz = tz(-s)
            pc[s] = [start(f"pc{s}", xg.at[0, :, zz], xg.at[0, :, zz], cw)]
        if s <= far_w:
            for c in pw[s - 1]:
                c.wait_recv()
            if s < far_w:
                zz = tz(s)
                pw[s] = [start(f"pw{s}", xg.at[0, :, zz], xg.at[0, :, zz], ccw)]
        qc[s - 1].wait_recv()
        zz = tz(-s)
        if s < far_c:
            qc[s] = start(f"qc{s}", block(1, zz, y), block(1, zz, y), cw)
        yq[-s] = start(f"yqc{s}", block(1, zz, y), block(1, zz, y), other)
        if s <= far_w:
            qw[s - 1].wait_recv()
            zz = tz(s)
            if s < far_w:
                qw[s] = start(f"qw{s}", block(1, zz, y), block(1, zz, y), ccw)
            yq[s] = start(f"yqw{s}", block(1, zz, y), block(1, zz, y), other)
        if s in work:
            work[s]()

    lane = lax.broadcasted_iota(jnp.int32, (1, LANES), 1)
    first = lane < LANES // 2
    col = lane % (LANES // 2)
    left_ok = col > 0
    right_ok = col < LANES // 2 - 1

    def valid(clip):
        h = 2 * r + lane // (LANES // 2)
        return (h < height_ref[clip]) & (col < width_ref[clip])

    top_ok = r > 0
    bottom_ok = r < rows - 1
    halo = {}

    def expand(half):
        gathered = xg[half].reshape(NZ * NY * chp, width)
        mask = jnp.concatenate(
            [valid(half * per_half + b).astype(F32) for b in range(per_half)], axis=1
        )
        for k in range(2):
            acc = jnp.dot(w_ref[k * ffp : (k + 1) * ffp], gathered, preferred_element_type=F32)
            acc = silu(acc + cols_ref[:, k : k + 1]) * mask
            ex[half, k] = acc.astype(BF16)

        for b in range(per_half):
            sl = slice(b * LANES, (b + 1) * LANES)
            e0, e1 = ex[half, 0, :, sl].astype(F32), ex[half, 1, :, sl].astype(F32)
            dn_out[half, :, sl] = jnp.where(first, pltpu.roll(e0, LANES // 2, 1), e1).astype(BF16)
            up_out[half, :, sl] = jnp.where(first, e0, pltpu.roll(e1, LANES // 2, 1)).astype(BF16)
        halo[half] = (
            start(f"dn{half}", dn_out.at[half], dn_in.at[half], below),
            start(f"up{half}", up_out.at[half], up_in.at[half], above),
        )

    def conv(half):
        for c in halo[half]:
            c.wait_recv()
        for b in range(per_half):
            sl = slice(b * LANES, (b + 1) * LANES)
            up = jnp.where(top_ok, dn_in[half, :, sl].astype(F32), 0.0)
            dn = jnp.where(bottom_ok, up_in[half, :, sl].astype(F32), 0.0)
            outs = []
            for k in range(2):
                mid = ex[half, k, :, sl].astype(F32)
                turned = pltpu.roll(mid, LANES // 2, 1)
                a = up if k == 0 else pltpu.roll(up, LANES // 2, 1)
                d = pltpu.roll(dn, LANES // 2, 1) if k == 0 else dn
                taps = [jnp.where(first, a, turned), mid, jnp.where(first, turned, d)]
                sums = []
                for j in range(3):
                    total = None
                    for i in range(3):
                        n = 4 + (i * 3 + j) * 2 + k
                        term = cols_ref[:, n : n + 1] * taps[i]
                        total = term if total is None else total + term
                    sums.append(total)
                res = sums[1] + cols_ref[:, 2 + k : 3 + k]
                res = res + jnp.where(left_ok, pltpu.roll(sums[0], 1, 1), 0.0)
                res = res + jnp.where(right_ok, pltpu.roll(sums[2], LANES - 1, 1), 0.0)
                outs.append(res)
            hid[half, :, sl] = (outs[0] * silu(outs[1])).astype(BF16)

    def share(half, zz, yy=None):
        if yy is None:
            w = p_ref[zz].reshape(NY * chp, ffp)
        else:
            w = p_ref[zz, yy]
        return jnp.dot(w, hid[half], preferred_element_type=F32)

    pc[far_c - 1][0]
    expand(0)
    for c in yq.values():
        c.wait_recv()
    expand(1)
    conv(0)

    rc, rw, sc, sw = {}, {}, {}, {}

    def p_step(s):
        if s < far_c:
            total = share(0, tz(far_c - s))
            if s > 0:
                rc[s - 1].wait_recv()
                total = total + zc_in[s - 1].astype(F32)
            zc_out[s] = total.astype(BF16)
            rc[s] = start(f"rc{s}", zc_out.at[s], zc_in.at[s], cw)
        if s < far_w:
            total = share(0, tz(s - far_w))
            if s > 0:
                rw[s - 1].wait_recv()
                total = total + zw_in[s - 1].astype(F32)
            zw_out[s] = total.astype(BF16)
            rw[s] = start(f"rw{s}", zw_out.at[s], zw_in.at[s], ccw)

    p_step(0)
    conv(1)
    order = []
    for s in range(far_c):
        order.append(far_c - s)
        if s < far_w:
            order.append(s - far_w)
    order.append(0)
    qy = {}
    for n, d in enumerate(order):
        qy_out[n] = share(1, tz(d), 1 - y).astype(BF16)
        qy[d] = (n, start(f"qy{n}", qy_out.at[n], qy_in.at[n], other))

    def q_block(d):
        n, c = qy[d]
        total = share(1, tz(d), y)
        c.wait_recv()
        return total + qy_in[n].astype(F32)

    def q_step(s):
        if s < far_c:
            total = q_block(far_c - s)
            if s > 0:
                sc[s - 1].wait_recv()
                total = total + qc_in[s - 1].astype(F32)
            qc_out[s] = total.astype(BF16)
            sc[s] = start(f"sc{s}", qc_out.at[s], qc_in.at[s], cw)
        if s < far_w:
            total = q_block(s - far_w)
            if s > 0:
                sw[s - 1].wait_recv()
                total = total + qw_in[s - 1].astype(F32)
            qw_out[s] = total.astype(BF16)
            sw[s] = start(f"sw{s}", qw_out.at[s], qw_in.at[s], ccw)

    for s in range(far_c):
        q_step(s)
        p_step(s + 1)

    def emit(half, total):
        for b in range(per_half):
            clip = half * per_half + b
            part = total[:, b * LANES : (b + 1) * LANES]
            part = jnp.where(valid(clip), part, 0.0)
            tok = part.T[:, :ch].astype(BF16)
            out_ref[clip] = tok.reshape(out_ref.shape[1:])

    rc[far_c - 1].wait_recv()
    rw[far_w - 1].wait_recv()
    whole = share(0, z, 1 - y)
    py_out[...] = (
        whole
        + zc_in[far_c - 1, pl.ds((1 - y) * chp, chp)].astype(F32)
        + zw_in[far_w - 1, pl.ds((1 - y) * chp, chp)].astype(F32)
    ).astype(BF16)
    last = start("py", py_out, py_in, other)
    mine = (
        share(0, z, y)
        + zc_in[far_c - 1, pl.ds(y * chp, chp)].astype(F32)
        + zw_in[far_w - 1, pl.ds(y * chp, chp)].astype(F32)
    )
    total = q_block(0)
    sc[far_c - 1].wait_recv()
    sw[far_w - 1].wait_recv()
    total = total + qc_in[far_c - 1].astype(F32) + qw_in[far_w - 1].astype(F32)
    emit(1, total)
    last.wait_recv()
    emit(0, mine + py_in[...].astype(F32))
    for c in pending:
        c.wait_send()


def on_device(
    row_devices,
    latents,
    clip_height,
    clip_width,
    expand_weight,
    expand_bias,
    depth_weight,
    depth_bias,
    project_weight,
):
    batch, row_count, col_count, ch = latents.shape
    ff = expand_bias.shape[1]
    assert row_count * col_count == LANES and batch % 2 == 0
    chp, ffp = ceil_to(ch, 16), ceil_to(ff, 16)
    width = batch // 2 * LANES

    far_c, far_w = NZ // 2, NZ - 1 - NZ // 2
    vmem = pl.BlockSpec(memory_space=pltpu.VMEM)
    hbm = pl.BlockSpec(memory_space=pl.ANY)
    flat = ceil_to(NY * NZ * chp, LANES) + LANES
    smem = pl.BlockSpec(memory_space=pltpu.SMEM)
    return pl.pallas_call(
        functools.partial(kernel, row_devices, ch),
        out_shape=jax.ShapeDtypeStruct(latents.shape, BF16),
        in_specs=[vmem, smem, smem, hbm, vmem, vmem, vmem, hbm],
        out_specs=vmem,
        scratch_shapes=[
            pltpu.VMEM((ffp, 2, NY * NZ * ch), BF16),
            pltpu.VMEM((2 * ffp, flat), BF16),
            pltpu.VMEM((2 * ffp, NY * NZ * chp), BF16),
            pltpu.VMEM((ff, NY * NZ * ch), BF16),
            pltpu.VMEM((NZ, NY, chp, ffp), BF16),
            pltpu.VMEM((LANES, ceil_to(ffp, LANES)), F32),
            pltpu.VMEM((ffp, LANES), F32),
            pltpu.VMEM((2, NY, NZ, chp, width), BF16),
            pltpu.VMEM((2, 2, ffp, width), BF16),
        ]
        + [pltpu.VMEM((2, ffp, width), BF16)] * 5
        + [pltpu.VMEM((far_c, NY * chp, width), BF16)] * 2
        + [pltpu.VMEM((far_w, NY * chp, width), BF16)] * 2
        + [pltpu.VMEM((far_c, chp, width), BF16)] * 2
        + [pltpu.VMEM((far_w, chp, width), BF16)] * 2
        + [pltpu.VMEM((NZ, chp, width), BF16)] * 2
        + [pltpu.VMEM((chp, width), BF16)] * 2
        + [pltpu.SemaphoreType.DMA((2,)), pltpu.SemaphoreType.DMA((64,)), pltpu.SemaphoreType.DMA((64,))],
        compiler_params=pltpu.CompilerParams(
            collective_id=0, has_side_effects=True, vmem_limit_bytes=60 * 1024 * 1024
        ),
    )(
        latents,
        clip_height,
        clip_width,
        expand_weight.transpose(2, 0, 1),
        expand_bias,
        depth_weight,
        depth_bias,
        project_weight,
    )


def solution(mesh):
    in_specs = (
        P(None, "row", None, "tensor"),
        P(),
        P(),
        P(None, None, "tensor"),
        P(None, "tensor"),
        P(None, None, None, "tensor"),
        P(None, "tensor"),
        P("tensor", None),
    )
    return jax.shard_map(
        functools.partial(on_device, mesh.shape["row"]),
        mesh=mesh,
        in_specs=in_specs,
        out_specs=P(None, "row", None, "tensor"),
        check_vma=False,
    )
```

```python
import functools

import jax
import jax.numpy as jnp
from jax import lax
from jax.experimental import pallas as pl
from jax.experimental.pallas import tpu as pltpu
from jax.sharding import PartitionSpec as P

MESH = pl.DeviceIdType.MESH
NY, NZ = 2, 8
FAR = NZ // 2
LANES = 128
HALF = LANES // 2
PAIR = 2 * LANES
BF16 = jnp.bfloat16
F32 = jnp.float32
NEAR_ORDER = (4, 3, -3, 2, -2, 1, -1, 0)


def ceil_to(n, m):
    return -(-n // m) * m


def silu(v):
    return v / (1.0 + jnp.exp(-v))


def iota(shape, dim):
    return lax.broadcasted_iota(jnp.int32, shape, dim)


def one_hot(cond):
    return jnp.where(cond, 1.0, 0.0).astype(BF16)


def across(a, b):
    return lax.dot_general(a, b, (((1,), (1,)), ((), ())), preferred_element_type=F32)


def kernel(
    rows,
    x_ref,
    height_ref,
    width_ref,
    w_hbm,
    bias_ref,
    taps_ref,
    shift_ref,
    p_hbm,
    out_ref,
    w_raw,
    w_flat,
    w_ref,
    p_raw,
    p_ref,
    rows_s,
    cols_s,
    taps_s,
    place,
    spot,
    xp_full,
    xp_half,
    xq,
    hx_out,
    hx_in,
    ec,
    ex,
    dn_out,
    up_out,
    dn_in,
    up_in,
    hid,
    hc,
    part,
    pf_out,
    pf_in,
    ph_out,
    ph_in,
    qz_out,
    qz_in,
    qy_out,
    qy_in,
    py_out,
    py_in,
    load,
    send,
    recv,
):
    r = lax.axis_index("row")
    t = lax.axis_index("tensor")
    y, z = t // NZ, t % NZ
    clips, row_count, col_count, ch = x_ref.shape
    ff, ffp, chp = bias_ref.shape[1], ex.shape[1], xq.shape[3]
    wide, spread = NY * NZ * ch, NY * NZ * chp
    cut = ceil_to(chp // 2, 16)

    def tz(step):
        return (z + NZ + step) % NZ

    ring = ({"tensor": y * NZ + tz(1)}, {"tensor": y * NZ + tz(-1)})
    other = {"tensor": (1 - y) * NZ + z}
    above = {"row": (r + rows - 1) % rows}
    below = {"row": (r + 1) % rows}

    w_load = pltpu.make_async_copy(w_hbm, w_raw.at[pl.ds(0, ff)], load.at[0])
    p_load = pltpu.make_async_copy(p_hbm, p_raw, load.at[1])
    w_load.start()
    p_load.start()

    barrier = pltpu.get_barrier_semaphore()
    for target in ring + (other, above, below):
        pl.semaphore_signal(barrier, inc=1, device_id=target, device_id_type=MESH)

    pending = {}

    def start(key, src, dst, target):
        n = len(pending)
        c = pltpu.make_async_remote_copy(
            src_ref=src,
            dst_ref=dst,
            send_sem=send.at[n],
            recv_sem=recv.at[n],
            device_id=target,
            device_id_type=MESH,
        )
        c.start()
        pending[key] = c

    def same(key, ref, target):
        start(key, ref, ref, target)

    def arrived(*key):
        pending[key].wait_recv()

    widths = [width_ref[b] for b in range(clips)]
    heights = [height_ref[b] for b in range(clips)]
    narrow = jnp.int32(clips - 1)
    for b in reversed(range(clips - 1)):
        narrow = jnp.where(widths[b] == col_count // 2, b, narrow)
    slots = [jnp.where(narrow == b, clips - 1, jnp.where(narrow < b, b - 1, b)) for b in range(clips)]

    def of_slot(s, values):
        total = jnp.int32(0)
        for b in range(clips):
            total = total + jnp.where(slots[b] == s, values[b], 0)
        return total

    slot_w = [of_slot(s, widths) for s in range(clips)]
    slot_h = [of_slot(s, heights) for s in range(clips)]

    sub, lane2 = iota((LANES, PAIR), 0), iota((LANES, PAIR), 1)
    sub_row, sub_col = sub // HALF, sub % HALF
    canvas_row = row_count * r + sub_row

    def make_place():
        for g in range(2):
            for b in range(clips):
                limit = jnp.where(slots[b] // 2 == g, widths[b], 0)
                first_slot = jnp.where(slots[b] == 2 * g + 1, 2 * slot_w[2 * g], 0)
                a = first_slot + sub_row * widths[b] + sub_col
                if g == 1:
                    a = jnp.where(a < HALF, a + HALF * y, a + HALF)
                ok = (sub_col < limit) & (canvas_row < heights[b])
                place[g, b * LANES : (b + 1) * LANES] = one_hot(ok & (lane2 == a))

    def make_spot():
        for g in range(2):
            for s in range(2):
                w, h = slot_w[2 * g + s], slot_h[2 * g + s]
                a = s * 2 * slot_w[2 * g] + sub_row * w + sub_col
                ok = (sub_col < w) & (canvas_row < h)
                if g == 0:
                    hit = lane2 == a
                else:
                    hit = (lane2 == a + HALF) | ((a < HALF) & (lane2 == a))
                spot[g, s * LANES : (s + 1) * LANES] = one_hot(ok & hit)

    make_place()
    tokens = x_ref[...].reshape(clips * LANES, ch).T
    for g in range(2):
        block = jnp.dot(tokens, place[g], preferred_element_type=F32).astype(BF16)
        empty = jnp.zeros((chp - ch, LANES), BF16)
        if g == 0:
            xp_full[y, z, 0:ch] = block[:, :LANES]
            xp_full[y, z, ch:chp] = empty
        else:
            hx_out[0:ch] = block[:, :LANES]
            hx_out[ch:chp] = empty
        xq[g, y, z, 0:ch] = block[:, LANES:]
        xq[g, y, z, ch:chp] = empty

    pl.semaphore_wait(barrier, 5)

    def gather_begin(g):
        if g == 0:
            same((g, "y"), xp_full.at[y, z], other)
            for d in range(2):
                same((g, "own", d), xp_full.at[y, z], ring[d])
        else:
            start((g, "y"), hx_out, hx_in, other)
        for d in range(2):
            same((g, "q", d, 0), xq.at[g, y, z], ring[d])
        same((g, "qy", 0), xq.at[g, y, z], other)

    def gather_pair(g):
        arrived(g, "y")
        if g == 0:
            for d in range(2):
                same((g, "p", d, 0), xp_full.at[1 - y, z], ring[d])
        else:
            xp_half[z] = hx_out[...] + hx_in[...]
            for d in range(2):
                same((g, "p", d, 0), xp_half.at[z], ring[d])

    def gather_step(g, s):
        for d in range(2):
            zz = tz(-s if d == 0 else s)
            arrived(g, "p", d, s - 1)
            if g == 0:
                if s == 1:
                    arrived(g, "own", d)
                if s < FAR - 1:
                    same((g, "p", d, s), xp_full.at[:, zz], ring[d])
                elif s < FAR:
                    same((g, "p", d, s), xp_full.at[d, zz], ring[d])
            else:
                if s < FAR - 1:
                    same((g, "p", d, s), xp_half.at[zz], ring[d])
                elif s < FAR:
                    at = pl.ds(0, cut) if d == 0 else pl.ds(cut, chp - cut)
                    same((g, "p", d, s), xp_half.at[zz, at], ring[d])
            arrived(g, "q", d, s - 1)
            if s < FAR - 1:
                same((g, "q", d, s), xq.at[g, y, zz], ring[d])
            elif s < FAR:
                at = pl.ds(0, cut) if d == 0 else pl.ds(cut, chp - cut)
                same((g, "q", d, s), xq.at[g, y, zz, at], ring[d])
            if s < FAR:
                same((g, "qy", -s if d == 0 else s), xq.at[g, y, zz], other)
        if s == FAR:
            same((g, "qy", FAR), xq.at[g, y, tz(FAR)], other)

    def flatten_w():
        w_flat[:, wide:] = jnp.zeros((2 * ffp, w_flat.shape[1] - wide), BF16)
        w_load.wait()
        w_raw[ff:ffp] = jnp.zeros((ffp - ff, 2, wide), BF16)

        def body(i, _):
            dst = pl.ds(pl.multiple_of(i * 32, 32), 32)
            w_flat[dst, 0:wide] = w_raw[pl.ds(i * 16, 16)].reshape(32, wide)
            return 0

        lax.fori_loop(0, ffp // 16, body, 0)

    def spread_w():
        for j in range(spread // LANES):
            c = LANES * j + iota((PAIR, LANES), 1)
            begin = LANES * j - (chp - ch) * (LANES * j // chp)
            base = begin // LANES * LANES
            p = base + iota((PAIR, LANES), 0)
            owner = c // chp
            pick = one_hot((p == c - (chp - ch) * owner) & (c - chp * owner < ch))
            moved = jnp.dot(w_flat[:, base : base + PAIR], pick, preferred_element_type=F32)
            w_ref[:, LANES * j : LANES * (j + 1)] = moved.astype(BF16)

    def split_w():
        to, at = iota((2 * ffp, 2 * ffp), 0), iota((2 * ffp, 2 * ffp), 1)
        pick = one_hot(at == jnp.where(to < ffp, 2 * to, 2 * (to - ffp) + 1))
        for n in range(spread // PAIR):
            sl = slice(PAIR * n, PAIR * (n + 1))
            w_ref[:, sl] = jnp.dot(pick, w_ref[:, sl], preferred_element_type=F32).astype(BF16)

    def turn_p():
        p_ref[...] = jnp.zeros_like(p_ref)
        p_load.wait()
        for zz in range(NZ):
            for yy in range(NY):
                o = yy * NZ + zz
                p_ref[zz, yy, 0:ch, 0:ff] = p_raw[:, ch * o : ch * (o + 1)].T

    def turn_columns():
        rows_s[...] = jnp.zeros_like(rows_s)
        rows_s[0:2, 0:ff] = bias_ref[...]
        rows_s[2:4, 0:ff] = shift_ref[...]
        for i in range(3):
            for j in range(3):
                n = 4 + 2 * (3 * i + j)
                rows_s[n : n + 2, 0:ff] = taps_ref[i, j]
        cols_s[...] = rows_s[...].T[:ffp]
        for n in range(taps_s.shape[0]):
            taps_s[n] = jnp.broadcast_to(cols_s[:, n : n + 1], (ffp, LANES))

    lane = iota((1, LANES), 1)
    first = lane < HALF
    col = lane % HALF
    left_ok = col > 0
    right_ok = col < HALF - 1
    top_ok = r > 0
    bottom_ok = r < rows - 1

    def expand_p(g):
        if g == 0:
            x = xp_full[...].reshape(spread, LANES)
            pre = jnp.dot(w_ref[...], x, preferred_element_type=F32)
        else:
            x = xp_half[...].reshape(spread // 2, LANES)
            pre = jnp.dot(w_ref[:, : spread // 2], x, preferred_element_type=F32)
            more = jnp.dot(w_ref[:, spread // 2 :], x, preferred_element_type=F32)
            pre = jnp.where(first, pre + pltpu.roll(more, HALF, 1), 0.0)
        for k in range(2):
            value = silu(pre[k * ffp : (k + 1) * ffp] + taps_s[k])
            if g == 1:
                value = jnp.where(first, value, 0.0)
            ec[k * ffp : (k + 1) * ffp, :LANES] = value.astype(BF16)

    def expand_q(g):
        x = xq[g].reshape(spread, LANES)
        pre = jnp.dot(w_ref[...], x, preferred_element_type=F32)
        for k in range(2):
            value = silu(pre[k * ffp : (k + 1) * ffp] + taps_s[k])
            ec[k * ffp : (k + 1) * ffp, LANES:] = value.astype(BF16)

    def restore(g):
        for k in range(2):
            ex[k] = across(ec[k * ffp : (k + 1) * ffp], spot[g])

        def body(i, _):
            at = pl.ds(pl.multiple_of(i * 16, 16), 16)
            for s in range(2):
                sl = slice(s * LANES, (s + 1) * LANES)
                e0, e1 = ex[0, at, sl], ex[1, at, sl]
                dn_out[g, at, sl] = jnp.where(first, pltpu.roll(e0, HALF, 1), e1).astype(BF16)
                up_out[g, at, sl] = jnp.where(first, e0, pltpu.roll(e1, HALF, 1)).astype(BF16)
            return 0

        lax.fori_loop(0, ffp // 16, body, 0)
        start((g, "dn"), dn_out.at[g], dn_in.at[g], below)
        start((g, "up"), up_out.at[g], up_in.at[g], above)

    def convolve(g):
        arrived(g, "dn")
        arrived(g, "up")

        def body(i, _):
            at = pl.ds(pl.multiple_of(i * 16, 16), 16)
            for s in range(2):
                sl = slice(s * LANES, (s + 1) * LANES)
                up = jnp.where(top_ok, dn_in[g, at, sl].astype(F32), 0.0)
                dn = jnp.where(bottom_ok, up_in[g, at, sl].astype(F32), 0.0)
                outs = []
                for k in range(2):
                    mid = ex[k, at, sl]
                    turned = pltpu.roll(mid, HALF, 1)
                    a = up if k == 0 else pltpu.roll(up, HALF, 1)
                    d = pltpu.roll(dn, HALF, 1) if k == 0 else dn
                    seen = [jnp.where(first, a, turned), mid, jnp.where(first, turned, d)]
                    sums = []
                    for j in range(3):
                        n = 4 + 2 * j + k
                        total = taps_s[n, at] * seen[0] + taps_s[n + 6, at] * seen[1]
                        sums.append(total + taps_s[n + 12, at] * seen[2])
                    res = sums[1] + taps_s[2 + k, at]
                    res = res + jnp.where(left_ok, pltpu.roll(sums[0], 1, 1), 0.0)
                    res = res + jnp.where(right_ok, pltpu.roll(sums[2], LANES - 1, 1), 0.0)
                    outs.append(res)
                hid[at, sl] = (outs[0] * silu(outs[1])).astype(BF16)
            return 0

        lax.fori_loop(0, ffp // 16, body, 0)

    def project(g):
        hc[...] = jnp.dot(hid[...], spot[g], preferred_element_type=F32).astype(BF16)
        p = p_ref[...].reshape(spread, ffp)
        part[g] = jnp.dot(p, hc[...], preferred_element_type=F32).reshape(NZ, NY, chp, PAIR)

    def scatter_begin(g):
        for n, d in enumerate(NEAR_ORDER):
            qy_out[g, n] = part[g, tz(d), 1 - y, :, LANES:].astype(BF16)
            start((g, "ry", d), qy_out.at[g, n], qy_in.at[g, n], other)

    def scatter_p(g, s):
        for d in range(2):
            zz = tz(FAR - s if d == 0 else s - FAR)
            if s > 0:
                arrived(g, "rp", d, s - 1)
            if g == 0:
                for yy in range(NY):
                    if s == 0 and yy != d:
                        continue
                    total = part[g, zz, yy, :, :LANES]
                    if s > 1 or (s == 1 and yy == d):
                        total = total + pf_in[d, s - 1, yy].astype(F32)
                    pf_out[d, s, yy] = total.astype(BF16)
                if s == 0:
                    src, dst = pf_out.at[d, s, d], pf_in.at[d, s, d]
                else:
                    src, dst = pf_out.at[d, s], pf_in.at[d, s]
            else:
                near = slice(0, cut) if d == 0 else slice(cut, chp)
                rest = slice(cut, chp) if d == 0 else slice(0, cut)
                for at in (near, rest):
                    if s == 0 and at is rest:
                        continue
                    total = jnp.where(first, part[g, zz, 0, at, :LANES], part[g, zz, 1, at, :LANES])
                    if s > 1 or (s == 1 and at is near):
                        total = total + ph_in[d, s - 1, at].astype(F32)
                    ph_out[d, s, at] = total.astype(BF16)
                if s == 0:
                    src, dst = ph_out.at[d, s, near], ph_in.at[d, s, near]
                else:
                    src, dst = ph_out.at[d, s], ph_in.at[d, s]
            start((g, "rp", d, s), src, dst, ring[d])

    def scatter_q(g, s):
        for d in range(2):
            step = FAR - s if d == 0 else s - FAR
            step = FAR if step == -FAR else step
            n = NEAR_ORDER.index(step)
            if s > 0 or d == 0:
                arrived(g, "ry", step)
            if s > 0:
                arrived(g, "rq", d, s - 1)
            near = slice(0, cut) if d == 0 else slice(cut, chp)
            rest = slice(cut, chp) if d == 0 else slice(0, cut)
            for at in (near, rest):
                if s == 0 and at is rest:
                    continue
                total = part[g, tz(step), y, at, LANES:] + qy_in[g, n, at].astype(F32)
                if s > 1 or (s == 1 and at is near):
                    total = total + qz_in[g, d, s - 1, at].astype(F32)
                qz_out[g, d, s, at] = total.astype(BF16)
            if s == 0:
                src, dst = qz_out.at[g, d, s, near], qz_in.at[g, d, s, near]
            else:
                src, dst = qz_out.at[g, d, s], qz_in.at[g, d, s]
            start((g, "rq", d, s), src, dst, ring[d])

    last = FAR - 1

    def scatter_pair(g):
        for d in range(2):
            arrived(g, "rp", d, last)
        if g == 0:
            total = part[g, z, 1 - y, :, :LANES]
            total = total + pf_in[0, last, 1 - y].astype(F32) + pf_in[1, last, 1 - y].astype(F32)
            py_out[g] = total.astype(BF16)
        else:
            py_out[g] = half_sum(1).astype(BF16)
        start((g, "py"), py_out.at[g], py_in.at[g], other)

    def half_sum(g):
        total = jnp.where(first, part[g, z, 0, :, :LANES], part[g, z, 1, :, :LANES])
        return total + ph_in[0, last].astype(F32) + ph_in[1, last].astype(F32)

    def finish_q(g):
        for d in range(2):
            arrived(g, "rq", d, last)
        arrived(g, "ry", 0)
        n = NEAR_ORDER.index(0)
        total = part[g, z, y, :, LANES:] + qy_in[g, n].astype(F32)
        return total + qz_in[g, 0, last].astype(F32) + qz_in[g, 1, last].astype(F32)

    def finish_p(g):
        if g == 0:
            total = part[g, z, y, :, :LANES]
            total = total + pf_in[0, last, y].astype(F32) + pf_in[1, last, y].astype(F32)
        else:
            total = half_sum(1)
        arrived(g, "py")
        return total + py_in[g].astype(F32)

    def restored(g):
        q = finish_q(g).astype(BF16)
        p = finish_p(g).astype(BF16)
        return across(place[g, :, :LANES], p) + across(place[g, :, LANES:], q)

    gather_begin(0)
    turn_columns()
    gather_pair(0)
    flatten_w()
    gather_step(0, 1)
    gather_begin(1)
    spread_w()
    gather_step(0, 2)
    gather_pair(1)
    split_w()
    gather_step(0, 3)
    gather_step(1, 1)
    make_spot()
    gather_step(0, 4)
    gather_step(1, 2)
    expand_p(0)
    for d in NEAR_ORDER:
        arrived(0, "qy", d)
    expand_q(0)
    restore(0)
    gather_step(1, 3)
    turn_p()
    gather_step(1, 4)
    convolve(0)
    project(0)
    scatter_begin(0)
    scatter_p(0, 0)
    scatter_q(0, 0)
    expand_p(1)
    for d in NEAR_ORDER:
        arrived(1, "qy", d)
    expand_q(1)
    scatter_p(0, 1)
    scatter_q(0, 1)
    restore(1)
    scatter_p(0, 2)
    scatter_q(0, 2)
    convolve(1)
    project(1)
    scatter_begin(1)
    scatter_p(1, 0)
    scatter_p(0, 3)
    scatter_q(0, 3)
    scatter_q(1, 0)
    scatter_p(1, 1)
    scatter_q(1, 1)
    scatter_pair(0)
    scatter_p(1, 2)
    scatter_q(1, 2)
    acc = restored(0)
    scatter_p(1, 3)
    scatter_q(1, 3)
    scatter_pair(1)
    acc = acc + restored(1)
    out_ref[...] = acc[:, :ch].astype(BF16).reshape(out_ref.shape)
    for c in pending.values():
        c.wait_send()


def on_device(
    row_devices,
    latents,
    clip_height,
    clip_width,
    expand_weight,
    expand_bias,
    depth_weight,
    depth_bias,
    project_weight,
):
    batch, row_count, col_count, ch = latents.shape
    ff = expand_bias.shape[1]
    assert batch == 4 and row_count == 2 and col_count == HALF
    chp, ffp = ceil_to(ch, 16), ceil_to(ff, 16)
    spread = NY * NZ * chp

    vmem = pl.BlockSpec(memory_space=pltpu.VMEM)
    smem = pl.BlockSpec(memory_space=pltpu.SMEM)
    hbm = pl.BlockSpec(memory_space=pl.ANY)
    scratch = [
        pltpu.VMEM((ffp, 2, NY * NZ * ch), BF16),
        pltpu.VMEM((2 * ffp, spread + LANES), BF16),
        pltpu.VMEM((2 * ffp, spread), BF16),
        pltpu.VMEM((ff, NY * NZ * ch), BF16),
        pltpu.VMEM((NZ, NY, chp, ffp), BF16),
        pltpu.VMEM((LANES, ceil_to(ffp, LANES)), F32),
        pltpu.VMEM((ffp, LANES), F32),
        pltpu.VMEM((22, ffp, LANES), F32),
        pltpu.VMEM((2, batch * LANES, PAIR), BF16),
        pltpu.VMEM((2, PAIR, PAIR), BF16),
        pltpu.VMEM((NY, NZ, chp, LANES), BF16),
        pltpu.VMEM((NZ, chp, LANES), BF16),
        pltpu.VMEM((2, NY, NZ, chp, LANES), BF16),
        pltpu.VMEM((chp, LANES), BF16),
        pltpu.VMEM((chp, LANES), BF16),
        pltpu.VMEM((2 * ffp, PAIR), BF16),
        pltpu.VMEM((2, ffp, PAIR), F32),
        pltpu.VMEM((2, ffp, PAIR), BF16),
        pltpu.VMEM((2, ffp, PAIR), BF16),
        pltpu.VMEM((2, ffp, PAIR), BF16),
        pltpu.VMEM((2, ffp, PAIR), BF16),
        pltpu.VMEM((ffp, PAIR), BF16),
        pltpu.VMEM((ffp, PAIR), BF16),
        pltpu.VMEM((2, NZ, NY, chp, PAIR), F32),
        pltpu.VMEM((2, FAR, NY, chp, LANES), BF16),
        pltpu.VMEM((2, FAR, NY, chp, LANES), BF16),
        pltpu.VMEM((2, FAR, chp, LANES), BF16),
        pltpu.VMEM((2, FAR, chp, LANES), BF16),
        pltpu.VMEM((2, 2, FAR, chp, LANES), BF16),
        pltpu.VMEM((2, 2, FAR, chp, LANES), BF16),
        pltpu.VMEM((2, NZ, chp, LANES), BF16),
        pltpu.VMEM((2, NZ, chp, LANES), BF16),
        pltpu.VMEM((2, chp, LANES), BF16),
        pltpu.VMEM((2, chp, LANES), BF16),
        pltpu.SemaphoreType.DMA((2,)),
        pltpu.SemaphoreType.DMA((128,)),
        pltpu.SemaphoreType.DMA((128,)),
    ]
    return pl.pallas_call(
        functools.partial(kernel, row_devices),
        out_shape=jax.ShapeDtypeStruct(latents.shape, BF16),
        in_specs=[vmem, smem, smem, hbm, vmem, vmem, vmem, hbm],
        out_specs=vmem,
        scratch_shapes=scratch,
        compiler_params=pltpu.CompilerParams(
            collective_id=0, has_side_effects=True, vmem_limit_bytes=60 * 1024 * 1024
        ),
    )(
        latents,
        clip_height,
        clip_width,
        expand_weight.transpose(2, 0, 1),
        expand_bias,
        depth_weight,
        depth_bias,
        project_weight,
    )


def solution(mesh):
    in_specs = (
        P(None, "row", None, "tensor"),
        P(),
        P(),
        P(None, None, "tensor"),
        P(None, "tensor"),
        P(None, None, None, "tensor"),
        P(None, "tensor"),
        P("tensor", None),
    )
    return jax.shard_map(
        functools.partial(on_device, mesh.shape["row"]),
        mesh=mesh,
        in_specs=in_specs,
        out_specs=P(None, "row", None, "tensor"),
        check_vma=False,
    )
```

```python
import functools

import jax
import jax.numpy as jnp
from jax import lax
from jax.experimental import pallas as pl
from jax.experimental.pallas import tpu as pltpu
from jax.sharding import PartitionSpec as P

MESH = pl.DeviceIdType.MESH
NY, NZ = 2, 8
FAR = NZ // 2
LANES = 128
HALF = LANES // 2
PAIR = 2 * LANES
BF16 = jnp.bfloat16
F32 = jnp.float32
NEAR_ORDER = (4, 3, -3, 2, -2, 1, -1, 0)


def ceil_to(n, m):
    return -(-n // m) * m


def silu(v):
    return v / (1.0 + jnp.exp(-v))


def iota(shape, dim):
    return lax.broadcasted_iota(jnp.int32, shape, dim)


def one_hot(cond):
    return jnp.where(cond, 1.0, 0.0).astype(BF16)


def across(a, b):
    return lax.dot_general(a, b, (((1,), (1,)), ((), ())), preferred_element_type=F32)


def kernel(
    rows,
    x_ref,
    height_ref,
    width_ref,
    w_hbm,
    bias_ref,
    taps_ref,
    shift_ref,
    p_hbm,
    out_ref,
    w_raw,
    w_flat,
    w_ref,
    p_raw,
    p_ref,
    rows_s,
    cols_s,
    taps_s,
    place,
    spot,
    xp_full,
    xp_half,
    xq,
    hx_out,
    hx_in,
    ec,
    ex,
    dn_out,
    up_out,
    dn_in,
    up_in,
    hid,
    hc,
    part,
    pf_out,
    pf_in,
    ph_out,
    ph_in,
    qz_out,
    qz_in,
    qy_out,
    qy_in,
    py_out,
    py_in,
    load,
    send,
    recv,
):
    r = lax.axis_index("row")
    t = lax.axis_index("tensor")
    y, z = t // NZ, t % NZ
    clips, row_count, col_count, ch = x_ref.shape
    ff, ffp, chp = bias_ref.shape[1], ex.shape[2], xq.shape[3]
    wide, spread = NY * NZ * ch, NY * NZ * chp
    cut = ceil_to(chp // 2, 16)

    def tz(step):
        return (z + NZ + step) % NZ

    ring = ({"tensor": y * NZ + tz(1)}, {"tensor": y * NZ + tz(-1)})
    other = {"tensor": (1 - y) * NZ + z}
    above = {"row": (r + rows - 1) % rows}
    below = {"row": (r + 1) % rows}

    w_load = pltpu.make_async_copy(w_hbm, w_raw.at[pl.ds(0, ff)], load.at[0])
    p_load = pltpu.make_async_copy(p_hbm, p_raw, load.at[1])
    w_load.start()
    p_load.start()

    barrier = pltpu.get_barrier_semaphore()
    for target in ring + (other, above, below):
        pl.semaphore_signal(barrier, inc=1, device_id=target, device_id_type=MESH)

    pending = {}

    def start(key, src, dst, target):
        n = len(pending)
        c = pltpu.make_async_remote_copy(
            src_ref=src,
            dst_ref=dst,
            send_sem=send.at[n],
            recv_sem=recv.at[n],
            device_id=target,
            device_id_type=MESH,
        )
        c.start()
        pending[key] = c

    def same(key, ref, target):
        start(key, ref, ref, target)

    def arrived(*key):
        pending[key].wait_recv()

    widths = [width_ref[b] for b in range(clips)]
    heights = [height_ref[b] for b in range(clips)]
    narrow = jnp.int32(clips - 1)
    for b in reversed(range(clips - 1)):
        narrow = jnp.where(widths[b] == col_count // 2, b, narrow)
    slots = [jnp.where(narrow == b, clips - 1, jnp.where(narrow < b, b - 1, b)) for b in range(clips)]

    def of_slot(s, values):
        total = jnp.int32(0)
        for b in range(clips):
            total = total + jnp.where(slots[b] == s, values[b], 0)
        return total

    slot_w = [of_slot(s, widths) for s in range(clips)]
    slot_h = [of_slot(s, heights) for s in range(clips)]

    sub, lane2 = iota((LANES, PAIR), 0), iota((LANES, PAIR), 1)
    sub_row, sub_col = sub // HALF, sub % HALF
    canvas_row = row_count * r + sub_row

    def make_place():
        for g in range(2):
            for b in range(clips):
                limit = jnp.where(slots[b] // 2 == g, widths[b], 0)
                first_slot = jnp.where(slots[b] == 2 * g + 1, 2 * slot_w[2 * g], 0)
                a = first_slot + sub_row * widths[b] + sub_col
                if g == 1:
                    a = jnp.where(a < HALF, a + HALF * y, a + HALF)
                ok = (sub_col < limit) & (canvas_row < heights[b])
                place[g, b * LANES : (b + 1) * LANES] = one_hot(ok & (lane2 == a))

    def make_spot():
        for g in range(2):
            for s in range(2):
                w, h = slot_w[2 * g + s], slot_h[2 * g + s]
                a = s * 2 * slot_w[2 * g] + sub_row * w + sub_col
                ok = (sub_col < w) & (canvas_row < h)
                if g == 0:
                    hit = lane2 == a
                else:
                    hit = (lane2 == a + HALF) | ((a < HALF) & (lane2 == a))
                spot[g, s * LANES : (s + 1) * LANES] = one_hot(ok & hit)

    make_place()
    tokens = x_ref[...].reshape(clips * LANES, ch).T
    for g in range(2):
        block = jnp.dot(tokens, place[g], preferred_element_type=F32).astype(BF16)
        empty = jnp.zeros((chp - ch, LANES), BF16)
        if g == 0:
            xp_full[y, z, 0:ch] = block[:, :LANES]
            xp_full[y, z, ch:chp] = empty
        else:
            hx_out[0:ch] = block[:, :LANES]
            hx_out[ch:chp] = empty
        xq[g, y, z, 0:ch] = block[:, LANES:]
        xq[g, y, z, ch:chp] = empty

    pl.semaphore_wait(barrier, 5)

    def gather_begin(g):
        if g == 0:
            same((g, "y"), xp_full.at[y, z], other)
            for d in range(2):
                same((g, "own", d), xp_full.at[y, z], ring[d])
        else:
            start((g, "y"), hx_out, hx_in, other)
        for d in range(2):
            same((g, "q", d, 0), xq.at[g, y, z], ring[d])
        same((g, "qy", 0), xq.at[g, y, z], other)

    def gather_pair(g):
        arrived(g, "y")
        if g == 0:
            for d in range(2):
                same((g, "p", d, 0), xp_full.at[1 - y, z], ring[d])
        else:
            xp_half[z] = hx_out[...] + hx_in[...]
            for d in range(2):
                same((g, "p", d, 0), xp_half.at[z], ring[d])

    def gather_step(g, s):
        for d in range(2):
            zz = tz(-s if d == 0 else s)
            arrived(g, "p", d, s - 1)
            if g == 0:
                if s == 1:
                    arrived(g, "own", d)
                if s < FAR - 1:
                    same((g, "p", d, s), xp_full.at[:, zz], ring[d])
                elif s < FAR:
                    same((g, "p", d, s), xp_full.at[d, zz], ring[d])
            else:
                if s < FAR - 1:
                    same((g, "p", d, s), xp_half.at[zz], ring[d])
                elif s < FAR:
                    at = pl.ds(0, cut) if d == 0 else pl.ds(cut, chp - cut)
                    same((g, "p", d, s), xp_half.at[zz, at], ring[d])
            arrived(g, "q", d, s - 1)
            if s < FAR - 1:
                same((g, "q", d, s), xq.at[g, y, zz], ring[d])
            elif s < FAR:
                at = pl.ds(0, cut) if d == 0 else pl.ds(cut, chp - cut)
                same((g, "q", d, s), xq.at[g, y, zz, at], ring[d])
            if s < FAR:
                same((g, "qy", -s if d == 0 else s), xq.at[g, y, zz], other)
        if s == FAR:
            same((g, "qy", FAR), xq.at[g, y, tz(FAR)], other)

    def flatten_w():
        w_flat[:, wide:] = jnp.zeros((2 * ffp, w_flat.shape[1] - wide), BF16)
        w_load.wait()
        w_raw[ff:ffp] = jnp.zeros((ffp - ff, 2, wide), BF16)

        def body(i, _):
            dst = pl.ds(pl.multiple_of(i * 32, 32), 32)
            w_flat[dst, 0:wide] = w_raw[pl.ds(i * 16, 16)].reshape(32, wide)
            return 0

        lax.fori_loop(0, ffp // 16, body, 0)

    def spread_w():
        for j in range(spread // LANES):
            c = LANES * j + iota((PAIR, LANES), 1)
            begin = LANES * j - (chp - ch) * (LANES * j // chp)
            base = begin // LANES * LANES
            p = base + iota((PAIR, LANES), 0)
            owner = c // chp
            pick = one_hot((p == c - (chp - ch) * owner) & (c - chp * owner < ch))
            moved = jnp.dot(w_flat[:, base : base + PAIR], pick, preferred_element_type=F32)
            w_ref[:, LANES * j : LANES * (j + 1)] = moved.astype(BF16)

    def split_w():
        to, at = iota((2 * ffp, 2 * ffp), 0), iota((2 * ffp, 2 * ffp), 1)
        pick = one_hot(at == jnp.where(to < ffp, 2 * to, 2 * (to - ffp) + 1))
        for n in range(spread // PAIR):
            sl = slice(PAIR * n, PAIR * (n + 1))
            w_ref[:, sl] = jnp.dot(pick, w_ref[:, sl], preferred_element_type=F32).astype(BF16)

    def turn_p():
        p_ref[...] = jnp.zeros_like(p_ref)
        p_load.wait()
        for zz in range(NZ):
            for yy in range(NY):
                o = yy * NZ + zz
                p_ref[zz, yy, 0:ch, 0:ff] = p_raw[:, ch * o : ch * (o + 1)].T

    def turn_columns():
        rows_s[...] = jnp.zeros_like(rows_s)
        rows_s[0:2, 0:ff] = bias_ref[...]
        rows_s[2:4, 0:ff] = shift_ref[...]
        for i in range(3):
            for j in range(3):
                n = 4 + 2 * (3 * i + j)
                rows_s[n : n + 2, 0:ff] = taps_ref[i, j]
        cols_s[...] = rows_s[...].T[:ffp]
        for n in range(taps_s.shape[0]):
            taps_s[n] = jnp.broadcast_to(cols_s[:, n : n + 1], (ffp, LANES))

    lane = iota((1, LANES), 1)
    first = lane < HALF
    col = lane % HALF
    left_ok = col > 0
    right_ok = col < HALF - 1
    top_ok = r > 0
    bottom_ok = r < rows - 1

    def expand_p(g):
        if g == 0:
            x = xp_full[...].reshape(spread, LANES)
            pre = jnp.dot(w_ref[...], x, preferred_element_type=F32)
        else:
            x = xp_half[...].reshape(spread // 2, LANES)
            pre = jnp.dot(w_ref[:, : spread // 2], x, preferred_element_type=F32)
            more = jnp.dot(w_ref[:, spread // 2 :], x, preferred_element_type=F32)
            pre = jnp.where(first, pre + pltpu.roll(more, HALF, 1), 0.0)
        for k in range(2):
            value = silu(pre[k * ffp : (k + 1) * ffp] + taps_s[k])
            if g == 1:
                value = jnp.where(first, value, 0.0)
            ec[k * ffp : (k + 1) * ffp, :LANES] = value.astype(BF16)

    def expand_q(g):
        x = xq[g].reshape(spread, LANES)
        pre = jnp.dot(w_ref[...], x, preferred_element_type=F32)
        for k in range(2):
            value = silu(pre[k * ffp : (k + 1) * ffp] + taps_s[k])
            ec[k * ffp : (k + 1) * ffp, LANES:] = value.astype(BF16)

    def restore(g):
        for k in range(2):
            ex[g, k] = across(ec[k * ffp : (k + 1) * ffp], spot[g])

        def body(i, _):
            at = pl.ds(pl.multiple_of(i * 16, 16), 16)
            for s in range(2):
                sl = slice(s * LANES, (s + 1) * LANES)
                e0, e1 = ex[g, 0, at, sl], ex[g, 1, at, sl]
                dn_out[g, at, sl] = jnp.where(first, pltpu.roll(e0, HALF, 1), e1).astype(BF16)
                up_out[g, at, sl] = jnp.where(first, e0, pltpu.roll(e1, HALF, 1)).astype(BF16)
            return 0

        lax.fori_loop(0, ffp // 16, body, 0, unroll=11)
        start((g, "dn"), dn_out.at[g], dn_in.at[g], below)
        start((g, "up"), up_out.at[g], up_in.at[g], above)

    def convolve(g):
        arrived(g, "dn")
        arrived(g, "up")

        def body(i, _):
            at = pl.ds(pl.multiple_of(i * 16, 16), 16)
            for s in range(2):
                sl = slice(s * LANES, (s + 1) * LANES)
                up = jnp.where(top_ok, dn_in[g, at, sl].astype(F32), 0.0)
                dn = jnp.where(bottom_ok, up_in[g, at, sl].astype(F32), 0.0)
                outs = []
                for k in range(2):
                    mid = ex[g, k, at, sl]
                    turned = pltpu.roll(mid, HALF, 1)
                    a = up if k == 0 else pltpu.roll(up, HALF, 1)
                    d = pltpu.roll(dn, HALF, 1) if k == 0 else dn
                    seen = [jnp.where(first, a, turned), mid, jnp.where(first, turned, d)]
                    sums = []
                    for j in range(3):
                        n = 4 + 2 * j + k
                        total = taps_s[n, at] * seen[0] + taps_s[n + 6, at] * seen[1]
                        sums.append(total + taps_s[n + 12, at] * seen[2])
                    res = sums[1] + taps_s[2 + k, at]
                    res = res + jnp.where(left_ok, pltpu.roll(sums[0], 1, 1), 0.0)
                    res = res + jnp.where(right_ok, pltpu.roll(sums[2], LANES - 1, 1), 0.0)
                    outs.append(res)
                hid[at, sl] = (outs[0] * silu(outs[1])).astype(BF16)
            return 0

        lax.fori_loop(0, ffp // 16, body, 0, unroll=2)

    def project(g):
        hc[...] = jnp.dot(hid[...], spot[g], preferred_element_type=F32).astype(BF16)
        p = p_ref[...].reshape(spread, ffp)
        part[g] = jnp.dot(p, hc[...], preferred_element_type=F32).reshape(NZ, NY, chp, PAIR)

    def scatter_begin(g):
        for n, d in enumerate(NEAR_ORDER):
            qy_out[g, n] = part[g, tz(d), 1 - y, :, LANES:].astype(BF16)
            start((g, "ry", d), qy_out.at[g, n], qy_in.at[g, n], other)

    def scatter_p(g, s):
        for d in range(2):
            zz = tz(FAR - s if d == 0 else s - FAR)
            if s > 0:
                arrived(g, "rp", d, s - 1)
            if g == 0:
                for yy in range(NY):
                    if s == 0 and yy != d:
                        continue
                    total = part[g, zz, yy, :, :LANES]
                    if s > 1 or (s == 1 and yy == d):
                        total = total + pf_in[d, s - 1, yy].astype(F32)
                    pf_out[d, s, yy] = total.astype(BF16)
                if s == 0:
                    src, dst = pf_out.at[d, s, d], pf_in.at[d, s, d]
                else:
                    src, dst = pf_out.at[d, s], pf_in.at[d, s]
            else:
                near = slice(0, cut) if d == 0 else slice(cut, chp)
                rest = slice(cut, chp) if d == 0 else slice(0, cut)
                for at in (near, rest):
                    if s == 0 and at is rest:
                        continue
                    total = jnp.where(first, part[g, zz, 0, at, :LANES], part[g, zz, 1, at, :LANES])
                    if s > 1 or (s == 1 and at is near):
                        total = total + ph_in[d, s - 1, at].astype(F32)
                    ph_out[d, s, at] = total.astype(BF16)
                if s == 0:
                    src, dst = ph_out.at[d, s, near], ph_in.at[d, s, near]
                else:
                    src, dst = ph_out.at[d, s], ph_in.at[d, s]
            start((g, "rp", d, s), src, dst, ring[d])

    def scatter_q(g, s):
        for d in range(2):
            step = FAR - s if d == 0 else s - FAR
            step = FAR if step == -FAR else step
            n = NEAR_ORDER.index(step)
            if s > 0 or d == 0:
                arrived(g, "ry", step)
            if s > 0:
                arrived(g, "rq", d, s - 1)
            near = slice(0, cut) if d == 0 else slice(cut, chp)
            rest = slice(cut, chp) if d == 0 else slice(0, cut)
            for at in (near, rest):
                if s == 0 and at is rest:
                    continue
                total = part[g, tz(step), y, at, LANES:] + qy_in[g, n, at].astype(F32)
                if s > 1 or (s == 1 and at is near):
                    total = total + qz_in[g, d, s - 1, at].astype(F32)
                qz_out[g, d, s, at] = total.astype(BF16)
            if s == 0:
                src, dst = qz_out.at[g, d, s, near], qz_in.at[g, d, s, near]
            else:
                src, dst = qz_out.at[g, d, s], qz_in.at[g, d, s]
            start((g, "rq", d, s), src, dst, ring[d])

    last = FAR - 1

    def scatter_pair(g):
        for d in range(2):
            arrived(g, "rp", d, last)
        if g == 0:
            total = part[g, z, 1 - y, :, :LANES]
            total = total + pf_in[0, last, 1 - y].astype(F32) + pf_in[1, last, 1 - y].astype(F32)
            py_out[g] = total.astype(BF16)
        else:
            py_out[g] = half_sum(1).astype(BF16)
        start((g, "py"), py_out.at[g], py_in.at[g], other)

    def half_sum(g):
        total = jnp.where(first, part[g, z, 0, :, :LANES], part[g, z, 1, :, :LANES])
        return total + ph_in[0, last].astype(F32) + ph_in[1, last].astype(F32)

    def finish_q(g):
        for d in range(2):
            arrived(g, "rq", d, last)
        arrived(g, "ry", 0)
        n = NEAR_ORDER.index(0)
        total = part[g, z, y, :, LANES:] + qy_in[g, n].astype(F32)
        return total + qz_in[g, 0, last].astype(F32) + qz_in[g, 1, last].astype(F32)

    def finish_p(g):
        if g == 0:
            total = part[g, z, y, :, :LANES]
            total = total + pf_in[0, last, y].astype(F32) + pf_in[1, last, y].astype(F32)
        else:
            total = half_sum(1)
        arrived(g, "py")
        return total + py_in[g].astype(F32)

    def restored(g):
        q = finish_q(g).astype(BF16)
        p = finish_p(g).astype(BF16)
        return across(place[g, :, :LANES], p) + across(place[g, :, LANES:], q)

    gather_begin(0)
    gather_begin(1)
    turn_columns()
    gather_pair(0)
    gather_pair(1)
    flatten_w()
    gather_step(0, 1)
    gather_step(1, 1)
    spread_w()
    gather_step(0, 2)
    gather_step(1, 2)
    split_w()
    gather_step(0, 3)
    gather_step(1, 3)
    make_spot()
    turn_p()
    gather_step(0, 4)
    gather_step(1, 4)
    expand_p(0)
    for d in NEAR_ORDER:
        arrived(0, "qy", d)
    expand_q(0)
    restore(0)
    expand_p(1)
    for d in NEAR_ORDER:
        arrived(1, "qy", d)
    expand_q(1)
    restore(1)
    convolve(0)
    project(0)
    scatter_begin(0)
    scatter_p(0, 0)
    scatter_q(0, 0)
    convolve(1)
    project(1)
    scatter_begin(1)
    scatter_p(1, 0)
    scatter_q(1, 0)
    for s in range(1, FAR):
        for g in range(2):
            scatter_p(g, s)
            scatter_q(g, s)
    scatter_pair(0)
    scatter_pair(1)
    acc = restored(0)
    acc = acc + restored(1)
    out_ref[...] = acc[:, :ch].astype(BF16).reshape(out_ref.shape)
    for c in pending.values():
        c.wait_send()


def on_device(
    row_devices,
    latents,
    clip_height,
    clip_width,
    expand_weight,
    expand_bias,
    depth_weight,
    depth_bias,
    project_weight,
):
    batch, row_count, col_count, ch = latents.shape
    ff = expand_bias.shape[1]
    assert batch == 4 and row_count == 2 and col_count == HALF
    chp, ffp = ceil_to(ch, 16), ceil_to(ff, 16)
    spread = NY * NZ * chp

    vmem = pl.BlockSpec(memory_space=pltpu.VMEM)
    smem = pl.BlockSpec(memory_space=pltpu.SMEM)
    hbm = pl.BlockSpec(memory_space=pl.ANY)
    scratch = [
        pltpu.VMEM((ffp, 2, NY * NZ * ch), BF16),
        pltpu.VMEM((2 * ffp, spread + LANES), BF16),
        pltpu.VMEM((2 * ffp, spread), BF16),
        pltpu.VMEM((ff, NY * NZ * ch), BF16),
        pltpu.VMEM((NZ, NY, chp, ffp), BF16),
        pltpu.VMEM((LANES, ceil_to(ffp, LANES)), F32),
        pltpu.VMEM((ffp, LANES), F32),
        pltpu.VMEM((22, ffp, LANES), F32),
        pltpu.VMEM((2, batch * LANES, PAIR), BF16),
        pltpu.VMEM((2, PAIR, PAIR), BF16),
        pltpu.VMEM((NY, NZ, chp, LANES), BF16),
        pltpu.VMEM((NZ, chp, LANES), BF16),
        pltpu.VMEM((2, NY, NZ, chp, LANES), BF16),
        pltpu.VMEM((chp, LANES), BF16),
        pltpu.VMEM((chp, LANES), BF16),
        pltpu.VMEM((2 * ffp, PAIR), BF16),
        pltpu.VMEM((2, 2, ffp, PAIR), F32),
        pltpu.VMEM((2, ffp, PAIR), BF16),
        pltpu.VMEM((2, ffp, PAIR), BF16),
        pltpu.VMEM((2, ffp, PAIR), BF16),
        pltpu.VMEM((2, ffp, PAIR), BF16),
        pltpu.VMEM((ffp, PAIR), BF16),
        pltpu.VMEM((ffp, PAIR), BF16),
        pltpu.VMEM((2, NZ, NY, chp, PAIR), F32),
        pltpu.VMEM((2, FAR, NY, chp, LANES), BF16),
        pltpu.VMEM((2, FAR, NY, chp, LANES), BF16),
        pltpu.VMEM((2, FAR, chp, LANES), BF16),
        pltpu.VMEM((2, FAR, chp, LANES), BF16),
        pltpu.VMEM((2, 2, FAR, chp, LANES), BF16),
        pltpu.VMEM((2, 2, FAR, chp, LANES), BF16),
        pltpu.VMEM((2, NZ, chp, LANES), BF16),
        pltpu.VMEM((2, NZ, chp, LANES), BF16),
        pltpu.VMEM((2, chp, LANES), BF16),
        pltpu.VMEM((2, chp, LANES), BF16),
        pltpu.SemaphoreType.DMA((2,)),
        pltpu.SemaphoreType.DMA((128,)),
        pltpu.SemaphoreType.DMA((128,)),
    ]
    return pl.pallas_call(
        functools.partial(kernel, row_devices),
        out_shape=jax.ShapeDtypeStruct(latents.shape, BF16),
        in_specs=[vmem, smem, smem, hbm, vmem, vmem, vmem, hbm],
        out_specs=vmem,
        scratch_shapes=scratch,
        compiler_params=pltpu.CompilerParams(
            collective_id=0, has_side_effects=True, vmem_limit_bytes=60 * 1024 * 1024
        ),
    )(
        latents,
        clip_height,
        clip_width,
        expand_weight.transpose(2, 0, 1),
        expand_bias,
        depth_weight,
        depth_bias,
        project_weight,
    )


def solution(mesh):
    in_specs = (
        P(None, "row", None, "tensor"),
        P(),
        P(),
        P(None, None, "tensor"),
        P(None, "tensor"),
        P(None, None, None, "tensor"),
        P(None, "tensor"),
        P("tensor", None),
    )
    return jax.shard_map(
        functools.partial(on_device, mesh.shape["row"]),
        mesh=mesh,
        in_specs=in_specs,
        out_specs=P(None, "row", None, "tensor"),
        check_vma=False,
    )
```

```python
import functools

import jax
import jax.numpy as jnp
from jax import lax
from jax.experimental import pallas as pl
from jax.experimental.pallas import tpu as pltpu
from jax.sharding import PartitionSpec as P

MESH = pl.DeviceIdType.MESH
NY, NZ = 2, 8
FAR = NZ // 2
LANES = 128
HALF = LANES // 2
PAIR = 2 * LANES
BF16 = jnp.bfloat16
F32 = jnp.float32
NEAR_ORDER = (3, -3, 4, 2, -2, 1, -1, 0)
STEPS = FAR - 1


def ceil_to(n, m):
    return -(-n // m) * m


def silu(v):
    return v / (1.0 + jnp.exp(-v))


def iota(shape, dim):
    return lax.broadcasted_iota(jnp.int32, shape, dim)


def one_hot(cond):
    return jnp.where(cond, 1.0, 0.0).astype(BF16)


def across(a, b):
    return lax.dot_general(a, b, (((1,), (1,)), ((), ())), preferred_element_type=F32)


def kernel(
    rows,
    x_ref,
    height_ref,
    width_ref,
    w_hbm,
    bias_ref,
    taps_ref,
    shift_ref,
    p_hbm,
    out_ref,
    w_raw,
    w_flat,
    w_ref,
    p_raw,
    p_ref,
    rows_s,
    cols_s,
    taps_s,
    place,
    spot,
    xp_full,
    xp_half,
    xq,
    hx_out,
    hx_in,
    ec,
    ex,
    turned,
    sums,
    dn_out,
    up_out,
    dn_in,
    up_in,
    hid,
    hc,
    part,
    pf_out,
    pf_in,
    ph_out,
    ph_in,
    qz_out,
    qz_in,
    qy_out,
    qy_in,
    py_out,
    py_in,
    load,
    send,
    recv,
):
    r = lax.axis_index("row")
    t = lax.axis_index("tensor")
    y, z = t // NZ, t % NZ
    clips, row_count, col_count, ch = x_ref.shape
    ff, ffp, chp = bias_ref.shape[1], ex.shape[2], xq.shape[3]
    wide, spread = NY * NZ * ch, NY * NZ * chp
    cut = ceil_to(chp // 2, 16)

    def tz(step):
        return (z + NZ + step) % NZ

    ring = ({"tensor": y * NZ + tz(1)}, {"tensor": y * NZ + tz(-1)})
    ring2 = ({"tensor": y * NZ + tz(2)}, {"tensor": y * NZ + tz(-2)})
    other = {"tensor": (1 - y) * NZ + z}
    above = {"row": (r + rows - 1) % rows}
    below = {"row": (r + 1) % rows}

    w_load = pltpu.make_async_copy(w_hbm, w_raw.at[pl.ds(0, ff)], load.at[0])
    p_load = pltpu.make_async_copy(p_hbm, p_raw, load.at[1])
    w_load.start()
    p_load.start()

    barrier = pltpu.get_barrier_semaphore()
    for target in ring + ring2 + (other, above, below):
        pl.semaphore_signal(barrier, inc=1, device_id=target, device_id_type=MESH)

    pending = {}

    def start(key, src, dst, target):
        n = len(pending)
        c = pltpu.make_async_remote_copy(
            src_ref=src,
            dst_ref=dst,
            send_sem=send.at[n],
            recv_sem=recv.at[n],
            device_id=target,
            device_id_type=MESH,
        )
        c.start()
        pending[key] = c

    def same(key, ref, target):
        start(key, ref, ref, target)

    def arrived(*key):
        pending[key].wait_recv()

    widths = [width_ref[b] for b in range(clips)]
    heights = [height_ref[b] for b in range(clips)]
    narrow = jnp.int32(clips - 1)
    for b in reversed(range(clips - 1)):
        narrow = jnp.where(widths[b] == col_count // 2, b, narrow)
    slots = [jnp.where(narrow == b, clips - 1, jnp.where(narrow < b, b - 1, b)) for b in range(clips)]

    def of_slot(s, values):
        total = jnp.int32(0)
        for b in range(clips):
            total = total + jnp.where(slots[b] == s, values[b], 0)
        return total

    slot_w = [of_slot(s, widths) for s in range(clips)]
    slot_h = [of_slot(s, heights) for s in range(clips)]

    sub, lane2 = iota((LANES, PAIR), 0), iota((LANES, PAIR), 1)
    sub_row, sub_col = sub // HALF, sub % HALF
    canvas_row = row_count * r + sub_row

    def make_place():
        for g in range(2):
            for b in range(clips):
                limit = jnp.where(slots[b] // 2 == g, widths[b], 0)
                first_slot = jnp.where(slots[b] == 2 * g + 1, 2 * slot_w[2 * g], 0)
                a = first_slot + sub_row * widths[b] + sub_col
                if g == 1:
                    a = jnp.where(a < HALF, a + HALF * y, a + HALF)
                ok = (sub_col < limit) & (canvas_row < heights[b])
                place[g, b * LANES : (b + 1) * LANES] = one_hot(ok & (lane2 == a))

    def make_spot():
        for g in range(2):
            for s in range(2):
                w, h = slot_w[2 * g + s], slot_h[2 * g + s]
                a = s * 2 * slot_w[2 * g] + sub_row * w + sub_col
                ok = (sub_col < w) & (canvas_row < h)
                if g == 0:
                    hit = lane2 == a
                else:
                    hit = (lane2 == a + HALF) | ((a < HALF) & (lane2 == a))
                spot[g, s * LANES : (s + 1) * LANES] = one_hot(ok & hit)

    make_place()
    tokens = x_ref[...].reshape(clips * LANES, ch).T
    for g in range(2):
        block = jnp.dot(tokens, place[g], preferred_element_type=F32).astype(BF16)
        empty = jnp.zeros((chp - ch, LANES), BF16)
        if g == 0:
            xp_full[y, z, 0:ch] = block[:, :LANES]
            xp_full[y, z, ch:chp] = empty
        else:
            hx_out[0:ch] = block[:, :LANES]
            hx_out[ch:chp] = empty
        xq[g, y, z, 0:ch] = block[:, LANES:]
        xq[g, y, z, ch:chp] = empty

    pl.semaphore_wait(barrier, 7)

    def gather_begin(g):
        if g == 0:
            same((g, "y"), xp_full.at[y, z], other)
            for d in range(2):
                same((g, "own", d), xp_full.at[y, z], ring[d])
        else:
            start((g, "y"), hx_out, hx_in, other)
        for d in range(2):
            same((g, "q", d, 0), xq.at[g, y, z], ring[d])
        same((g, "qy", 0), xq.at[g, y, z], other)

    def gather_pair(g):
        arrived(g, "y")
        if g == 0:
            for d in range(2):
                same((g, "p", d, 0), xp_full.at[1 - y, z], ring[d])
        else:
            xp_half[z] = hx_out[...] + hx_in[...]
            for d in range(2):
                same((g, "p", d, 0), xp_half.at[z], ring[d])

    def cut_at(d):
        return pl.ds(0, cut) if d == 0 else pl.ds(cut, chp - cut)

    def gather_step(g, s):
        for d in range(2):
            zz = tz(-s if d == 0 else s)
            arrived(g, "p", d, s - 1)
            if g == 0 and s == 1:
                arrived(g, "own", d)
            if s < STEPS:
                src = xp_full.at[:, zz] if g == 0 else xp_half.at[zz]
                same((g, "p", d, s), src, ring[d])
            if s == 2:
                src = xp_full.at[d, zz] if g == 0 else xp_half.at[zz, cut_at(d)]
                same((g, "pf", d), src, ring2[d])
        for d in range(2):
            zz = tz(-s if d == 0 else s)
            arrived(g, "q", d, s - 1)
            if s < STEPS:
                same((g, "q", d, s), xq.at[g, y, zz], ring[d])
            if s == 2:
                same((g, "qf", d), xq.at[g, y, zz, cut_at(d)], ring2[d])
            same((g, "qy", -s if d == 0 else s), xq.at[g, y, zz], other)
        if s == STEPS:
            for d in range(2):
                arrived(g, "qf", d)
            same((g, "qy", FAR), xq.at[g, y, tz(FAR)], other)
            for d in range(2):
                arrived(g, "pf", d)

    def flatten_w():
        w_flat[:, wide:] = jnp.zeros((2 * ffp, w_flat.shape[1] - wide), BF16)
        w_load.wait()
        w_raw[ff:ffp] = jnp.zeros((ffp - ff, 2, wide), BF16)

        def body(i, _):
            dst = pl.ds(pl.multiple_of(i * 32, 32), 32)
            w_flat[dst, 0:wide] = w_raw[pl.ds(i * 16, 16)].reshape(32, wide)
            return 0

        lax.fori_loop(0, ffp // 16, body, 0)

    def spread_w():
        for j in range(spread // LANES):
            c = LANES * j + iota((PAIR, LANES), 1)
            begin = LANES * j - (chp - ch) * (LANES * j // chp)
            base = begin // LANES * LANES
            p = base + iota((PAIR, LANES), 0)
            owner = c // chp
            pick = one_hot((p == c - (chp - ch) * owner) & (c - chp * owner < ch))
            moved = jnp.dot(w_flat[:, base : base + PAIR], pick, preferred_element_type=F32)
            w_ref[:, LANES * j : LANES * (j + 1)] = moved.astype(BF16)

    def split_w():
        to, at = iota((2 * ffp, 2 * ffp), 0), iota((2 * ffp, 2 * ffp), 1)
        pick = one_hot(at == jnp.where(to < ffp, 2 * to, 2 * (to - ffp) + 1))
        for n in range(spread // PAIR):
            sl = slice(PAIR * n, PAIR * (n + 1))
            w_ref[:, sl] = jnp.dot(pick, w_ref[:, sl], preferred_element_type=F32).astype(BF16)

    def turn_p():
        p_ref[...] = jnp.zeros_like(p_ref)
        p_load.wait()
        for zz in range(NZ):
            for yy in range(NY):
                o = yy * NZ + zz
                p_ref[zz, yy, 0:ch, 0:ff] = p_raw[:, ch * o : ch * (o + 1)].T

    def turn_columns():
        rows_s[...] = jnp.zeros_like(rows_s)
        rows_s[0:2, 0:ff] = bias_ref[...]
        rows_s[2:4, 0:ff] = shift_ref[...]
        for i in range(3):
            for j in range(3):
                n = 4 + 2 * (3 * i + j)
                rows_s[n : n + 2, 0:ff] = taps_ref[i, j]
        cols_s[...] = rows_s[...].T[:ffp]

        def wide_col(n):
            return jnp.broadcast_to(cols_s[:, n : n + 1], (ffp, LANES))

        for n in range(4):
            taps_s[n] = wide_col(n)
        for m in range(6):
            above_tap, below_tap = wide_col(4 + m), wide_col(16 + m)
            taps_s[4 + m] = wide_col(10 + m)
            taps_s[10 + m] = jnp.where(first, below_tap, above_tap)
            taps_s[16 + m] = jnp.where(first, above_tap, below_tap)

    lane = iota((1, LANES), 1)
    first = lane < HALF
    col = lane % HALF
    left_ok = col > 0
    right_ok = col < HALF - 1
    edge_row = row_count * r + jnp.where(first, -1, row_count)
    edge_ok = (edge_row >= 0) & (edge_row < rows * row_count)

    def expand_p(g):
        if g == 0:
            x = xp_full[...].reshape(spread, LANES)
            pre = jnp.dot(w_ref[...], x, preferred_element_type=F32)
        else:
            x = xp_half[...].reshape(spread // 2, LANES)
            pre = jnp.dot(w_ref[:, : spread // 2], x, preferred_element_type=F32)
            more = jnp.dot(w_ref[:, spread // 2 :], x, preferred_element_type=F32)
            pre = jnp.where(first, pre + pltpu.roll(more, HALF, 1), 0.0)
        for k in range(2):
            value = silu(pre[k * ffp : (k + 1) * ffp] + taps_s[k])
            if g == 1:
                value = jnp.where(first, value, 0.0)
            ec[k * ffp : (k + 1) * ffp, :LANES] = value.astype(BF16)

    def expand_q(g):
        x = xq[g].reshape(spread, LANES)
        pre = jnp.dot(w_ref[...], x, preferred_element_type=F32)
        for k in range(2):
            value = silu(pre[k * ffp : (k + 1) * ffp] + taps_s[k])
            ec[k * ffp : (k + 1) * ffp, LANES:] = value.astype(BF16)

    def restore(g):
        for k in range(2):
            ex[g, k] = across(ec[k * ffp : (k + 1) * ffp], spot[g])

        def body(i, _):
            at = pl.ds(pl.multiple_of(i * 16, 16), 16)
            for s in range(2):
                sl = slice(s * LANES, (s + 1) * LANES)
                e0, e1 = ex[g, 0, at, sl], ex[g, 1, at, sl]
                t0, t1 = pltpu.roll(e0, HALF, 1), pltpu.roll(e1, HALF, 1)
                turned[g, 0, at, sl] = t0
                turned[g, 1, at, sl] = t1
                dn_out[g, at, sl] = jnp.where(first, t0, e1).astype(BF16)
                up_out[g, at, sl] = jnp.where(first, e0, t1).astype(BF16)
            return 0

        lax.fori_loop(0, ffp // 16, body, 0, unroll=11)
        start((g, "dn"), dn_out.at[g], dn_in.at[g], below)
        start((g, "up"), up_out.at[g], up_in.at[g], above)

    def convolve(g):
        def body(i, _):
            at = pl.ds(pl.multiple_of(i * 16, 16), 16)
            for k in range(2):
                for s in range(2):
                    sl = slice(s * LANES, (s + 1) * LANES)
                    mid, swap = ex[g, k, at, sl], turned[g, k, at, sl]
                    for j in range(3):
                        n = 2 * j + k
                        total = taps_s[4 + n, at] * mid + taps_s[10 + n, at] * swap
                        sums[g, j, k, at, sl] = total
            return 0

        lax.fori_loop(0, ffp // 16, body, 0, unroll=2)

    def complete(g):
        arrived(g, "dn")
        arrived(g, "up")

        def body(i, _):
            at = pl.ds(pl.multiple_of(i * 16, 16), 16)
            for s in range(2):
                sl = slice(s * LANES, (s + 1) * LANES)
                dn, up = dn_in[g, at, sl].astype(F32), up_in[g, at, sl].astype(F32)
                edges = (
                    jnp.where(first, dn, pltpu.roll(up, HALF, 1)),
                    jnp.where(first, pltpu.roll(dn, HALF, 1), up),
                )
                outs = []
                for k in range(2):
                    edge = jnp.where(edge_ok, edges[k], 0.0)
                    got = [sums[g, j, k, at, sl] + taps_s[16 + 2 * j + k, at] * edge for j in range(3)]
                    res = got[1] + taps_s[2 + k, at]
                    res = res + jnp.where(left_ok, pltpu.roll(got[0], 1, 1), 0.0)
                    res = res + jnp.where(right_ok, pltpu.roll(got[2], LANES - 1, 1), 0.0)
                    outs.append(res)
                hid[at, sl] = (outs[0] * silu(outs[1])).astype(BF16)
            return 0

        lax.fori_loop(0, ffp // 16, body, 0, unroll=2)

    def project(g):
        hc[...] = jnp.dot(hid[...], spot[g], preferred_element_type=F32).astype(BF16)
        p = p_ref[...].reshape(spread, ffp)
        part[g] = jnp.dot(p, hc[...], preferred_element_type=F32).reshape(NZ, NY, chp, PAIR)

    def scatter_begin(g):
        for n, d in enumerate(NEAR_ORDER):
            qy_out[g, n] = part[g, tz(d), 1 - y, :, LANES:].astype(BF16)
            start((g, "ry", d), qy_out.at[g, n], qy_in.at[g, n], other)

    def cut_of(d):
        return slice(0, cut) if d == 0 else slice(cut, chp)

    def half_block(zz, at):
        return jnp.where(first, part[1, zz, 0, at, :LANES], part[1, zz, 1, at, :LANES])

    def scatter_p(g, s):
        for d in range(2):
            zz = tz(STEPS - s if d == 0 else s - STEPS)
            near = cut_of(d)
            if s == 0:
                if g == 0:
                    pf_out[d, STEPS, d] = part[0, tz(FAR), d, :, :LANES].astype(BF16)
                    src, dst = pf_out.at[d, STEPS, d], pf_in.at[d, STEPS, d]
                else:
                    ph_out[d, STEPS, near] = half_block(tz(FAR), near).astype(BF16)
                    src, dst = ph_out.at[d, STEPS, near], ph_in.at[d, STEPS, near]
                start((g, "rpf", d), src, dst, ring2[d])
            if s > 0:
                arrived(g, "rp", d, s - 1)
            if s == 1:
                arrived(g, "rpf", d)
            if g == 0:
                for yy in range(NY):
                    total = part[0, zz, yy, :, :LANES]
                    if s > 0:
                        total = total + pf_in[d, s - 1, yy].astype(F32)
                    if s == 1 and yy == d:
                        total = total + pf_in[d, STEPS, yy].astype(F32)
                    pf_out[d, s, yy] = total.astype(BF16)
                src, dst = pf_out.at[d, s], pf_in.at[d, s]
            else:
                for e in range(2):
                    at = cut_of(e)
                    total = half_block(zz, at)
                    if s > 0:
                        total = total + ph_in[d, s - 1, at].astype(F32)
                    if s == 1 and e == d:
                        total = total + ph_in[d, STEPS, at].astype(F32)
                    ph_out[d, s, at] = total.astype(BF16)
                src, dst = ph_out.at[d, s], ph_in.at[d, s]
            start((g, "rp", d, s), src, dst, ring[d])

    def q_block(g, step, at):
        n = NEAR_ORDER.index(step)
        return part[g, tz(step), y, at, LANES:] + qy_in[g, n, at].astype(F32)

    def scatter_q(g, s):
        for d in range(2):
            step = STEPS - s if d == 0 else s - STEPS
            arrived(g, "ry", step)
            if s > 0:
                arrived(g, "rq", d, s - 1)
            if s == 1:
                arrived(g, "rqf", d)
            for e in range(2):
                at = cut_of(e)
                total = q_block(g, step, at)
                if s > 0:
                    total = total + qz_in[g, d, s - 1, at].astype(F32)
                if s == 1 and e == d:
                    total = total + qz_in[g, d, STEPS, at].astype(F32)
                qz_out[g, d, s, at] = total.astype(BF16)
            start((g, "rq", d, s), qz_out.at[g, d, s], qz_in.at[g, d, s], ring[d])
        if s == 0:
            arrived(g, "ry", FAR)
            for d in range(2):
                at = cut_of(d)
                qz_out[g, d, STEPS, at] = q_block(g, FAR, at).astype(BF16)
                src, dst = qz_out.at[g, d, STEPS, at], qz_in.at[g, d, STEPS, at]
                start((g, "rqf", d), src, dst, ring2[d])

    last = STEPS - 1

    def scatter_pair(g):
        for d in range(2):
            arrived(g, "rp", d, last)
        if g == 0:
            total = part[g, z, 1 - y, :, :LANES]
            total = total + pf_in[0, last, 1 - y].astype(F32) + pf_in[1, last, 1 - y].astype(F32)
            py_out[g] = total.astype(BF16)
        else:
            py_out[g] = half_sum(1).astype(BF16)
        start((g, "py"), py_out.at[g], py_in.at[g], other)

    def half_sum(g):
        total = jnp.where(first, part[g, z, 0, :, :LANES], part[g, z, 1, :, :LANES])
        return total + ph_in[0, last].astype(F32) + ph_in[1, last].astype(F32)

    def finish_q(g):
        for d in range(2):
            arrived(g, "rq", d, last)
        arrived(g, "ry", 0)
        n = NEAR_ORDER.index(0)
        total = part[g, z, y, :, LANES:] + qy_in[g, n].astype(F32)
        return total + qz_in[g, 0, last].astype(F32) + qz_in[g, 1, last].astype(F32)

    def finish_p(g):
        if g == 0:
            total = part[g, z, y, :, :LANES]
            total = total + pf_in[0, last, y].astype(F32) + pf_in[1, last, y].astype(F32)
        else:
            total = half_sum(1)
        arrived(g, "py")
        return total + py_in[g].astype(F32)

    def restored(g):
        q = finish_q(g).astype(BF16)
        p = finish_p(g).astype(BF16)
        return across(place[g, :, :LANES], p) + across(place[g, :, LANES:], q)

    gather_begin(0)
    gather_begin(1)
    turn_columns()
    gather_pair(0)
    gather_pair(1)
    flatten_w()
    gather_step(0, 1)
    gather_step(1, 1)
    spread_w()
    gather_step(0, 2)
    gather_step(1, 2)
    split_w()
    make_spot()
    turn_p()
    gather_step(0, 3)
    gather_step(1, 3)
    expand_p(0)
    for d in NEAR_ORDER:
        arrived(0, "qy", d)
    expand_q(0)
    restore(0)
    expand_p(1)
    for d in NEAR_ORDER:
        arrived(1, "qy", d)
    expand_q(1)
    restore(1)
    convolve(0)
    convolve(1)
    complete(0)
    project(0)
    scatter_begin(0)
    scatter_p(0, 0)
    scatter_q(0, 0)
    complete(1)
    project(1)
    scatter_begin(1)
    scatter_p(1, 0)
    scatter_q(1, 0)
    for s in range(1, STEPS):
        for g in range(2):
            scatter_p(g, s)
            scatter_q(g, s)
    scatter_pair(0)
    scatter_pair(1)
    acc = restored(0)
    acc = acc + restored(1)
    out_ref[...] = acc[:, :ch].astype(BF16).reshape(out_ref.shape)
    for c in pending.values():
        c.wait_send()


def on_device(
    row_devices,
    latents,
    clip_height,
    clip_width,
    expand_weight,
    expand_bias,
    depth_weight,
    depth_bias,
    project_weight,
):
    batch, row_count, col_count, ch = latents.shape
    ff = expand_bias.shape[1]
    assert batch == 4 and row_count == 2 and col_count == HALF
    chp, ffp = ceil_to(ch, 16), ceil_to(ff, 16)
    spread = NY * NZ * chp

    vmem = pl.BlockSpec(memory_space=pltpu.VMEM)
    smem = pl.BlockSpec(memory_space=pltpu.SMEM)
    hbm = pl.BlockSpec(memory_space=pl.ANY)
    scratch = [
        pltpu.VMEM((ffp, 2, NY * NZ * ch), BF16),
        pltpu.VMEM((2 * ffp, spread + LANES), BF16),
        pltpu.VMEM((2 * ffp, spread), BF16),
        pltpu.VMEM((ff, NY * NZ * ch), BF16),
        pltpu.VMEM((NZ, NY, chp, ffp), BF16),
        pltpu.VMEM((LANES, ceil_to(ffp, LANES)), F32),
        pltpu.VMEM((ffp, LANES), F32),
        pltpu.VMEM((22, ffp, LANES), F32),
        pltpu.VMEM((2, batch * LANES, PAIR), BF16),
        pltpu.VMEM((2, PAIR, PAIR), BF16),
        pltpu.VMEM((NY, NZ, chp, LANES), BF16),
        pltpu.VMEM((NZ, chp, LANES), BF16),
        pltpu.VMEM((2, NY, NZ, chp, LANES), BF16),
        pltpu.VMEM((chp, LANES), BF16),
        pltpu.VMEM((chp, LANES), BF16),
        pltpu.VMEM((2 * ffp, PAIR), BF16),
        pltpu.VMEM((2, 2, ffp, PAIR), F32),
        pltpu.VMEM((2, 2, ffp, PAIR), F32),
        pltpu.VMEM((2, 3, 2, ffp, PAIR), F32),
        pltpu.VMEM((2, ffp, PAIR), BF16),
        pltpu.VMEM((2, ffp, PAIR), BF16),
        pltpu.VMEM((2, ffp, PAIR), BF16),
        pltpu.VMEM((2, ffp, PAIR), BF16),
        pltpu.VMEM((ffp, PAIR), BF16),
        pltpu.VMEM((ffp, PAIR), BF16),
        pltpu.VMEM((2, NZ, NY, chp, PAIR), F32),
        pltpu.VMEM((2, FAR, NY, chp, LANES), BF16),
        pltpu.VMEM((2, FAR, NY, chp, LANES), BF16),
        pltpu.VMEM((2, FAR, chp, LANES), BF16),
        pltpu.VMEM((2, FAR, chp, LANES), BF16),
        pltpu.VMEM((2, 2, FAR, chp, LANES), BF16),
        pltpu.VMEM((2, 2, FAR, chp, LANES), BF16),
        pltpu.VMEM((2, NZ, chp, LANES), BF16),
        pltpu.VMEM((2, NZ, chp, LANES), BF16),
        pltpu.VMEM((2, chp, LANES), BF16),
        pltpu.VMEM((2, chp, LANES), BF16),
        pltpu.SemaphoreType.DMA((2,)),
        pltpu.SemaphoreType.DMA((128,)),
        pltpu.SemaphoreType.DMA((128,)),
    ]
    return pl.pallas_call(
        functools.partial(kernel, row_devices),
        out_shape=jax.ShapeDtypeStruct(latents.shape, BF16),
        in_specs=[vmem, smem, smem, hbm, vmem, vmem, vmem, hbm],
        out_specs=vmem,
        scratch_shapes=scratch,
        compiler_params=pltpu.CompilerParams(
            collective_id=0, has_side_effects=True, vmem_limit_bytes=60 * 1024 * 1024
        ),
    )(
        latents,
        clip_height,
        clip_width,
        expand_weight.transpose(2, 0, 1),
        expand_bias,
        depth_weight,
        depth_bias,
        project_weight,
    )


def solution(mesh):
    in_specs = (
        P(None, "row", None, "tensor"),
        P(),
        P(),
        P(None, None, "tensor"),
        P(None, "tensor"),
        P(None, None, None, "tensor"),
        P(None, "tensor"),
        P("tensor", None),
    )
    return jax.shard_map(
        functools.partial(on_device, mesh.shape["row"]),
        mesh=mesh,
        in_specs=in_specs,
        out_specs=P(None, "row", None, "tensor"),
        check_vma=False,
    )
```

```python
import functools

import jax
import jax.numpy as jnp
from jax import lax
from jax.experimental import pallas as pl
from jax.experimental.pallas import tpu as pltpu
from jax.sharding import PartitionSpec as P

MESH = pl.DeviceIdType.MESH
NY, NZ = 2, 8
FAR = NZ // 2
LANES = 128
HALF = LANES // 2
PAIR = 2 * LANES
BF16 = jnp.bfloat16
F32 = jnp.float32
NEAR_ORDER = (3, -3, 4, 2, -2, 1, -1, 0)
STEPS = FAR - 1


def ceil_to(n, m):
    return -(-n // m) * m


def silu(v):
    h = 0.5 * v
    return h + h * jnp.tanh(h)


def iota(shape, dim):
    return lax.broadcasted_iota(jnp.int32, shape, dim)


def one_hot(cond):
    return jnp.where(cond, 1.0, 0.0).astype(BF16)


def across(a, b):
    return lax.dot_general(a, b, (((1,), (1,)), ((), ())), preferred_element_type=F32)


def kernel(
    rows,
    x_ref,
    height_ref,
    width_ref,
    w_hbm,
    bias_ref,
    taps_ref,
    shift_ref,
    p_hbm,
    out_ref,
    w_raw,
    w_flat,
    w_ref,
    p_raw,
    p_ref,
    rows_s,
    cols_s,
    taps_s,
    place,
    spot,
    xp_full,
    xp_half,
    xq,
    hx_out,
    hx_in,
    ec,
    ex,
    turned,
    sums,
    dn_out,
    up_out,
    dn_in,
    up_in,
    hid,
    hc,
    part,
    pf_out,
    pf_in,
    ph_out,
    ph_in,
    qz_out,
    qz_in,
    qy_out,
    qy_in,
    py_out,
    py_in,
    load,
    send,
    recv,
):
    r = lax.axis_index("row")
    t = lax.axis_index("tensor")
    y, z = t // NZ, t % NZ
    clips, row_count, col_count, ch = x_ref.shape
    ff, ffp, chp = bias_ref.shape[1], ex.shape[2], xq.shape[3]
    wide, spread = NY * NZ * ch, NY * NZ * chp
    cut = ceil_to(chp // 2, 16)

    def tz(step):
        return (z + NZ + step) % NZ

    ring = ({"tensor": y * NZ + tz(1)}, {"tensor": y * NZ + tz(-1)})
    ring2 = ({"tensor": y * NZ + tz(2)}, {"tensor": y * NZ + tz(-2)})
    other = {"tensor": (1 - y) * NZ + z}
    above = {"row": (r + rows - 1) % rows}
    below = {"row": (r + 1) % rows}

    w_load = pltpu.make_async_copy(w_hbm, w_raw.at[pl.ds(0, ff)], load.at[0])
    p_load = pltpu.make_async_copy(p_hbm, p_raw, load.at[1])
    w_load.start()
    p_load.start()

    barrier = pltpu.get_barrier_semaphore()
    for target in ring + ring2 + (other, above, below):
        pl.semaphore_signal(barrier, inc=1, device_id=target, device_id_type=MESH)

    pending = {}

    def start(key, src, dst, target):
        n = len(pending)
        c = pltpu.make_async_remote_copy(
            src_ref=src,
            dst_ref=dst,
            send_sem=send.at[n],
            recv_sem=recv.at[n],
            device_id=target,
            device_id_type=MESH,
        )
        c.start()
        pending[key] = c

    def same(key, ref, target):
        start(key, ref, ref, target)

    def arrived(*key):
        pending[key].wait_recv()

    widths = [width_ref[b] for b in range(clips)]
    heights = [height_ref[b] for b in range(clips)]
    narrow = jnp.int32(clips - 1)
    for b in reversed(range(clips - 1)):
        narrow = jnp.where(widths[b] == col_count // 2, b, narrow)
    slots = [jnp.where(narrow == b, clips - 1, jnp.where(narrow < b, b - 1, b)) for b in range(clips)]

    def of_slot(s, values):
        total = jnp.int32(0)
        for b in range(clips):
            total = total + jnp.where(slots[b] == s, values[b], 0)
        return total

    slot_w = [of_slot(s, widths) for s in range(clips)]
    slot_h = [of_slot(s, heights) for s in range(clips)]

    sub, lane2 = iota((LANES, PAIR), 0), iota((LANES, PAIR), 1)
    sub_row, sub_col = sub // HALF, sub % HALF
    canvas_row = row_count * r + sub_row

    def make_place():
        for g in range(2):
            for b in range(clips):
                limit = jnp.where(slots[b] // 2 == g, widths[b], 0)
                first_slot = jnp.where(slots[b] == 2 * g + 1, 2 * slot_w[2 * g], 0)
                a = first_slot + sub_row * widths[b] + sub_col
                if g == 1:
                    a = jnp.where(a < HALF, a + HALF * y, a + HALF)
                ok = (sub_col < limit) & (canvas_row < heights[b])
                place[g, b * LANES : (b + 1) * LANES] = one_hot(ok & (lane2 == a))

    def make_spot():
        for g in range(2):
            for s in range(2):
                w, h = slot_w[2 * g + s], slot_h[2 * g + s]
                a = s * 2 * slot_w[2 * g] + sub_row * w + sub_col
                ok = (sub_col < w) & (canvas_row < h)
                if g == 0:
                    hit = lane2 == a
                else:
                    hit = (lane2 == a + HALF) | ((a < HALF) & (lane2 == a))
                spot[g, s * LANES : (s + 1) * LANES] = one_hot(ok & hit)

    make_place()
    tokens = x_ref[...].reshape(clips * LANES, ch).T
    for g in range(2):
        block = jnp.dot(tokens, place[g], preferred_element_type=F32).astype(BF16)
        empty = jnp.zeros((chp - ch, LANES), BF16)
        if g == 0:
            xp_full[y, z, 0:ch] = block[:, :LANES]
            xp_full[y, z, ch:chp] = empty
        else:
            hx_out[0:ch] = block[:, :LANES]
            hx_out[ch:chp] = empty
        xq[g, y, z, 0:ch] = block[:, LANES:]
        xq[g, y, z, ch:chp] = empty

    pl.semaphore_wait(barrier, 7)

    def gather_begin(g):
        if g == 0:
            same((g, "y"), xp_full.at[y, z], other)
            for d in range(2):
                same((g, "own", d), xp_full.at[y, z], ring[d])
        else:
            start((g, "y"), hx_out, hx_in, other)
        for d in range(2):
            same((g, "q", d, 0), xq.at[g, y, z], ring[d])

    def gather_pair(g):
        arrived(g, "y")
        if g == 0:
            for d in range(2):
                same((g, "p", d, 0), xp_full.at[1 - y, z], ring[d])
        else:
            xp_half[z] = hx_out[...] + hx_in[...]
            for d in range(2):
                same((g, "p", d, 0), xp_half.at[z], ring[d])
        same((g, "qy", 0), xq.at[g, y, z], other)

    def cut_at(d):
        return pl.ds(0, cut) if d == 0 else pl.ds(cut, chp - cut)

    def gather_step(g, s):
        for d in range(2):
            zz = tz(-s if d == 0 else s)
            arrived(g, "p", d, s - 1)
            if g == 0 and s == 1:
                arrived(g, "own", d)
            if s < STEPS:
                src = xp_full.at[:, zz] if g == 0 else xp_half.at[zz]
                same((g, "p", d, s), src, ring[d])
            if s == 2:
                src = xp_full.at[d, zz] if g == 0 else xp_half.at[zz, cut_at(d)]
                same((g, "pf", d), src, ring2[d])
        for d in range(2):
            zz = tz(-s if d == 0 else s)
            arrived(g, "q", d, s - 1)
            if s < STEPS:
                same((g, "q", d, s), xq.at[g, y, zz], ring[d])
            if s == 2:
                same((g, "qf", d), xq.at[g, y, zz, cut_at(d)], ring2[d])
            same((g, "qy", -s if d == 0 else s), xq.at[g, y, zz], other)
        if s == STEPS:
            for d in range(2):
                arrived(g, "qf", d)
            same((g, "qy", FAR), xq.at[g, y, tz(FAR)], other)
            for d in range(2):
                arrived(g, "pf", d)

    def flatten_w():
        w_flat[:, wide:] = jnp.zeros((2 * ffp, w_flat.shape[1] - wide), BF16)
        w_load.wait()
        w_raw[ff:ffp] = jnp.zeros((ffp - ff, 2, wide), BF16)

        def body(i, _):
            dst = pl.ds(pl.multiple_of(i * 32, 32), 32)
            w_flat[dst, 0:wide] = w_raw[pl.ds(i * 16, 16)].reshape(32, wide)
            return 0

        lax.fori_loop(0, ffp // 16, body, 0)

    def spread_w():
        for j in range(spread // LANES):
            c = LANES * j + iota((PAIR, LANES), 1)
            begin = LANES * j - (chp - ch) * (LANES * j // chp)
            base = begin // LANES * LANES
            p = base + iota((PAIR, LANES), 0)
            owner = c // chp
            pick = one_hot((p == c - (chp - ch) * owner) & (c - chp * owner < ch))
            moved = jnp.dot(w_flat[:, base : base + PAIR], pick, preferred_element_type=F32)
            w_ref[:, LANES * j : LANES * (j + 1)] = moved.astype(BF16)

    def split_w():
        to, at = iota((2 * ffp, 2 * ffp), 0), iota((2 * ffp, 2 * ffp), 1)
        pick = one_hot(at == jnp.where(to < ffp, 2 * to, 2 * (to - ffp) + 1))
        for n in range(spread // PAIR):
            sl = slice(PAIR * n, PAIR * (n + 1))
            w_ref[:, sl] = jnp.dot(pick, w_ref[:, sl], preferred_element_type=F32).astype(BF16)

    def turn_p():
        p_ref[...] = jnp.zeros_like(p_ref)
        p_load.wait()
        for zz in range(NZ):
            for yy in range(NY):
                o = yy * NZ + zz
                p_ref[zz, yy, 0:ch, 0:ff] = p_raw[:, ch * o : ch * (o + 1)].T

    def turn_columns():
        rows_s[...] = jnp.zeros_like(rows_s)
        rows_s[0:2, 0:ff] = bias_ref[...]
        rows_s[2:4, 0:ff] = shift_ref[...]
        for i in range(3):
            for j in range(3):
                n = 4 + 2 * (3 * i + j)
                rows_s[n : n + 2, 0:ff] = taps_ref[i, j]
        cols_s[...] = rows_s[...].T[:ffp]

        def wide_col(n):
            return jnp.broadcast_to(cols_s[:, n : n + 1], (ffp, LANES))

        for n in range(4):
            taps_s[n] = wide_col(n)
        for m in range(6):
            above_tap, below_tap = wide_col(4 + m), wide_col(16 + m)
            taps_s[4 + m] = wide_col(10 + m)
            taps_s[10 + m] = jnp.where(first, below_tap, above_tap)
            taps_s[16 + m] = jnp.where(first, above_tap, below_tap)

    lane = iota((1, LANES), 1)
    first = lane < HALF
    col = lane % HALF
    left_ok = col > 0
    right_ok = col < HALF - 1
    edge_row = row_count * r + jnp.where(first, -1, row_count)
    edge_ok = (edge_row >= 0) & (edge_row < rows * row_count)

    def expand_p(g):
        if g == 0:
            x = xp_full[...].reshape(spread, LANES)
            pre = jnp.dot(w_ref[...], x, preferred_element_type=F32)
        else:
            x = xp_half[...].reshape(spread // 2, LANES)
            pre = jnp.dot(w_ref[:, : spread // 2], x, preferred_element_type=F32)
            more = jnp.dot(w_ref[:, spread // 2 :], x, preferred_element_type=F32)
            pre = jnp.where(first, pre + pltpu.roll(more, HALF, 1), 0.0)
        for k in range(2):
            value = silu(pre[k * ffp : (k + 1) * ffp] + taps_s[k])
            if g == 1:
                value = jnp.where(first, value, 0.0)
            ec[k * ffp : (k + 1) * ffp, :LANES] = value.astype(BF16)

    def expand_q(g):
        x = xq[g].reshape(spread, LANES)
        pre = jnp.dot(w_ref[...], x, preferred_element_type=F32)
        for k in range(2):
            value = silu(pre[k * ffp : (k + 1) * ffp] + taps_s[k])
            ec[k * ffp : (k + 1) * ffp, LANES:] = value.astype(BF16)

    def restore(g):
        for k in range(2):
            ex[g, k] = across(ec[k * ffp : (k + 1) * ffp], spot[g])

        def body(i, _):
            at = pl.ds(pl.multiple_of(i * 16, 16), 16)
            for s in range(2):
                sl = slice(s * LANES, (s + 1) * LANES)
                e0, e1 = ex[g, 0, at, sl], ex[g, 1, at, sl]
                t0, t1 = pltpu.roll(e0, HALF, 1), pltpu.roll(e1, HALF, 1)
                turned[g, 0, at, sl] = t0
                turned[g, 1, at, sl] = t1
                dn_out[g, at, sl] = jnp.where(first, t0, e1).astype(BF16)
                up_out[g, at, sl] = jnp.where(first, e0, t1).astype(BF16)
            return 0

        lax.fori_loop(0, ffp // 16, body, 0, unroll=11)
        start((g, "dn"), dn_out.at[g], dn_in.at[g], below)
        start((g, "up"), up_out.at[g], up_in.at[g], above)

    def convolve(g):
        def body(i, _):
            at = pl.ds(pl.multiple_of(i * 16, 16), 16)
            for k in range(2):
                for s in range(2):
                    sl = slice(s * LANES, (s + 1) * LANES)
                    mid, swap = ex[g, k, at, sl], turned[g, k, at, sl]
                    for j in range(3):
                        n = 2 * j + k
                        total = taps_s[4 + n, at] * mid + taps_s[10 + n, at] * swap
                        sums[g, j, k, at, sl] = total
            return 0

        lax.fori_loop(0, ffp // 16, body, 0, unroll=2)

    def complete(g):
        arrived(g, "dn")
        arrived(g, "up")

        def body(i, _):
            at = pl.ds(pl.multiple_of(i * 16, 16), 16)
            for s in range(2):
                sl = slice(s * LANES, (s + 1) * LANES)
                dn, up = dn_in[g, at, sl].astype(F32), up_in[g, at, sl].astype(F32)
                edges = (
                    jnp.where(first, dn, pltpu.roll(up, HALF, 1)),
                    jnp.where(first, pltpu.roll(dn, HALF, 1), up),
                )
                outs = []
                for k in range(2):
                    edge = jnp.where(edge_ok, edges[k], 0.0)
                    got = [sums[g, j, k, at, sl] + taps_s[16 + 2 * j + k, at] * edge for j in range(3)]
                    res = got[1] + taps_s[2 + k, at]
                    res = res + jnp.where(left_ok, pltpu.roll(got[0], 1, 1), 0.0)
                    res = res + jnp.where(right_ok, pltpu.roll(got[2], LANES - 1, 1), 0.0)
                    outs.append(res)
                hid[at, sl] = (outs[0] * silu(outs[1])).astype(BF16)
            return 0

        lax.fori_loop(0, ffp // 16, body, 0, unroll=2)

    def project(g):
        hc[...] = jnp.dot(hid[...], spot[g], preferred_element_type=F32).astype(BF16)
        p = p_ref[...].reshape(spread, ffp)
        part[g] = jnp.dot(p, hc[...], preferred_element_type=F32).reshape(NZ, NY, chp, PAIR)

    def scatter_y(g, *steps):
        for d in steps:
            n = NEAR_ORDER.index(d)
            qy_out[g, n] = part[g, tz(d), 1 - y, :, LANES:].astype(BF16)
            start((g, "ry", d), qy_out.at[g, n], qy_in.at[g, n], other)

    def cut_of(d):
        return slice(0, cut) if d == 0 else slice(cut, chp)

    def half_block(zz, at):
        return jnp.where(first, part[1, zz, 0, at, :LANES], part[1, zz, 1, at, :LANES])

    def scatter_p(g, s):
        for d in range(2):
            zz = tz(STEPS - s if d == 0 else s - STEPS)
            near = cut_of(d)
            if s == 0:
                if g == 0:
                    pf_out[d, STEPS, d] = part[0, tz(FAR), d, :, :LANES].astype(BF16)
                    src, dst = pf_out.at[d, STEPS, d], pf_in.at[d, STEPS, d]
                else:
                    ph_out[d, STEPS, near] = half_block(tz(FAR), near).astype(BF16)
                    src, dst = ph_out.at[d, STEPS, near], ph_in.at[d, STEPS, near]
                start((g, "rpf", d), src, dst, ring2[d])
            if s > 0:
                arrived(g, "rp", d, s - 1)
            if s == 1:
                arrived(g, "rpf", d)
            if g == 0:
                for yy in range(NY):
                    total = part[0, zz, yy, :, :LANES]
                    if s > 0:
                        total = total + pf_in[d, s - 1, yy].astype(F32)
                    if s == 1 and yy == d:
                        total = total + pf_in[d, STEPS, yy].astype(F32)
                    pf_out[d, s, yy] = total.astype(BF16)
                src, dst = pf_out.at[d, s], pf_in.at[d, s]
            else:
                for e in range(2):
                    at = cut_of(e)
                    total = half_block(zz, at)
                    if s > 0:
                        total = total + ph_in[d, s - 1, at].astype(F32)
                    if s == 1 and e == d:
                        total = total + ph_in[d, STEPS, at].astype(F32)
                    ph_out[d, s, at] = total.astype(BF16)
                src, dst = ph_out.at[d, s], ph_in.at[d, s]
            start((g, "rp", d, s), src, dst, ring[d])

    def q_block(g, step, at):
        n = NEAR_ORDER.index(step)
        return part[g, tz(step), y, at, LANES:] + qy_in[g, n, at].astype(F32)

    def scatter_q(g, s):
        for d in range(2):
            step = STEPS - s if d == 0 else s - STEPS
            arrived(g, "ry", step)
            if s > 0:
                arrived(g, "rq", d, s - 1)
            if s == 1:
                arrived(g, "rqf", d)
            for e in range(2):
                at = cut_of(e)
                total = q_block(g, step, at)
                if s > 0:
                    total = total + qz_in[g, d, s - 1, at].astype(F32)
                if s == 1 and e == d:
                    total = total + qz_in[g, d, STEPS, at].astype(F32)
                qz_out[g, d, s, at] = total.astype(BF16)
            start((g, "rq", d, s), qz_out.at[g, d, s], qz_in.at[g, d, s], ring[d])
        if s == 0:
            arrived(g, "ry", FAR)
            for d in range(2):
                at = cut_of(d)
                qz_out[g, d, STEPS, at] = q_block(g, FAR, at).astype(BF16)
                src, dst = qz_out.at[g, d, STEPS, at], qz_in.at[g, d, STEPS, at]
                start((g, "rqf", d), src, dst, ring2[d])

    last = STEPS - 1

    def scatter_pair(g):
        for d in range(2):
            arrived(g, "rp", d, last)
        if g == 0:
            total = part[g, z, 1 - y, :, :LANES]
            total = total + pf_in[0, last, 1 - y].astype(F32) + pf_in[1, last, 1 - y].astype(F32)
            py_out[g] = total.astype(BF16)
        else:
            py_out[g] = half_sum(1).astype(BF16)
        start((g, "py"), py_out.at[g], py_in.at[g], other)

    def half_sum(g):
        total = jnp.where(first, part[g, z, 0, :, :LANES], part[g, z, 1, :, :LANES])
        return total + ph_in[0, last].astype(F32) + ph_in[1, last].astype(F32)

    def finish_q(g):
        for d in range(2):
            arrived(g, "rq", d, last)
        arrived(g, "ry", 0)
        n = NEAR_ORDER.index(0)
        total = part[g, z, y, :, LANES:] + qy_in[g, n].astype(F32)
        return total + qz_in[g, 0, last].astype(F32) + qz_in[g, 1, last].astype(F32)

    def finish_p(g):
        if g == 0:
            total = part[g, z, y, :, :LANES]
            total = total + pf_in[0, last, y].astype(F32) + pf_in[1, last, y].astype(F32)
        else:
            total = half_sum(1)
        arrived(g, "py")
        return total + py_in[g].astype(F32)

    def restored(g):
        q = finish_q(g).astype(BF16)
        p = finish_p(g).astype(BF16)
        return across(place[g, :, :LANES], p) + across(place[g, :, LANES:], q)

    gather_begin(0)
    gather_begin(1)
    turn_columns()
    gather_pair(0)
    gather_pair(1)
    flatten_w()
    gather_step(0, 1)
    gather_step(1, 1)
    spread_w()
    gather_step(0, 2)
    gather_step(1, 2)
    split_w()
    make_spot()
    turn_p()
    gather_step(0, 3)
    gather_step(1, 3)
    expand_p(0)
    for d in NEAR_ORDER:
        arrived(0, "qy", d)
    expand_q(0)
    restore(0)
    expand_p(1)
    for d in NEAR_ORDER:
        arrived(1, "qy", d)
    expand_q(1)
    restore(1)
    convolve(0)
    convolve(1)
    complete(0)
    project(0)
    scatter_y(0, 3, -3, 4)
    scatter_p(0, 0)
    complete(1)
    project(1)
    scatter_y(1, 3, -3, 4)
    scatter_p(1, 0)
    scatter_y(0, 2, -2)
    scatter_q(0, 0)
    scatter_y(1, 2, -2)
    scatter_q(1, 0)
    scatter_p(0, 1)
    scatter_y(0, 1, -1)
    scatter_q(0, 1)
    scatter_p(1, 1)
    scatter_y(1, 1, -1)
    scatter_q(1, 1)
    scatter_y(0, 0)
    scatter_y(1, 0)
    for g in range(2):
        scatter_p(g, 2)
        scatter_q(g, 2)
    scatter_pair(0)
    scatter_pair(1)
    acc = restored(0)
    acc = acc + restored(1)
    out_ref[...] = acc[:, :ch].astype(BF16).reshape(out_ref.shape)
    for c in pending.values():
        c.wait_send()


def on_device(
    row_devices,
    latents,
    clip_height,
    clip_width,
    expand_weight,
    expand_bias,
    depth_weight,
    depth_bias,
    project_weight,
):
    batch, row_count, col_count, ch = latents.shape
    ff = expand_bias.shape[1]
    assert batch == 4 and row_count == 2 and col_count == HALF
    chp, ffp = ceil_to(ch, 16), ceil_to(ff, 16)
    spread = NY * NZ * chp

    vmem = pl.BlockSpec(memory_space=pltpu.VMEM)
    smem = pl.BlockSpec(memory_space=pltpu.SMEM)
    hbm = pl.BlockSpec(memory_space=pl.ANY)
    scratch = [
        pltpu.VMEM((ffp, 2, NY * NZ * ch), BF16),
        pltpu.VMEM((2 * ffp, spread + LANES), BF16),
        pltpu.VMEM((2 * ffp, spread), BF16),
        pltpu.VMEM((ff, NY * NZ * ch), BF16),
        pltpu.VMEM((NZ, NY, chp, ffp), BF16),
        pltpu.VMEM((LANES, ceil_to(ffp, LANES)), F32),
        pltpu.VMEM((ffp, LANES), F32),
        pltpu.VMEM((22, ffp, LANES), F32),
        pltpu.VMEM((2, batch * LANES, PAIR), BF16),
        pltpu.VMEM((2, PAIR, PAIR), BF16),
        pltpu.VMEM((NY, NZ, chp, LANES), BF16),
        pltpu.VMEM((NZ, chp, LANES), BF16),
        pltpu.VMEM((2, NY, NZ, chp, LANES), BF16),
        pltpu.VMEM((chp, LANES), BF16),
        pltpu.VMEM((chp, LANES), BF16),
        pltpu.VMEM((2 * ffp, PAIR), BF16),
        pltpu.VMEM((2, 2, ffp, PAIR), F32),
        pltpu.VMEM((2, 2, ffp, PAIR), F32),
        pltpu.VMEM((2, 3, 2, ffp, PAIR), F32),
        pltpu.VMEM((2, ffp, PAIR), BF16),
        pltpu.VMEM((2, ffp, PAIR), BF16),
        pltpu.VMEM((2, ffp, PAIR), BF16),
        pltpu.VMEM((2, ffp, PAIR), BF16),
        pltpu.VMEM((ffp, PAIR), BF16),
        pltpu.VMEM((ffp, PAIR), BF16),
        pltpu.VMEM((2, NZ, NY, chp, PAIR), F32),
        pltpu.VMEM((2, FAR, NY, chp, LANES), BF16),
        pltpu.VMEM((2, FAR, NY, chp, LANES), BF16),
        pltpu.VMEM((2, FAR, chp, LANES), BF16),
        pltpu.VMEM((2, FAR, chp, LANES), BF16),
        pltpu.VMEM((2, 2, FAR, chp, LANES), BF16),
        pltpu.VMEM((2, 2, FAR, chp, LANES), BF16),
        pltpu.VMEM((2, NZ, chp, LANES), BF16),
        pltpu.VMEM((2, NZ, chp, LANES), BF16),
        pltpu.VMEM((2, chp, LANES), BF16),
        pltpu.VMEM((2, chp, LANES), BF16),
        pltpu.SemaphoreType.DMA((2,)),
        pltpu.SemaphoreType.DMA((128,)),
        pltpu.SemaphoreType.DMA((128,)),
    ]
    return pl.pallas_call(
        functools.partial(kernel, row_devices),
        out_shape=jax.ShapeDtypeStruct(latents.shape, BF16),
        in_specs=[vmem, smem, smem, hbm, vmem, vmem, vmem, hbm],
        out_specs=vmem,
        scratch_shapes=scratch,
        compiler_params=pltpu.CompilerParams(
            collective_id=0, has_side_effects=True, vmem_limit_bytes=60 * 1024 * 1024
        ),
    )(
        latents,
        clip_height,
        clip_width,
        expand_weight.transpose(2, 0, 1),
        expand_bias,
        depth_weight,
        depth_bias,
        project_weight,
    )


def solution(mesh):
    in_specs = (
        P(None, "row", None, "tensor"),
        P(),
        P(),
        P(None, None, "tensor"),
        P(None, "tensor"),
        P(None, None, None, "tensor"),
        P(None, "tensor"),
        P("tensor", None),
    )
    return jax.shard_map(
        functools.partial(on_device, mesh.shape["row"]),
        mesh=mesh,
        in_specs=in_specs,
        out_specs=P(None, "row", None, "tensor"),
        check_vma=False,
    )
```

```python
import functools

import jax
import jax.numpy as jnp
from jax import lax
from jax.experimental import pallas as pl
from jax.experimental.pallas import tpu as pltpu
from jax.sharding import PartitionSpec as P

MESH = pl.DeviceIdType.MESH
NY, NZ = 2, 8
FAR = NZ // 2
LANES = 128
HALF = LANES // 2
PAIR = 2 * LANES
BF16 = jnp.bfloat16
F32 = jnp.float32
NEAR_ORDER = (3, -3, 4, 2, -2, 1, -1, 0)
STEPS = FAR - 1


def ceil_to(n, m):
    return -(-n // m) * m


def silu(v):
    h = 0.5 * v
    return h + h * jnp.tanh(h)


def iota(shape, dim):
    return lax.broadcasted_iota(jnp.int32, shape, dim)


def one_hot(cond):
    return jnp.where(cond, 1.0, 0.0).astype(BF16)


def across(a, b):
    return lax.dot_general(a, b, (((1,), (1,)), ((), ())), preferred_element_type=F32)


def kernel(
    rows,
    x_ref,
    height_ref,
    width_ref,
    w_hbm,
    bias_ref,
    taps_ref,
    shift_ref,
    p_hbm,
    out_ref,
    w_raw,
    w_flat,
    w_ref,
    p_raw,
    p_ref,
    rows_s,
    cols_s,
    taps_s,
    place,
    spot,
    xp_full,
    xp_half,
    xq,
    hx_out,
    hx_in,
    hx_own,
    hx_diag,
    ec,
    ex,
    turned,
    sums,
    dn_out,
    up_out,
    dn_in,
    up_in,
    hid,
    hc,
    part,
    pf_out,
    pf_in,
    ph_out,
    ph_in,
    ph_diag,
    qz_out,
    qz_in,
    qy_out,
    qy_in,
    py_out,
    py_in,
    load,
    send,
    recv,
):
    r = lax.axis_index("row")
    t = lax.axis_index("tensor")
    y, z = t // NZ, t % NZ
    clips, row_count, col_count, ch = x_ref.shape
    ff, ffp, chp = bias_ref.shape[1], ex.shape[2], xq.shape[3]
    wide, spread = NY * NZ * ch, NY * NZ * chp
    cut = ceil_to(chp // 2, 16)

    def tz(step):
        return (z + NZ + step) % NZ

    ring = ({"tensor": y * NZ + tz(1)}, {"tensor": y * NZ + tz(-1)})
    ring2 = ({"tensor": y * NZ + tz(2)}, {"tensor": y * NZ + tz(-2)})
    other = {"tensor": (1 - y) * NZ + z}
    diag = ({"tensor": (1 - y) * NZ + tz(1)}, {"tensor": (1 - y) * NZ + tz(-1)})
    above = {"row": (r + rows - 1) % rows}
    below = {"row": (r + 1) % rows}

    w_load = pltpu.make_async_copy(w_hbm, w_raw.at[pl.ds(0, ff)], load.at[0])
    p_load = pltpu.make_async_copy(p_hbm, p_raw, load.at[1])
    w_load.start()
    p_load.start()

    barrier = pltpu.get_barrier_semaphore()
    for target in ring + ring2 + diag + (other, above, below):
        pl.semaphore_signal(barrier, inc=1, device_id=target, device_id_type=MESH)

    pending = {}

    def start(key, src, dst, target):
        n = len(pending)
        c = pltpu.make_async_remote_copy(
            src_ref=src,
            dst_ref=dst,
            send_sem=send.at[n],
            recv_sem=recv.at[n],
            device_id=target,
            device_id_type=MESH,
        )
        c.start()
        pending[key] = c

    def same(key, ref, target):
        start(key, ref, ref, target)

    def arrived(*key):
        pending[key].wait_recv()

    widths = [width_ref[b] for b in range(clips)]
    heights = [height_ref[b] for b in range(clips)]
    narrow = jnp.int32(clips - 1)
    for b in reversed(range(clips - 1)):
        narrow = jnp.where(widths[b] == col_count // 2, b, narrow)
    slots = [jnp.where(narrow == b, clips - 1, jnp.where(narrow < b, b - 1, b)) for b in range(clips)]

    def of_slot(s, values):
        total = jnp.int32(0)
        for b in range(clips):
            total = total + jnp.where(slots[b] == s, values[b], 0)
        return total

    slot_w = [of_slot(s, widths) for s in range(clips)]
    slot_h = [of_slot(s, heights) for s in range(clips)]

    sub, lane2 = iota((LANES, PAIR), 0), iota((LANES, PAIR), 1)
    sub_row, sub_col = sub // HALF, sub % HALF
    canvas_row = row_count * r + sub_row

    def make_place():
        for g in range(2):
            for b in range(clips):
                limit = jnp.where(slots[b] // 2 == g, widths[b], 0)
                first_slot = jnp.where(slots[b] == 2 * g + 1, 2 * slot_w[2 * g], 0)
                a = first_slot + sub_row * widths[b] + sub_col
                if g == 1:
                    a = jnp.where(a < HALF, a + HALF * y, a + HALF)
                ok = (sub_col < limit) & (canvas_row < heights[b])
                place[g, b * LANES : (b + 1) * LANES] = one_hot(ok & (lane2 == a))

    def make_spot():
        for g in range(2):
            for s in range(2):
                w, h = slot_w[2 * g + s], slot_h[2 * g + s]
                a = s * 2 * slot_w[2 * g] + sub_row * w + sub_col
                ok = (sub_col < w) & (canvas_row < h)
                if g == 0:
                    hit = lane2 == a
                else:
                    hit = (lane2 == a + HALF) | ((a < HALF) & (lane2 == a))
                spot[g, s * LANES : (s + 1) * LANES] = one_hot(ok & hit)

    make_place()
    tokens = x_ref[...].reshape(clips * LANES, ch).T
    for g in range(2):
        block = jnp.dot(tokens, place[g], preferred_element_type=F32).astype(BF16)
        empty = jnp.zeros((chp - ch, LANES), BF16)
        if g == 0:
            xp_full[y, z, 0:ch] = block[:, :LANES]
            xp_full[y, z, ch:chp] = empty
        else:
            hx_out[0:ch] = block[:, :LANES]
            hx_out[ch:chp] = empty
        xq[g, y, z, 0:ch] = block[:, LANES:]
        xq[g, y, z, ch:chp] = empty

    pl.semaphore_wait(barrier, 9)

    def gather_begin(g):
        for d in range(2):
            if g == 0:
                same((g, "own", d), xp_full.at[y, z], ring[d])
            else:
                start((g, "own", d), hx_out, hx_own.at[d], ring[d])
        for d in range(2):
            if g == 0:
                same((g, "p", d, 0), xp_full.at[y, z], diag[d])
            else:
                start((g, "p", d, 0), hx_out, hx_diag.at[d], diag[d])
        for d in range(2):
            same((g, "q", d, 0), xq.at[g, y, z], ring[d])

    def gather_own(g):
        if g == 0:
            same((g, "y"), xp_full.at[y, z], other)
        else:
            start((g, "y"), hx_out, hx_in, other)
        same((g, "qy", 0), xq.at[g, y, z], other)

    def gather_pair(g):
        arrived(g, "y")
        if g == 1:
            xp_half[z] = hx_out[...] + hx_in[...]

    def cut_at(d):
        return pl.ds(0, cut) if d == 0 else pl.ds(cut, chp - cut)

    def gather_step(g, s):
        for d in range(2):
            zz = tz(-s if d == 0 else s)
            arrived(g, "p", d, s - 1)
            if s == 1:
                arrived(g, "own", d)
                if g == 1:
                    xp_half[zz] = hx_own[d] + hx_diag[d]
            if s < STEPS:
                src = xp_full.at[:, zz] if g == 0 else xp_half.at[zz]
                same((g, "p", d, s), src, ring[d])
            if s == 2:
                src = xp_full.at[d, zz] if g == 0 else xp_half.at[zz, cut_at(d)]
                same((g, "pf", d), src, ring2[d])
        for d in range(2):
            zz = tz(-s if d == 0 else s)
            arrived(g, "q", d, s - 1)
            if s < STEPS:
                same((g, "q", d, s), xq.at[g, y, zz], ring[d])
            if s == 2:
                same((g, "qf", d), xq.at[g, y, zz, cut_at(d)], ring2[d])
            same((g, "qy", -s if d == 0 else s), xq.at[g, y, zz], other)
        if s == STEPS:
            for d in range(2):
                arrived(g, "qf", d)
            same((g, "qy", FAR), xq.at[g, y, tz(FAR)], other)
            for d in range(2):
                arrived(g, "pf", d)

    def flatten_w():
        w_flat[:, wide:] = jnp.zeros((2 * ffp, w_flat.shape[1] - wide), BF16)
        w_load.wait()
        w_raw[ff:ffp] = jnp.zeros((ffp - ff, 2, wide), BF16)

        def body(i, _):
            dst = pl.ds(pl.multiple_of(i * 32, 32), 32)
            w_flat[dst, 0:wide] = w_raw[pl.ds(i * 16, 16)].reshape(32, wide)
            return 0

        lax.fori_loop(0, ffp // 16, body, 0)

    def spread_w():
        for j in range(spread // LANES):
            c = LANES * j + iota((PAIR, LANES), 1)
            begin = LANES * j - (chp - ch) * (LANES * j // chp)
            base = begin // LANES * LANES
            p = base + iota((PAIR, LANES), 0)
            owner = c // chp
            pick = one_hot((p == c - (chp - ch) * owner) & (c - chp * owner < ch))
            moved = jnp.dot(w_flat[:, base : base + PAIR], pick, preferred_element_type=F32)
            w_ref[:, LANES * j : LANES * (j + 1)] = moved.astype(BF16)

    def split_w():
        to, at = iota((2 * ffp, 2 * ffp), 0), iota((2 * ffp, 2 * ffp), 1)
        pick = one_hot(at == jnp.where(to < ffp, 2 * to, 2 * (to - ffp) + 1))
        for n in range(spread // PAIR):
            sl = slice(PAIR * n, PAIR * (n + 1))
            w_ref[:, sl] = jnp.dot(pick, w_ref[:, sl], preferred_element_type=F32).astype(BF16)

    def turn_p():
        p_ref[...] = jnp.zeros_like(p_ref)
        p_load.wait()
        for zz in range(NZ):
            for yy in range(NY):
                o = yy * NZ + zz
                p_ref[zz, yy, 0:ch, 0:ff] = p_raw[:, ch * o : ch * (o + 1)].T

    def turn_columns():
        rows_s[...] = jnp.zeros_like(rows_s)
        rows_s[0:2, 0:ff] = bias_ref[...]
        rows_s[2:4, 0:ff] = shift_ref[...]
        for i in range(3):
            for j in range(3):
                n = 4 + 2 * (3 * i + j)
                rows_s[n : n + 2, 0:ff] = taps_ref[i, j]
        cols_s[...] = rows_s[...].T[:ffp]

        def wide_col(n):
            return jnp.broadcast_to(cols_s[:, n : n + 1], (ffp, LANES))

        for n in range(4):
            taps_s[n] = wide_col(n)
        for m in range(6):
            above_tap, below_tap = wide_col(4 + m), wide_col(16 + m)
            taps_s[4 + m] = wide_col(10 + m)
            taps_s[10 + m] = jnp.where(first, below_tap, above_tap)
            taps_s[16 + m] = jnp.where(first, above_tap, below_tap)

    lane = iota((1, LANES), 1)
    first = lane < HALF
    col = lane % HALF
    left_ok = col > 0
    right_ok = col < HALF - 1
    edge_row = row_count * r + jnp.where(first, -1, row_count)
    edge_ok = (edge_row >= 0) & (edge_row < rows * row_count)

    def expand_p(g):
        if g == 0:
            x = xp_full[...].reshape(spread, LANES)
            pre = jnp.dot(w_ref[...], x, preferred_element_type=F32)
        else:
            x = xp_half[...].reshape(spread // 2, LANES)
            pre = jnp.dot(w_ref[:, : spread // 2], x, preferred_element_type=F32)
            more = jnp.dot(w_ref[:, spread // 2 :], x, preferred_element_type=F32)
            pre = jnp.where(first, pre + pltpu.roll(more, HALF, 1), 0.0)
        for k in range(2):
            value = silu(pre[k * ffp : (k + 1) * ffp] + taps_s[k])
            if g == 1:
                value = jnp.where(first, value, 0.0)
            ec[k * ffp : (k + 1) * ffp, :LANES] = value.astype(BF16)

    def expand_q(g):
        x = xq[g].reshape(spread, LANES)
        pre = jnp.dot(w_ref[...], x, preferred_element_type=F32)
        for k in range(2):
            value = silu(pre[k * ffp : (k + 1) * ffp] + taps_s[k])
            ec[k * ffp : (k + 1) * ffp, LANES:] = value.astype(BF16)

    def restore(g):
        for k in range(2):
            ex[g, k] = across(ec[k * ffp : (k + 1) * ffp], spot[g])

        def body(i, _):
            at = pl.ds(pl.multiple_of(i * 16, 16), 16)
            for s in range(2):
                sl = slice(s * LANES, (s + 1) * LANES)
                e0, e1 = ex[g, 0, at, sl], ex[g, 1, at, sl]
                t0, t1 = pltpu.roll(e0, HALF, 1), pltpu.roll(e1, HALF, 1)
                turned[g, 0, at, sl] = t0
                turned[g, 1, at, sl] = t1
                dn_out[g, at, sl] = jnp.where(first, t0, e1).astype(BF16)
                up_out[g, at, sl] = jnp.where(first, e0, t1).astype(BF16)
            return 0

        lax.fori_loop(0, ffp // 16, body, 0, unroll=11)
        start((g, "dn"), dn_out.at[g], dn_in.at[g], below)
        start((g, "up"), up_out.at[g], up_in.at[g], above)

    def convolve(g):
        def body(i, _):
            at = pl.ds(pl.multiple_of(i * 16, 16), 16)
            for k in range(2):
                for s in range(2):
                    sl = slice(s * LANES, (s + 1) * LANES)
                    mid, swap = ex[g, k, at, sl], turned[g, k, at, sl]
                    for j in range(3):
                        n = 2 * j + k
                        total = taps_s[4 + n, at] * mid + taps_s[10 + n, at] * swap
                        sums[g, j, k, at, sl] = total
            return 0

        lax.fori_loop(0, ffp // 16, body, 0, unroll=2)

    def complete(g):
        arrived(g, "dn")
        arrived(g, "up")

        def body(i, _):
            at = pl.ds(pl.multiple_of(i * 16, 16), 16)
            for s in range(2):
                sl = slice(s * LANES, (s + 1) * LANES)
                dn, up = dn_in[g, at, sl].astype(F32), up_in[g, at, sl].astype(F32)
                edges = (
                    jnp.where(first, dn, pltpu.roll(up, HALF, 1)),
                    jnp.where(first, pltpu.roll(dn, HALF, 1), up),
                )
                outs = []
                for k in range(2):
                    edge = jnp.where(edge_ok, edges[k], 0.0)
                    got = [sums[g, j, k, at, sl] + taps_s[16 + 2 * j + k, at] * edge for j in range(3)]
                    res = got[1] + taps_s[2 + k, at]
                    res = res + jnp.where(left_ok, pltpu.roll(got[0], 1, 1), 0.0)
                    res = res + jnp.where(right_ok, pltpu.roll(got[2], LANES - 1, 1), 0.0)
                    outs.append(res)
                hid[at, sl] = (outs[0] * silu(outs[1])).astype(BF16)
            return 0

        lax.fori_loop(0, ffp // 16, body, 0, unroll=2)

    def project(g):
        hc[...] = jnp.dot(hid[...], spot[g], preferred_element_type=F32).astype(BF16)
        p = p_ref[...].reshape(spread, ffp)
        part[g] = jnp.dot(p, hc[...], preferred_element_type=F32).reshape(NZ, NY, chp, PAIR)

    def scatter_y(g, *steps):
        for d in steps:
            n = NEAR_ORDER.index(d)
            qy_out[g, n] = part[g, tz(d), 1 - y, :, LANES:].astype(BF16)
            start((g, "ry", d), qy_out.at[g, n], qy_in.at[g, n], other)

    last = STEPS - 1

    def cut_of(d):
        return slice(0, cut) if d == 0 else slice(cut, chp)

    def half_block(zz, at):
        return jnp.where(first, part[1, zz, 0, at, :LANES], part[1, zz, 1, at, :LANES])

    def scatter_p(g, s):
        for d in range(2):
            zz = tz(STEPS - s if d == 0 else s - STEPS)
            near = cut_of(d)
            if s == 0:
                if g == 0:
                    pf_out[d, STEPS, d] = part[0, tz(FAR), d, :, :LANES].astype(BF16)
                    src, dst = pf_out.at[d, STEPS, d], pf_in.at[d, STEPS, d]
                else:
                    ph_out[d, STEPS, near] = half_block(tz(FAR), near).astype(BF16)
                    src, dst = ph_out.at[d, STEPS, near], ph_in.at[d, STEPS, near]
                start((g, "rpf", d), src, dst, ring2[d])
            if s > 0:
                arrived(g, "rp", d, s - 1)
            if s == 1:
                arrived(g, "rpf", d)
            if g == 0:
                for yy in range(NY):
                    total = part[0, zz, yy, :, :LANES]
                    if s > 0:
                        total = total + pf_in[d, s - 1, yy].astype(F32)
                    if s == 1 and yy == d:
                        total = total + pf_in[d, STEPS, yy].astype(F32)
                    pf_out[d, s, yy] = total.astype(BF16)
                if s < last:
                    src, dst = pf_out.at[d, s], pf_in.at[d, s]
                else:
                    src, dst = pf_out.at[d, s, 1 - y], pf_in.at[d, s, 1]
                    start((g, "rpd", d), src, dst, diag[d])
                    src, dst = pf_out.at[d, s, y], pf_in.at[d, s, 0]
            else:
                for e in range(2):
                    at = cut_of(e)
                    total = half_block(zz, at)
                    if s > 0:
                        total = total + ph_in[d, s - 1, at].astype(F32)
                    if s == 1 and e == d:
                        total = total + ph_in[d, STEPS, at].astype(F32)
                    ph_out[d, s, at] = total.astype(BF16)
                src, dst = ph_out.at[d, s], ph_in.at[d, s]
                if s == last:
                    start((g, "rpd", d), src, ph_diag.at[d], diag[d])
            start((g, "rp", d, s), src, dst, ring[d])

    def q_block(g, step, at):
        n = NEAR_ORDER.index(step)
        return part[g, tz(step), y, at, LANES:] + qy_in[g, n, at].astype(F32)

    def scatter_q(g, s):
        for d in range(2):
            step = STEPS - s if d == 0 else s - STEPS
            arrived(g, "ry", step)
            if s > 0:
                arrived(g, "rq", d, s - 1)
            if s == 1:
                arrived(g, "rqf", d)
            for e in range(2):
                at = cut_of(e)
                total = q_block(g, step, at)
                if s > 0:
                    total = total + qz_in[g, d, s - 1, at].astype(F32)
                if s == 1 and e == d:
                    total = total + qz_in[g, d, STEPS, at].astype(F32)
                qz_out[g, d, s, at] = total.astype(BF16)
            start((g, "rq", d, s), qz_out.at[g, d, s], qz_in.at[g, d, s], ring[d])
        if s == 0:
            arrived(g, "ry", FAR)
            for d in range(2):
                at = cut_of(d)
                qz_out[g, d, STEPS, at] = q_block(g, FAR, at).astype(BF16)
                src, dst = qz_out.at[g, d, STEPS, at], qz_in.at[g, d, STEPS, at]
                start((g, "rqf", d), src, dst, ring2[d])

    def scatter_own(g):
        if g == 0:
            py_out[g] = part[g, z, 1 - y, :, :LANES].astype(BF16)
        else:
            py_out[g] = half_block(z, slice(0, chp)).astype(BF16)
        start((g, "py"), py_out.at[g], py_in.at[g], other)

    def finish_q(g):
        for d in range(2):
            arrived(g, "rq", d, last)
        arrived(g, "ry", 0)
        n = NEAR_ORDER.index(0)
        total = part[g, z, y, :, LANES:] + qy_in[g, n].astype(F32)
        return total + qz_in[g, 0, last].astype(F32) + qz_in[g, 1, last].astype(F32)

    def finish_p(g):
        arrived(g, "py")
        if g == 0:
            total = part[g, z, y, :, :LANES]
        else:
            total = half_block(z, slice(0, chp))
        total = total + py_in[g].astype(F32)
        for d in range(2):
            arrived(g, "rp", d, last)
            arrived(g, "rpd", d)
            if g == 0:
                total = total + pf_in[d, last, 0].astype(F32) + pf_in[d, last, 1].astype(F32)
            else:
                total = total + ph_in[d, last].astype(F32) + ph_diag[d].astype(F32)
        return total

    def restored(g):
        q = finish_q(g).astype(BF16)
        p = finish_p(g).astype(BF16)
        return across(place[g, :, :LANES], p) + across(place[g, :, LANES:], q)

    gather_begin(0)
    gather_begin(1)
    gather_own(0)
    gather_own(1)
    turn_columns()
    flatten_w()
    gather_step(0, 1)
    gather_step(1, 1)
    gather_pair(0)
    gather_pair(1)
    spread_w()
    gather_step(0, 2)
    gather_step(1, 2)
    split_w()
    make_spot()
    turn_p()
    gather_step(0, 3)
    gather_step(1, 3)
    expand_p(0)
    for d in NEAR_ORDER:
        arrived(0, "qy", d)
    expand_q(0)
    restore(0)
    expand_p(1)
    for d in NEAR_ORDER:
        arrived(1, "qy", d)
    expand_q(1)
    restore(1)
    convolve(0)
    convolve(1)
    complete(0)
    project(0)
    scatter_y(0, 3, -3, 4)
    scatter_p(0, 0)
    complete(1)
    project(1)
    scatter_y(1, 3, -3, 4)
    scatter_p(1, 0)
    scatter_y(0, 2, -2)
    scatter_q(0, 0)
    scatter_y(1, 2, -2)
    scatter_q(1, 0)
    scatter_p(0, 1)
    scatter_y(0, 1, -1)
    scatter_q(0, 1)
    scatter_p(1, 1)
    scatter_y(1, 1, -1)
    scatter_q(1, 1)
    scatter_y(0, 0)
    scatter_y(1, 0)
    scatter_own(0)
    scatter_own(1)
    for g in range(2):
        scatter_p(g, 2)
        scatter_q(g, 2)
    acc = restored(0)
    acc = acc + restored(1)
    out_ref[...] = acc[:, :ch].astype(BF16).reshape(out_ref.shape)
    for c in pending.values():
        c.wait_send()


def on_device(
    row_devices,
    latents,
    clip_height,
    clip_width,
    expand_weight,
    expand_bias,
    depth_weight,
    depth_bias,
    project_weight,
):
    batch, row_count, col_count, ch = latents.shape
    ff = expand_bias.shape[1]
    assert batch == 4 and row_count == 2 and col_count == HALF
    chp, ffp = ceil_to(ch, 16), ceil_to(ff, 16)
    spread = NY * NZ * chp

    vmem = pl.BlockSpec(memory_space=pltpu.VMEM)
    smem = pl.BlockSpec(memory_space=pltpu.SMEM)
    hbm = pl.BlockSpec(memory_space=pl.ANY)
    scratch = [
        pltpu.VMEM((ffp, 2, NY * NZ * ch), BF16),
        pltpu.VMEM((2 * ffp, spread + LANES), BF16),
        pltpu.VMEM((2 * ffp, spread), BF16),
        pltpu.VMEM((ff, NY * NZ * ch), BF16),
        pltpu.VMEM((NZ, NY, chp, ffp), BF16),
        pltpu.VMEM((LANES, ceil_to(ffp, LANES)), F32),
        pltpu.VMEM((ffp, LANES), F32),
        pltpu.VMEM((22, ffp, LANES), F32),
        pltpu.VMEM((2, batch * LANES, PAIR), BF16),
        pltpu.VMEM((2, PAIR, PAIR), BF16),
        pltpu.VMEM((NY, NZ, chp, LANES), BF16),
        pltpu.VMEM((NZ, chp, LANES), BF16),
        pltpu.VMEM((2, NY, NZ, chp, LANES), BF16),
        pltpu.VMEM((chp, LANES), BF16),
        pltpu.VMEM((chp, LANES), BF16),
        pltpu.VMEM((2, chp, LANES), BF16),
        pltpu.VMEM((2, chp, LANES), BF16),
        pltpu.VMEM((2 * ffp, PAIR), BF16),
        pltpu.VMEM((2, 2, ffp, PAIR), F32),
        pltpu.VMEM((2, 2, ffp, PAIR), F32),
        pltpu.VMEM((2, 3, 2, ffp, PAIR), F32),
        pltpu.VMEM((2, ffp, PAIR), BF16),
        pltpu.VMEM((2, ffp, PAIR), BF16),
        pltpu.VMEM((2, ffp, PAIR), BF16),
        pltpu.VMEM((2, ffp, PAIR), BF16),
        pltpu.VMEM((ffp, PAIR), BF16),
        pltpu.VMEM((ffp, PAIR), BF16),
        pltpu.VMEM((2, NZ, NY, chp, PAIR), F32),
        pltpu.VMEM((2, FAR, NY, chp, LANES), BF16),
        pltpu.VMEM((2, FAR, NY, chp, LANES), BF16),
        pltpu.VMEM((2, FAR, chp, LANES), BF16),
        pltpu.VMEM((2, FAR, chp, LANES), BF16),
        pltpu.VMEM((2, chp, LANES), BF16),
        pltpu.VMEM((2, 2, FAR, chp, LANES), BF16),
        pltpu.VMEM((2, 2, FAR, chp, LANES), BF16),
        pltpu.VMEM((2, NZ, chp, LANES), BF16),
        pltpu.VMEM((2, NZ, chp, LANES), BF16),
        pltpu.VMEM((2, chp, LANES), BF16),
        pltpu.VMEM((2, chp, LANES), BF16),
        pltpu.SemaphoreType.DMA((2,)),
        pltpu.SemaphoreType.DMA((128,)),
        pltpu.SemaphoreType.DMA((128,)),
    ]
    return pl.pallas_call(
        functools.partial(kernel, row_devices),
        out_shape=jax.ShapeDtypeStruct(latents.shape, BF16),
        in_specs=[vmem, smem, smem, hbm, vmem, vmem, vmem, hbm],
        out_specs=vmem,
        scratch_shapes=scratch,
        compiler_params=pltpu.CompilerParams(
            collective_id=0, has_side_effects=True, vmem_limit_bytes=60 * 1024 * 1024
        ),
    )(
        latents,
        clip_height,
        clip_width,
        expand_weight.transpose(2, 0, 1),
        expand_bias,
        depth_weight,
        depth_bias,
        project_weight,
    )


def solution(mesh):
    in_specs = (
        P(None, "row", None, "tensor"),
        P(),
        P(),
        P(None, None, "tensor"),
        P(None, "tensor"),
        P(None, None, None, "tensor"),
        P(None, "tensor"),
        P("tensor", None),
    )
    return jax.shard_map(
        functools.partial(on_device, mesh.shape["row"]),
        mesh=mesh,
        in_specs=in_specs,
        out_specs=P(None, "row", None, "tensor"),
        check_vma=False,
    )
```

```python
import functools

import jax
import jax.numpy as jnp
from jax import lax
from jax.experimental import pallas as pl
from jax.experimental.pallas import tpu as pltpu
from jax.sharding import PartitionSpec as P

MESH = pl.DeviceIdType.MESH
NY, NZ = 2, 8
FAR = NZ // 2
LANES = 128
HALF = LANES // 2
PAIR = 2 * LANES
BF16 = jnp.bfloat16
F32 = jnp.float32
NEAR_ORDER = (2, -2, 1, -1, 0)
STEPS = FAR - 1


def ceil_to(n, m):
    return -(-n // m) * m


def silu(v):
    h = 0.5 * v
    return h + h * jnp.tanh(h)


def iota(shape, dim):
    return lax.broadcasted_iota(jnp.int32, shape, dim)


def one_hot(cond):
    return jnp.where(cond, 1.0, 0.0).astype(BF16)


def across(a, b):
    return lax.dot_general(a, b, (((1,), (1,)), ((), ())), preferred_element_type=F32)


def kernel(
    rows,
    x_ref,
    height_ref,
    width_ref,
    w_hbm,
    bias_ref,
    taps_ref,
    shift_ref,
    p_hbm,
    out_ref,
    w_raw,
    w_flat,
    w_ref,
    p_raw,
    p_ref,
    rows_s,
    cols_s,
    taps_s,
    place,
    spot,
    xp_full,
    xp_half,
    xq,
    hx_out,
    hx_in,
    hx_own,
    hx_diag,
    ec,
    ex,
    turned,
    sums,
    dn_out,
    up_out,
    dn_in,
    up_in,
    hid,
    hc,
    part,
    pf_out,
    pf_in,
    ph_out,
    ph_in,
    ph_diag,
    qz_out,
    qz_in,
    qd_out,
    qd_in,
    qy_out,
    qy_in,
    py_out,
    py_in,
    load,
    send,
    recv,
):
    r = lax.axis_index("row")
    t = lax.axis_index("tensor")
    y, z = t // NZ, t % NZ
    clips, row_count, col_count, ch = x_ref.shape
    ff, ffp, chp = bias_ref.shape[1], ex.shape[2], xq.shape[3]
    wide, spread = NY * NZ * ch, NY * NZ * chp
    cut = ceil_to(chp // 2, 16)

    def tz(step):
        return (z + NZ + step) % NZ

    ring = ({"tensor": y * NZ + tz(1)}, {"tensor": y * NZ + tz(-1)})
    ring2 = ({"tensor": y * NZ + tz(2)}, {"tensor": y * NZ + tz(-2)})
    other = {"tensor": (1 - y) * NZ + z}
    diag = ({"tensor": (1 - y) * NZ + tz(1)}, {"tensor": (1 - y) * NZ + tz(-1)})
    above = {"row": (r + rows - 1) % rows}
    below = {"row": (r + 1) % rows}

    w_load = pltpu.make_async_copy(w_hbm, w_raw.at[pl.ds(0, ff)], load.at[0])
    p_load = pltpu.make_async_copy(p_hbm, p_raw, load.at[1])
    w_load.start()
    p_load.start()

    diag2 = ({"tensor": (1 - y) * NZ + tz(2)}, {"tensor": (1 - y) * NZ + tz(-2)})
    barrier = pltpu.get_barrier_semaphore()
    for target in ring + ring2 + diag + diag2 + (other, above, below):
        pl.semaphore_signal(barrier, inc=1, device_id=target, device_id_type=MESH)

    pending = {}

    def start(key, src, dst, target):
        n = len(pending)
        c = pltpu.make_async_remote_copy(
            src_ref=src,
            dst_ref=dst,
            send_sem=send.at[n],
            recv_sem=recv.at[n],
            device_id=target,
            device_id_type=MESH,
        )
        c.start()
        pending[key] = c

    def same(key, ref, target):
        start(key, ref, ref, target)

    def arrived(*key):
        pending[key].wait_recv()

    widths = [width_ref[b] for b in range(clips)]
    heights = [height_ref[b] for b in range(clips)]
    narrow = jnp.int32(clips - 1)
    for b in reversed(range(clips - 1)):
        narrow = jnp.where(widths[b] == col_count // 2, b, narrow)
    slots = [jnp.where(narrow == b, clips - 1, jnp.where(narrow < b, b - 1, b)) for b in range(clips)]

    def of_slot(s, values):
        total = jnp.int32(0)
        for b in range(clips):
            total = total + jnp.where(slots[b] == s, values[b], 0)
        return total

    slot_w = [of_slot(s, widths) for s in range(clips)]
    slot_h = [of_slot(s, heights) for s in range(clips)]

    sub, lane2 = iota((LANES, PAIR), 0), iota((LANES, PAIR), 1)
    sub_row, sub_col = sub // HALF, sub % HALF
    canvas_row = row_count * r + sub_row

    def make_place():
        for g in range(2):
            for b in range(clips):
                limit = jnp.where(slots[b] // 2 == g, widths[b], 0)
                first_slot = jnp.where(slots[b] == 2 * g + 1, 2 * slot_w[2 * g], 0)
                a = first_slot + sub_row * widths[b] + sub_col
                if g == 1:
                    a = jnp.where(a < HALF, a + HALF * y, a + HALF)
                ok = (sub_col < limit) & (canvas_row < heights[b])
                place[g, b * LANES : (b + 1) * LANES] = one_hot(ok & (lane2 == a))

    def make_spot():
        for g in range(2):
            for s in range(2):
                w, h = slot_w[2 * g + s], slot_h[2 * g + s]
                a = s * 2 * slot_w[2 * g] + sub_row * w + sub_col
                ok = (sub_col < w) & (canvas_row < h)
                if g == 0:
                    hit = lane2 == a
                else:
                    hit = (lane2 == a + HALF) | ((a < HALF) & (lane2 == a))
                spot[g, s * LANES : (s + 1) * LANES] = one_hot(ok & hit)

    make_place()
    tokens = x_ref[...].reshape(clips * LANES, ch).T
    for g in range(2):
        block = jnp.dot(tokens, place[g], preferred_element_type=F32).astype(BF16)
        empty = jnp.zeros((chp - ch, LANES), BF16)
        if g == 0:
            xp_full[y, z, 0:ch] = block[:, :LANES]
            xp_full[y, z, ch:chp] = empty
        else:
            hx_out[0:ch] = block[:, :LANES]
            hx_out[ch:chp] = empty
        xq[g, y, z, 0:ch] = block[:, LANES:]
        xq[g, y, z, ch:chp] = empty

    pl.semaphore_wait(barrier, 11)

    def gather_begin(g):
        for d in range(2):
            if g == 0:
                same((g, "own", d), xp_full.at[y, z], ring[d])
            else:
                start((g, "own", d), hx_out, hx_own.at[d], ring[d])
        for d in range(2):
            if g == 0:
                same((g, "p", d, 0), xp_full.at[y, z], diag[d])
            else:
                start((g, "p", d, 0), hx_out, hx_diag.at[d], diag[d])
        for d in range(2):
            same((g, "q", d, 0), xq.at[g, y, z], ring[d])

    def gather_own(g):
        if g == 0:
            same((g, "y"), xp_full.at[y, z], other)
        else:
            start((g, "y"), hx_out, hx_in, other)
        same((g, "qy", 0), xq.at[g, y, z], other)

    def gather_pair(g):
        arrived(g, "y")
        if g == 1:
            xp_half[z] = hx_out[...] + hx_in[...]

    def cut_at(d):
        return pl.ds(0, cut) if d == 0 else pl.ds(cut, chp - cut)

    def gather_step(g, s):
        for d in range(2):
            zz = tz(-s if d == 0 else s)
            arrived(g, "p", d, s - 1)
            if s == 1:
                arrived(g, "own", d)
                if g == 1:
                    xp_half[zz] = hx_own[d] + hx_diag[d]
            src = xp_full.at[:, zz] if g == 0 else xp_half.at[zz]
            same((g, "p", d, s), src, ring[d])
            if s == 2:
                src = xp_full.at[d, zz] if g == 0 else xp_half.at[zz, cut_at(d)]
                same((g, "pf", d), src, ring2[d])
        for d in range(2):
            zz = tz(-s if d == 0 else s)
            arrived(g, "q", d, s - 1)
            same((g, "q", d, s), xq.at[g, y, zz], ring[d])
            if s == 2:
                same((g, "qd", d), xq.at[g, y, zz], diag[d])
                same((g, "qf", d), xq.at[g, y, zz, cut_at(d)], ring2[d])
                same((g, "qfd", d), xq.at[g, y, zz, cut_at(d)], diag2[d])
            same((g, "qy", d, s), xq.at[g, y, zz], other)

    def gathered_p(g):
        for d in range(2):
            arrived(g, "p", d, 2)
            arrived(g, "pf", d)

    def gathered_q(g):
        arrived(g, "qy", 0)
        for d in range(2):
            arrived(g, "qy", d, 1)
            arrived(g, "qy", d, 2)
            for key in ("qd", "qf", "qfd"):
                arrived(g, key, d)
            arrived(g, "q", d, 2)

    def flatten_w():
        w_flat[:, wide:] = jnp.zeros((2 * ffp, w_flat.shape[1] - wide), BF16)
        w_load.wait()
        w_raw[ff:ffp] = jnp.zeros((ffp - ff, 2, wide), BF16)

        def body(i, _):
            dst = pl.ds(pl.multiple_of(i * 32, 32), 32)
            w_flat[dst, 0:wide] = w_raw[pl.ds(i * 16, 16)].reshape(32, wide)
            return 0

        lax.fori_loop(0, ffp // 16, body, 0)

    def spread_w():
        for j in range(spread // LANES):
            c = LANES * j + iota((PAIR, LANES), 1)
            begin = LANES * j - (chp - ch) * (LANES * j // chp)
            base = begin // LANES * LANES
            p = base + iota((PAIR, LANES), 0)
            owner = c // chp
            pick = one_hot((p == c - (chp - ch) * owner) & (c - chp * owner < ch))
            moved = jnp.dot(w_flat[:, base : base + PAIR], pick, preferred_element_type=F32)
            w_ref[:, LANES * j : LANES * (j + 1)] = moved.astype(BF16)

    def split_w():
        to, at = iota((2 * ffp, 2 * ffp), 0), iota((2 * ffp, 2 * ffp), 1)
        pick = one_hot(at == jnp.where(to < ffp, 2 * to, 2 * (to - ffp) + 1))
        for n in range(spread // PAIR):
            sl = slice(PAIR * n, PAIR * (n + 1))
            w_ref[:, sl] = jnp.dot(pick, w_ref[:, sl], preferred_element_type=F32).astype(BF16)

    def turn_p():
        p_ref[...] = jnp.zeros_like(p_ref)
        p_load.wait()
        for zz in range(NZ):
            for yy in range(NY):
                o = yy * NZ + zz
                p_ref[zz, yy, 0:ch, 0:ff] = p_raw[:, ch * o : ch * (o + 1)].T

    def turn_columns():
        rows_s[...] = jnp.zeros_like(rows_s)
        rows_s[0:2, 0:ff] = bias_ref[...]
        rows_s[2:4, 0:ff] = shift_ref[...]
        for i in range(3):
            for j in range(3):
                n = 4 + 2 * (3 * i + j)
                rows_s[n : n + 2, 0:ff] = taps_ref[i, j]
        cols_s[...] = rows_s[...].T[:ffp]

        def wide_col(n):
            return jnp.broadcast_to(cols_s[:, n : n + 1], (ffp, LANES))

        for n in range(4):
            taps_s[n] = wide_col(n)
        for m in range(6):
            above_tap, below_tap = wide_col(4 + m), wide_col(16 + m)
            taps_s[4 + m] = wide_col(10 + m)
            taps_s[10 + m] = jnp.where(first, below_tap, above_tap)
            taps_s[16 + m] = jnp.where(first, above_tap, below_tap)

    lane = iota((1, LANES), 1)
    first = lane < HALF
    col = lane % HALF
    left_ok = col > 0
    right_ok = col < HALF - 1
    edge_row = row_count * r + jnp.where(first, -1, row_count)
    edge_ok = (edge_row >= 0) & (edge_row < rows * row_count)

    def expand_p(g):
        if g == 0:
            x = xp_full[...].reshape(spread, LANES)
            pre = jnp.dot(w_ref[...], x, preferred_element_type=F32)
        else:
            x = xp_half[...].reshape(spread // 2, LANES)
            pre = jnp.dot(w_ref[:, : spread // 2], x, preferred_element_type=F32)
            more = jnp.dot(w_ref[:, spread // 2 :], x, preferred_element_type=F32)
            pre = jnp.where(first, pre + pltpu.roll(more, HALF, 1), 0.0)
        for k in range(2):
            value = silu(pre[k * ffp : (k + 1) * ffp] + taps_s[k])
            if g == 1:
                value = jnp.where(first, value, 0.0)
            ec[k * ffp : (k + 1) * ffp, :LANES] = value.astype(BF16)

    def expand_q(g):
        x = xq[g].reshape(spread, LANES)
        pre = jnp.dot(w_ref[...], x, preferred_element_type=F32)
        for k in range(2):
            value = silu(pre[k * ffp : (k + 1) * ffp] + taps_s[k])
            ec[k * ffp : (k + 1) * ffp, LANES:] = value.astype(BF16)

    def restore(g):
        for k in range(2):
            ex[g, k] = across(ec[k * ffp : (k + 1) * ffp], spot[g])

        def body(i, _):
            at = pl.ds(pl.multiple_of(i * 16, 16), 16)
            for s in range(2):
                sl = slice(s * LANES, (s + 1) * LANES)
                e0, e1 = ex[g, 0, at, sl], ex[g, 1, at, sl]
                t0, t1 = pltpu.roll(e0, HALF, 1), pltpu.roll(e1, HALF, 1)
                turned[g, 0, at, sl] = t0
                turned[g, 1, at, sl] = t1
                dn_out[g, at, sl] = jnp.where(first, t0, e1).astype(BF16)
                up_out[g, at, sl] = jnp.where(first, e0, t1).astype(BF16)
            return 0

        lax.fori_loop(0, ffp // 16, body, 0, unroll=11)
        start((g, "dn"), dn_out.at[g], dn_in.at[g], below)
        start((g, "up"), up_out.at[g], up_in.at[g], above)

    def convolve(g):
        def body(i, _):
            at = pl.ds(pl.multiple_of(i * 16, 16), 16)
            for k in range(2):
                for s in range(2):
                    sl = slice(s * LANES, (s + 1) * LANES)
                    mid, swap = ex[g, k, at, sl], turned[g, k, at, sl]
                    for j in range(3):
                        n = 2 * j + k
                        total = taps_s[4 + n, at] * mid + taps_s[10 + n, at] * swap
                        sums[g, j, k, at, sl] = total
            return 0

        lax.fori_loop(0, ffp // 16, body, 0, unroll=2)

    def complete(g):
        arrived(g, "dn")
        arrived(g, "up")

        def body(i, _):
            at = pl.ds(pl.multiple_of(i * 16, 16), 16)
            for s in range(2):
                sl = slice(s * LANES, (s + 1) * LANES)
                dn, up = dn_in[g, at, sl].astype(F32), up_in[g, at, sl].astype(F32)
                edges = (
                    jnp.where(first, dn, pltpu.roll(up, HALF, 1)),
                    jnp.where(first, pltpu.roll(dn, HALF, 1), up),
                )
                outs = []
                for k in range(2):
                    edge = jnp.where(edge_ok, edges[k], 0.0)
                    got = [sums[g, j, k, at, sl] + taps_s[16 + 2 * j + k, at] * edge for j in range(3)]
                    res = got[1] + taps_s[2 + k, at]
                    res = res + jnp.where(left_ok, pltpu.roll(got[0], 1, 1), 0.0)
                    res = res + jnp.where(right_ok, pltpu.roll(got[2], LANES - 1, 1), 0.0)
                    outs.append(res)
                hid[at, sl] = (outs[0] * silu(outs[1])).astype(BF16)
            return 0

        lax.fori_loop(0, ffp // 16, body, 0, unroll=2)

    def project(g):
        hc[...] = jnp.dot(hid[...], spot[g], preferred_element_type=F32).astype(BF16)
        p = p_ref[...].reshape(spread, ffp)
        part[g] = jnp.dot(p, hc[...], preferred_element_type=F32).reshape(NZ, NY, chp, PAIR)

    def scatter_y(g, *steps):
        for d in steps:
            n = NEAR_ORDER.index(d)
            qy_out[g, n] = part[g, tz(d), 1 - y, :, LANES:].astype(BF16)
            start((g, "ry", d), qy_out.at[g, n], qy_in.at[g, n], other)

    last = STEPS - 1

    def cut_of(d):
        return slice(0, cut) if d == 0 else slice(cut, chp)

    def half_block(zz, at):
        return jnp.where(first, part[1, zz, 0, at, :LANES], part[1, zz, 1, at, :LANES])

    def scatter_p(g, s):
        for d in range(2):
            zz = tz(STEPS - s if d == 0 else s - STEPS)
            near = cut_of(d)
            if s == 0:
                if g == 0:
                    pf_out[d, STEPS, d] = part[0, tz(FAR), d, :, :LANES].astype(BF16)
                    src, dst = pf_out.at[d, STEPS, d], pf_in.at[d, STEPS, d]
                else:
                    ph_out[d, STEPS, near] = half_block(tz(FAR), near).astype(BF16)
                    src, dst = ph_out.at[d, STEPS, near], ph_in.at[d, STEPS, near]
                start((g, "rpf", d), src, dst, ring2[d])
            if s > 0:
                arrived(g, "rp", d, s - 1)
            if s == 1:
                arrived(g, "rpf", d)
            if g == 0:
                for yy in range(NY):
                    total = part[0, zz, yy, :, :LANES]
                    if s > 0:
                        total = total + pf_in[d, s - 1, yy].astype(F32)
                    if s == 1 and yy == d:
                        total = total + pf_in[d, STEPS, yy].astype(F32)
                    pf_out[d, s, yy] = total.astype(BF16)
                if s < last:
                    src, dst = pf_out.at[d, s], pf_in.at[d, s]
                else:
                    src, dst = pf_out.at[d, s, 1 - y], pf_in.at[d, s, 1]
                    start((g, "rpd", d), src, dst, diag[d])
                    src, dst = pf_out.at[d, s, y], pf_in.at[d, s, 0]
            else:
                for e in range(2):
                    at = cut_of(e)
                    total = half_block(zz, at)
                    if s > 0:
                        total = total + ph_in[d, s - 1, at].astype(F32)
                    if s == 1 and e == d:
                        total = total + ph_in[d, STEPS, at].astype(F32)
                    ph_out[d, s, at] = total.astype(BF16)
                src, dst = ph_out.at[d, s], ph_in.at[d, s]
                if s == last:
                    start((g, "rpd", d), src, ph_diag.at[d], diag[d])
            start((g, "rp", d, s), src, dst, ring[d])

    def q_block(g, step, at):
        n = NEAR_ORDER.index(step)
        return part[g, tz(step), y, at, LANES:] + qy_in[g, n, at].astype(F32)

    def scatter_q(g, s):
        for d in range(2):
            step = STEPS - s if d == 0 else s - STEPS
            if s == 0:
                near = cut_of(d)
                qz_out[g, d, 0] = part[g, tz(step), y, :, LANES:].astype(BF16)
                qd_out[g, d, 0] = part[g, tz(step), 1 - y, :, LANES:].astype(BF16)
                qz_out[g, d, STEPS, near] = part[g, tz(FAR), y, near, LANES:].astype(BF16)
                qd_out[g, d, 1, near] = part[g, tz(FAR), 1 - y, near, LANES:].astype(BF16)
                src, dst = qz_out.at[g, d, STEPS, near], qz_in.at[g, d, STEPS, near]
                start((g, "rqf", d), src, dst, ring2[d])
                src, dst = qd_out.at[g, d, 1, near], qd_in.at[g, d, 1, near]
                start((g, "rqfd", d), src, dst, diag2[d])
                start((g, "rqd", d), qd_out.at[g, d, 0], qd_in.at[g, d, 0], diag[d])
            else:
                arrived(g, "ry", step)
                arrived(g, "rq", d, s - 1)
                if s == 1:
                    for key in ("rqf", "rqfd", "rqd"):
                        arrived(g, key, d)
                for e in range(2):
                    at = cut_of(e)
                    total = q_block(g, step, at) + qz_in[g, d, s - 1, at].astype(F32)
                    if s == 1:
                        total = total + qd_in[g, d, 0, at].astype(F32)
                        if e == d:
                            total = total + qz_in[g, d, STEPS, at].astype(F32)
                            total = total + qd_in[g, d, 1, at].astype(F32)
                    qz_out[g, d, s, at] = total.astype(BF16)
            start((g, "rq", d, s), qz_out.at[g, d, s], qz_in.at[g, d, s], ring[d])

    def scatter_own(g):
        if g == 0:
            py_out[g] = part[g, z, 1 - y, :, :LANES].astype(BF16)
        else:
            py_out[g] = half_block(z, slice(0, chp)).astype(BF16)
        start((g, "py"), py_out.at[g], py_in.at[g], other)

    def finish_q(g):
        for d in range(2):
            arrived(g, "rq", d, last)
        arrived(g, "ry", 0)
        n = NEAR_ORDER.index(0)
        total = part[g, z, y, :, LANES:] + qy_in[g, n].astype(F32)
        return total + qz_in[g, 0, last].astype(F32) + qz_in[g, 1, last].astype(F32)

    def finish_p(g):
        arrived(g, "py")
        if g == 0:
            total = part[g, z, y, :, :LANES]
        else:
            total = half_block(z, slice(0, chp))
        total = total + py_in[g].astype(F32)
        for d in range(2):
            arrived(g, "rp", d, last)
            arrived(g, "rpd", d)
            if g == 0:
                total = total + pf_in[d, last, 0].astype(F32) + pf_in[d, last, 1].astype(F32)
            else:
                total = total + ph_in[d, last].astype(F32) + ph_diag[d].astype(F32)
        return total

    def restored(g):
        q = finish_q(g).astype(BF16)
        p = finish_p(g).astype(BF16)
        return across(place[g, :, :LANES], p) + across(place[g, :, LANES:], q)

    gather_begin(0)
    gather_begin(1)
    gather_own(0)
    gather_own(1)
    turn_columns()
    flatten_w()
    gather_step(0, 1)
    gather_step(1, 1)
    gather_pair(0)
    gather_pair(1)
    spread_w()
    gather_step(0, 2)
    gather_step(1, 2)
    split_w()
    make_spot()
    turn_p()
    gathered_p(0)
    expand_p(0)
    gathered_q(0)
    expand_q(0)
    restore(0)
    gathered_p(1)
    expand_p(1)
    gathered_q(1)
    expand_q(1)
    restore(1)
    convolve(0)
    convolve(1)
    complete(0)
    project(0)
    scatter_p(0, 0)
    scatter_q(0, 0)
    scatter_y(0, 2, -2)
    complete(1)
    project(1)
    scatter_p(1, 0)
    scatter_q(1, 0)
    scatter_y(1, 2, -2)
    scatter_y(0, 1, -1)
    scatter_p(0, 1)
    scatter_q(0, 1)
    scatter_y(1, 1, -1)
    scatter_p(1, 1)
    scatter_q(1, 1)
    scatter_y(0, 0)
    scatter_y(1, 0)
    scatter_own(0)
    scatter_own(1)
    for g in range(2):
        scatter_p(g, 2)
        scatter_q(g, 2)
    acc = restored(0)
    acc = acc + restored(1)
    out_ref[...] = acc[:, :ch].astype(BF16).reshape(out_ref.shape)
    for c in pending.values():
        c.wait_send()


def on_device(
    row_devices,
    latents,
    clip_height,
    clip_width,
    expand_weight,
    expand_bias,
    depth_weight,
    depth_bias,
    project_weight,
):
    batch, row_count, col_count, ch = latents.shape
    ff = expand_bias.shape[1]
    assert batch == 4 and row_count == 2 and col_count == HALF
    chp, ffp = ceil_to(ch, 16), ceil_to(ff, 16)
    spread = NY * NZ * chp

    vmem = pl.BlockSpec(memory_space=pltpu.VMEM)
    smem = pl.BlockSpec(memory_space=pltpu.SMEM)
    hbm = pl.BlockSpec(memory_space=pl.ANY)
    scratch = [
        pltpu.VMEM((ffp, 2, NY * NZ * ch), BF16),
        pltpu.VMEM((2 * ffp, spread + LANES), BF16),
        pltpu.VMEM((2 * ffp, spread), BF16),
        pltpu.VMEM((ff, NY * NZ * ch), BF16),
        pltpu.VMEM((NZ, NY, chp, ffp), BF16),
        pltpu.VMEM((LANES, ceil_to(ffp, LANES)), F32),
        pltpu.VMEM((ffp, LANES), F32),
        pltpu.VMEM((22, ffp, LANES), F32),
        pltpu.VMEM((2, batch * LANES, PAIR), BF16),
        pltpu.VMEM((2, PAIR, PAIR), BF16),
        pltpu.VMEM((NY, NZ, chp, LANES), BF16),
        pltpu.VMEM((NZ, chp, LANES), BF16),
        pltpu.VMEM((2, NY, NZ, chp, LANES), BF16),
        pltpu.VMEM((chp, LANES), BF16),
        pltpu.VMEM((chp, LANES), BF16),
        pltpu.VMEM((2, chp, LANES), BF16),
        pltpu.VMEM((2, chp, LANES), BF16),
        pltpu.VMEM((2 * ffp, PAIR), BF16),
        pltpu.VMEM((2, 2, ffp, PAIR), F32),
        pltpu.VMEM((2, 2, ffp, PAIR), F32),
        pltpu.VMEM((2, 3, 2, ffp, PAIR), F32),
        pltpu.VMEM((2, ffp, PAIR), BF16),
        pltpu.VMEM((2, ffp, PAIR), BF16),
        pltpu.VMEM((2, ffp, PAIR), BF16),
        pltpu.VMEM((2, ffp, PAIR), BF16),
        pltpu.VMEM((ffp, PAIR), BF16),
        pltpu.VMEM((ffp, PAIR), BF16),
        pltpu.VMEM((2, NZ, NY, chp, PAIR), F32),
        pltpu.VMEM((2, FAR, NY, chp, LANES), BF16),
        pltpu.VMEM((2, FAR, NY, chp, LANES), BF16),
        pltpu.VMEM((2, FAR, chp, LANES), BF16),
        pltpu.VMEM((2, FAR, chp, LANES), BF16),
        pltpu.VMEM((2, chp, LANES), BF16),
        pltpu.VMEM((2, 2, FAR, chp, LANES), BF16),
        pltpu.VMEM((2, 2, FAR, chp, LANES), BF16),
        pltpu.VMEM((2, 2, 2, chp, LANES), BF16),
        pltpu.VMEM((2, 2, 2, chp, LANES), BF16),
        pltpu.VMEM((2, NZ, chp, LANES), BF16),
        pltpu.VMEM((2, NZ, chp, LANES), BF16),
        pltpu.VMEM((2, chp, LANES), BF16),
        pltpu.VMEM((2, chp, LANES), BF16),
        pltpu.SemaphoreType.DMA((2,)),
        pltpu.SemaphoreType.DMA((128,)),
        pltpu.SemaphoreType.DMA((128,)),
    ]
    return pl.pallas_call(
        functools.partial(kernel, row_devices),
        out_shape=jax.ShapeDtypeStruct(latents.shape, BF16),
        in_specs=[vmem, smem, smem, hbm, vmem, vmem, vmem, hbm],
        out_specs=vmem,
        scratch_shapes=scratch,
        compiler_params=pltpu.CompilerParams(
            collective_id=0, has_side_effects=True, vmem_limit_bytes=60 * 1024 * 1024
        ),
    )(
        latents,
        clip_height,
        clip_width,
        expand_weight.transpose(2, 0, 1),
        expand_bias,
        depth_weight,
        depth_bias,
        project_weight,
    )


def solution(mesh):
    in_specs = (
        P(None, "row", None, "tensor"),
        P(),
        P(),
        P(None, None, "tensor"),
        P(None, "tensor"),
        P(None, None, None, "tensor"),
        P(None, "tensor"),
        P("tensor", None),
    )
    return jax.shard_map(
        functools.partial(on_device, mesh.shape["row"]),
        mesh=mesh,
        in_specs=in_specs,
        out_specs=P(None, "row", None, "tensor"),
        check_vma=False,
    )
```

```python
import functools

import jax
import jax.numpy as jnp
from jax import lax
from jax.experimental import pallas as pl
from jax.experimental.pallas import tpu as pltpu
from jax.sharding import PartitionSpec as P

MESH = pl.DeviceIdType.MESH
NY, NZ = 2, 8
FAR = NZ // 2
LANES = 128
HALF = LANES // 2
PAIR = 2 * LANES
BF16 = jnp.bfloat16
F32 = jnp.float32
NEAR_ORDER = (3, -3, 4, 2, -2, 1, -1, 0)
STEPS = FAR - 1


def ceil_to(n, m):
    return -(-n // m) * m


def silu(v):
    h = 0.5 * v
    return h + h * jnp.tanh(h)


def iota(shape, dim):
    return lax.broadcasted_iota(jnp.int32, shape, dim)


def one_hot(cond):
    return jnp.where(cond, 1.0, 0.0).astype(BF16)


def across(a, b):
    return lax.dot_general(a, b, (((1,), (1,)), ((), ())), preferred_element_type=F32)


def kernel(
    rows,
    x_ref,
    height_ref,
    width_ref,
    w_hbm,
    bias_ref,
    taps_ref,
    shift_ref,
    p_hbm,
    out_ref,
    w_raw,
    w_flat,
    w_ref,
    p_raw,
    p_ref,
    rows_s,
    cols_s,
    taps_s,
    place,
    spot,
    xp_full,
    xp_half,
    xq,
    hx_out,
    hx_in,
    hx_own,
    hx_diag,
    ec,
    ex,
    turned,
    sums,
    dn_out,
    up_out,
    dn_in,
    up_in,
    hid,
    hc,
    part,
    pf_out,
    pf_in,
    ph_out,
    ph_in,
    ph_diag,
    qz_out,
    qz_in,
    qy_out,
    qy_in,
    py_out,
    py_in,
    load,
    send,
    recv,
):
    r = lax.axis_index("row")
    t = lax.axis_index("tensor")
    y, z = t // NZ, t % NZ
    clips, row_count, col_count, ch = x_ref.shape
    ff, ffp, chp = bias_ref.shape[1], ex.shape[2], xq.shape[3]
    wide, spread = NY * NZ * ch, NY * NZ * chp
    cut = ceil_to(chp // 2, 16)

    def tz(step):
        return (z + NZ + step) % NZ

    ring = ({"tensor": y * NZ + tz(1)}, {"tensor": y * NZ + tz(-1)})
    ring2 = ({"tensor": y * NZ + tz(2)}, {"tensor": y * NZ + tz(-2)})
    other = {"tensor": (1 - y) * NZ + z}
    diag = ({"tensor": (1 - y) * NZ + tz(1)}, {"tensor": (1 - y) * NZ + tz(-1)})
    above = {"row": (r + rows - 1) % rows}
    below = {"row": (r + 1) % rows}

    w_load = pltpu.make_async_copy(w_hbm, w_raw.at[pl.ds(0, ff)], load.at[0])
    p_load = pltpu.make_async_copy(p_hbm, p_raw, load.at[1])
    w_load.start()
    p_load.start()

    barrier = pltpu.get_barrier_semaphore()
    for target in ring + ring2 + diag + (other, above, below):
        pl.semaphore_signal(barrier, inc=1, device_id=target, device_id_type=MESH)

    pending = {}

    def start(key, src, dst, target):
        n = len(pending)
        c = pltpu.make_async_remote_copy(
            src_ref=src,
            dst_ref=dst,
            send_sem=send.at[n],
            recv_sem=recv.at[n],
            device_id=target,
            device_id_type=MESH,
        )
        c.start()
        pending[key] = c

    def same(key, ref, target):
        start(key, ref, ref, target)

    def arrived(*key):
        pending[key].wait_recv()

    widths = [width_ref[b] for b in range(clips)]
    heights = [height_ref[b] for b in range(clips)]
    narrow = jnp.int32(clips - 1)
    for b in reversed(range(clips - 1)):
        narrow = jnp.where(widths[b] == col_count // 2, b, narrow)
    slots = [jnp.where(narrow == b, clips - 1, jnp.where(narrow < b, b - 1, b)) for b in range(clips)]

    def of_slot(s, values):
        total = jnp.int32(0)
        for b in range(clips):
            total = total + jnp.where(slots[b] == s, values[b], 0)
        return total

    slot_w = [of_slot(s, widths) for s in range(clips)]
    slot_h = [of_slot(s, heights) for s in range(clips)]

    sub, lane2 = iota((LANES, PAIR), 0), iota((LANES, PAIR), 1)
    sub_row, sub_col = sub // HALF, sub % HALF
    canvas_row = row_count * r + sub_row

    def make_place(g):
        for b in range(clips):
            limit = jnp.where(slots[b] // 2 == g, widths[b], 0)
            first_slot = jnp.where(slots[b] == 2 * g + 1, 2 * slot_w[2 * g], 0)
            a = first_slot + sub_row * widths[b] + sub_col
            if g == 1:
                a = jnp.where(a < HALF, a + HALF * y, a + HALF)
            ok = (sub_col < limit) & (canvas_row < heights[b])
            place[g, b * LANES : (b + 1) * LANES] = one_hot(ok & (lane2 == a))

    def make_spot():
        for g in range(2):
            for s in range(2):
                w, h = slot_w[2 * g + s], slot_h[2 * g + s]
                a = s * 2 * slot_w[2 * g] + sub_row * w + sub_col
                ok = (sub_col < w) & (canvas_row < h)
                if g == 0:
                    hit = lane2 == a
                else:
                    hit = (lane2 == a + HALF) | ((a < HALF) & (lane2 == a))
                spot[g, s * LANES : (s + 1) * LANES] = one_hot(ok & hit)

    tokens = x_ref[...].reshape(clips * LANES, ch).T

    def make_block(g):
        make_place(g)
        block = jnp.dot(tokens, place[g], preferred_element_type=F32).astype(BF16)
        empty = jnp.zeros((chp - ch, LANES), BF16)
        if g == 0:
            xp_full[y, z, 0:ch] = block[:, :LANES]
            xp_full[y, z, ch:chp] = empty
        else:
            hx_out[0:ch] = block[:, :LANES]
            hx_out[ch:chp] = empty
        xq[g, y, z, 0:ch] = block[:, LANES:]
        xq[g, y, z, ch:chp] = empty

    make_block(0)
    pl.semaphore_wait(barrier, 9)

    def gather_begin(g):
        for d in range(2):
            if g == 0:
                same((g, "own", d), xp_full.at[y, z], ring[d])
            else:
                start((g, "own", d), hx_out, hx_own.at[d], ring[d])
        for d in range(2):
            if g == 0:
                same((g, "p", d, 0), xp_full.at[y, z], diag[d])
            else:
                start((g, "p", d, 0), hx_out, hx_diag.at[d], diag[d])
        for d in range(2):
            same((g, "q", d, 0), xq.at[g, y, z], ring[d])

    def gather_own(g):
        if g == 0:
            same((g, "y"), xp_full.at[y, z], other)
        else:
            start((g, "y"), hx_out, hx_in, other)
        same((g, "qy", 0), xq.at[g, y, z], other)

    def gather_pair(g):
        arrived(g, "y")
        if g == 1:
            xp_half[z] = hx_out[...] + hx_in[...]

    def cut_at(d):
        return pl.ds(0, cut) if d == 0 else pl.ds(cut, chp - cut)

    def gather_step(g, s):
        for d in range(2):
            zz = tz(-s if d == 0 else s)
            arrived(g, "p", d, s - 1)
            if s == 1:
                arrived(g, "own", d)
                if g == 1:
                    xp_half[zz] = hx_own[d] + hx_diag[d]
            if s < STEPS:
                src = xp_full.at[:, zz] if g == 0 else xp_half.at[zz]
                same((g, "p", d, s), src, ring[d])
            if s == 2:
                src = xp_full.at[d, zz] if g == 0 else xp_half.at[zz, cut_at(d)]
                same((g, "pf", d), src, ring2[d])
        for d in range(2):
            zz = tz(-s if d == 0 else s)
            arrived(g, "q", d, s - 1)
            if s < STEPS:
                same((g, "q", d, s), xq.at[g, y, zz], ring[d])
            if s == 2:
                same((g, "qf", d), xq.at[g, y, zz, cut_at(d)], ring2[d])
            same((g, "qy", -s if d == 0 else s), xq.at[g, y, zz], other)
        if s == STEPS:
            for d in range(2):
                arrived(g, "qf", d)
            same((g, "qy", FAR), xq.at[g, y, tz(FAR)], other)
            for d in range(2):
                arrived(g, "pf", d)

    def flatten_w():
        w_flat[:, wide:] = jnp.zeros((2 * ffp, w_flat.shape[1] - wide), BF16)
        w_load.wait()
        w_raw[ff:ffp] = jnp.zeros((ffp - ff, 2, wide), BF16)

        def body(i, _):
            dst = pl.ds(pl.multiple_of(i * 32, 32), 32)
            w_flat[dst, 0:wide] = w_raw[pl.ds(i * 16, 16)].reshape(32, wide)
            return 0

        lax.fori_loop(0, ffp // 16, body, 0)

    def spread_w():
        for j in range(spread // LANES):
            c = LANES * j + iota((PAIR, LANES), 1)
            begin = LANES * j - (chp - ch) * (LANES * j // chp)
            base = begin // LANES * LANES
            p = base + iota((PAIR, LANES), 0)
            owner = c // chp
            pick = one_hot((p == c - (chp - ch) * owner) & (c - chp * owner < ch))
            moved = jnp.dot(w_flat[:, base : base + PAIR], pick, preferred_element_type=F32)
            w_ref[:, LANES * j : LANES * (j + 1)] = moved.astype(BF16)

    def split_w():
        to, at = iota((2 * ffp, 2 * ffp), 0), iota((2 * ffp, 2 * ffp), 1)
        pick = one_hot(at == jnp.where(to < ffp, 2 * to, 2 * (to - ffp) + 1))
        for n in range(spread // PAIR):
            sl = slice(PAIR * n, PAIR * (n + 1))
            w_ref[:, sl] = jnp.dot(pick, w_ref[:, sl], preferred_element_type=F32).astype(BF16)

    def turn_p():
        p_ref[...] = jnp.zeros_like(p_ref)
        p_load.wait()
        for zz in range(NZ):
            for yy in range(NY):
                o = yy * NZ + zz
                p_ref[zz, yy, 0:ch, 0:ff] = p_raw[:, ch * o : ch * (o + 1)].T

    def turn_columns():
        rows_s[...] = jnp.zeros_like(rows_s)
        rows_s[0:2, 0:ff] = bias_ref[...]
        rows_s[2:4, 0:ff] = shift_ref[...]
        for i in range(3):
            for j in range(3):
                n = 4 + 2 * (3 * i + j)
                rows_s[n : n + 2, 0:ff] = taps_ref[i, j]
        cols_s[...] = rows_s[...].T[:ffp]

        def wide_col(n):
            return jnp.broadcast_to(cols_s[:, n : n + 1], (ffp, LANES))

        for n in range(4):
            taps_s[n] = wide_col(n)
        for m in range(6):
            above_tap, below_tap = wide_col(4 + m), wide_col(16 + m)
            taps_s[4 + m] = wide_col(10 + m)
            taps_s[10 + m] = jnp.where(first, below_tap, above_tap)
            taps_s[16 + m] = jnp.where(first, above_tap, below_tap)

    lane = iota((1, LANES), 1)
    first = lane < HALF
    col = lane % HALF
    left_ok = col > 0
    right_ok = col < HALF - 1
    edge_row = row_count * r + jnp.where(first, -1, row_count)
    edge_ok = (edge_row >= 0) & (edge_row < rows * row_count)

    def expand_p(g):
        if g == 0:
            x = xp_full[...].reshape(spread, LANES)
            pre = jnp.dot(w_ref[...], x, preferred_element_type=F32)
        else:
            x = xp_half[...].reshape(spread // 2, LANES)
            pre = jnp.dot(w_ref[:, : spread // 2], x, preferred_element_type=F32)
            more = jnp.dot(w_ref[:, spread // 2 :], x, preferred_element_type=F32)
            pre = jnp.where(first, pre + pltpu.roll(more, HALF, 1), 0.0)
        for k in range(2):
            value = silu(pre[k * ffp : (k + 1) * ffp] + taps_s[k])
            if g == 1:
                value = jnp.where(first, value, 0.0)
            ec[k * ffp : (k + 1) * ffp, :LANES] = value.astype(BF16)

    def expand_q(g):
        x = xq[g].reshape(spread, LANES)
        pre = jnp.dot(w_ref[...], x, preferred_element_type=F32)
        for k in range(2):
            value = silu(pre[k * ffp : (k + 1) * ffp] + taps_s[k])
            ec[k * ffp : (k + 1) * ffp, LANES:] = value.astype(BF16)

    def restore(g):
        for k in range(2):
            ex[g, k] = across(ec[k * ffp : (k + 1) * ffp], spot[g])

        def body(i, _):
            at = pl.ds(pl.multiple_of(i * 16, 16), 16)
            for s in range(2):
                sl = slice(s * LANES, (s + 1) * LANES)
                e0, e1 = ex[g, 0, at, sl], ex[g, 1, at, sl]
                t0, t1 = pltpu.roll(e0, HALF, 1), pltpu.roll(e1, HALF, 1)
                turned[g, 0, at, sl] = t0
                turned[g, 1, at, sl] = t1
                dn_out[g, at, sl] = jnp.where(first, t0, e1).astype(BF16)
                up_out[g, at, sl] = jnp.where(first, e0, t1).astype(BF16)
            return 0

        lax.fori_loop(0, ffp // 16, body, 0, unroll=11)
        start((g, "dn"), dn_out.at[g], dn_in.at[g], below)
        start((g, "up"), up_out.at[g], up_in.at[g], above)

    def convolve(g):
        def body(i, _):
            at = pl.ds(pl.multiple_of(i * 16, 16), 16)
            for k in range(2):
                for s in range(2):
                    sl = slice(s * LANES, (s + 1) * LANES)
                    mid, swap = ex[g, k, at, sl], turned[g, k, at, sl]
                    for j in range(3):
                        n = 2 * j + k
                        total = taps_s[4 + n, at] * mid + taps_s[10 + n, at] * swap
                        sums[g, j, k, at, sl] = total
            return 0

        lax.fori_loop(0, ffp // 16, body, 0, unroll=2)

    def complete(g):
        arrived(g, "dn")
        arrived(g, "up")

        def body(i, _):
            at = pl.ds(pl.multiple_of(i * 16, 16), 16)
            for s in range(2):
                sl = slice(s * LANES, (s + 1) * LANES)
                dn, up = dn_in[g, at, sl].astype(F32), up_in[g, at, sl].astype(F32)
                edges = (
                    jnp.where(first, dn, pltpu.roll(up, HALF, 1)),
                    jnp.where(first, pltpu.roll(dn, HALF, 1), up),
                )
                outs = []
                for k in range(2):
                    edge = jnp.where(edge_ok, edges[k], 0.0)
                    got = [sums[g, j, k, at, sl] + taps_s[16 + 2 * j + k, at] * edge for j in range(3)]
                    res = got[1] + taps_s[2 + k, at]
                    res = res + jnp.where(left_ok, pltpu.roll(got[0], 1, 1), 0.0)
                    res = res + jnp.where(right_ok, pltpu.roll(got[2], LANES - 1, 1), 0.0)
                    outs.append(res)
                hid[at, sl] = (outs[0] * silu(outs[1])).astype(BF16)
            return 0

        lax.fori_loop(0, ffp // 16, body, 0, unroll=4)

    def project(g):
        hc[...] = jnp.dot(hid[...], spot[g], preferred_element_type=F32).astype(BF16)
        p = p_ref[...].reshape(spread, ffp)
        part[g] = jnp.dot(p, hc[...], preferred_element_type=F32).reshape(NZ, NY, chp, PAIR)

    def scatter_y(g, *steps):
        for d in steps:
            n = NEAR_ORDER.index(d)
            qy_out[g, n] = part[g, tz(d), 1 - y, :, LANES:].astype(BF16)
            start((g, "ry", d), qy_out.at[g, n], qy_in.at[g, n], other)

    last = STEPS - 1

    def cut_of(d):
        return slice(0, cut) if d == 0 else slice(cut, chp)

    def half_block(zz, at):
        return jnp.where(first, part[1, zz, 0, at, :LANES], part[1, zz, 1, at, :LANES])

    def scatter_p(g, s):
        for d in range(2):
            zz = tz(STEPS - s if d == 0 else s - STEPS)
            near = cut_of(d)
            if s == 0:
                if g == 0:
                    pf_out[d, STEPS, d] = part[0, tz(FAR), d, :, :LANES].astype(BF16)
                    src, dst = pf_out.at[d, STEPS, d], pf_in.at[d, STEPS, d]
                else:
                    ph_out[d, STEPS, near] = half_block(tz(FAR), near).astype(BF16)
                    src, dst = ph_out.at[d, STEPS, near], ph_in.at[d, STEPS, near]
                start((g, "rpf", d), src, dst, ring2[d])
            if s > 0:
                arrived(g, "rp", d, s - 1)
            if s == 1:
                arrived(g, "rpf", d)
            if g == 0:
                for yy in range(NY):
                    total = part[0, zz, yy, :, :LANES]
                    if s > 0:
                        total = total + pf_in[d, s - 1, yy].astype(F32)
                    if s == 1 and yy == d:
                        total = total + pf_in[d, STEPS, yy].astype(F32)
                    pf_out[d, s, yy] = total.astype(BF16)
                if s < last:
                    src, dst = pf_out.at[d, s], pf_in.at[d, s]
                else:
                    src, dst = pf_out.at[d, s, 1 - y], pf_in.at[d, s, 1]
                    start((g, "rpd", d), src, dst, diag[d])
                    src, dst = pf_out.at[d, s, y], pf_in.at[d, s, 0]
            else:
                for e in range(2):
                    at = cut_of(e)
                    total = half_block(zz, at)
                    if s > 0:
                        total = total + ph_in[d, s - 1, at].astype(F32)
                    if s == 1 and e == d:
                        total = total + ph_in[d, STEPS, at].astype(F32)
                    ph_out[d, s, at] = total.astype(BF16)
                src, dst = ph_out.at[d, s], ph_in.at[d, s]
                if s == last:
                    start((g, "rpd", d), src, ph_diag.at[d], diag[d])
            start((g, "rp", d, s), src, dst, ring[d])

    def q_block(g, step, at):
        n = NEAR_ORDER.index(step)
        return part[g, tz(step), y, at, LANES:] + qy_in[g, n, at].astype(F32)

    def scatter_q(g, s):
        for d in range(2):
            step = STEPS - s if d == 0 else s - STEPS
            arrived(g, "ry", step)
            if s > 0:
                arrived(g, "rq", d, s - 1)
            if s == 1:
                arrived(g, "rqf", d)
            for e in range(2):
                at = cut_of(e)
                total = q_block(g, step, at)
                if s > 0:
                    total = total + qz_in[g, d, s - 1, at].astype(F32)
                if s == 1 and e == d:
                    total = total + qz_in[g, d, STEPS, at].astype(F32)
                qz_out[g, d, s, at] = total.astype(BF16)
            start((g, "rq", d, s), qz_out.at[g, d, s], qz_in.at[g, d, s], ring[d])
        if s == 0:
            arrived(g, "ry", FAR)
            for d in range(2):
                at = cut_of(d)
                qz_out[g, d, STEPS, at] = q_block(g, FAR, at).astype(BF16)
                src, dst = qz_out.at[g, d, STEPS, at], qz_in.at[g, d, STEPS, at]
                start((g, "rqf", d), src, dst, ring2[d])

    def scatter_own(g):
        if g == 0:
            py_out[g] = part[g, z, 1 - y, :, :LANES].astype(BF16)
        else:
            py_out[g] = half_block(z, slice(0, chp)).astype(BF16)
        start((g, "py"), py_out.at[g], py_in.at[g], other)

    def finish_q(g):
        for d in range(2):
            arrived(g, "rq", d, last)
        arrived(g, "ry", 0)
        n = NEAR_ORDER.index(0)
        total = part[g, z, y, :, LANES:] + qy_in[g, n].astype(F32)
        return total + qz_in[g, 0, last].astype(F32) + qz_in[g, 1, last].astype(F32)

    def finish_p(g):
        arrived(g, "py")
        if g == 0:
            total = part[g, z, y, :, :LANES]
        else:
            total = half_block(z, slice(0, chp))
        total = total + py_in[g].astype(F32)
        for d in range(2):
            arrived(g, "rp", d, last)
            arrived(g, "rpd", d)
            if g == 0:
                total = total + pf_in[d, last, 0].astype(F32) + pf_in[d, last, 1].astype(F32)
            else:
                total = total + ph_in[d, last].astype(F32) + ph_diag[d].astype(F32)
        return total

    def restored(g):
        q = finish_q(g).astype(BF16)
        p = finish_p(g).astype(BF16)
        return across(place[g, :, :LANES], p) + across(place[g, :, LANES:], q)

    gather_begin(0)
    gather_own(0)
    make_block(1)
    gather_begin(1)
    gather_own(1)
    turn_columns()
    flatten_w()
    gather_step(0, 1)
    gather_step(1, 1)
    gather_pair(0)
    gather_pair(1)
    spread_w()
    gather_step(0, 2)
    gather_step(1, 2)
    split_w()
    make_spot()
    turn_p()
    gather_step(0, 3)
    expand_p(0)
    gather_step(1, 3)
    for d in NEAR_ORDER:
        arrived(0, "qy", d)
    expand_q(0)
    restore(0)
    expand_p(1)
    for d in NEAR_ORDER:
        arrived(1, "qy", d)
    expand_q(1)
    restore(1)
    convolve(0)
    convolve(1)
    complete(0)
    project(0)
    scatter_y(0, 3, -3, 4)
    scatter_p(0, 0)
    complete(1)
    project(1)
    scatter_y(1, 3, -3, 4)
    scatter_p(1, 0)
    scatter_y(0, 2, -2)
    scatter_q(0, 0)
    scatter_y(1, 2, -2)
    scatter_q(1, 0)
    scatter_p(0, 1)
    scatter_y(0, 1, -1)
    scatter_q(0, 1)
    scatter_p(1, 1)
    scatter_y(1, 1, -1)
    scatter_q(1, 1)
    scatter_y(0, 0)
    scatter_y(1, 0)
    scatter_own(0)
    scatter_own(1)
    for g in range(2):
        scatter_p(g, 2)
        scatter_q(g, 2)
    acc = restored(0)
    acc = acc + restored(1)
    out_ref[...] = acc[:, :ch].astype(BF16).reshape(out_ref.shape)
    for c in pending.values():
        c.wait_send()


def on_device(
    row_devices,
    latents,
    clip_height,
    clip_width,
    expand_weight,
    expand_bias,
    depth_weight,
    depth_bias,
    project_weight,
):
    batch, row_count, col_count, ch = latents.shape
    ff = expand_bias.shape[1]
    assert batch == 4 and row_count == 2 and col_count == HALF
    chp, ffp = ceil_to(ch, 16), ceil_to(ff, 16)
    spread = NY * NZ * chp

    vmem = pl.BlockSpec(memory_space=pltpu.VMEM)
    smem = pl.BlockSpec(memory_space=pltpu.SMEM)
    hbm = pl.BlockSpec(memory_space=pl.ANY)
    scratch = [
        pltpu.VMEM((ffp, 2, NY * NZ * ch), BF16),
        pltpu.VMEM((2 * ffp, spread + LANES), BF16),
        pltpu.VMEM((2 * ffp, spread), BF16),
        pltpu.VMEM((ff, NY * NZ * ch), BF16),
        pltpu.VMEM((NZ, NY, chp, ffp), BF16),
        pltpu.VMEM((LANES, ceil_to(ffp, LANES)), F32),
        pltpu.VMEM((ffp, LANES), F32),
        pltpu.VMEM((22, ffp, LANES), F32),
        pltpu.VMEM((2, batch * LANES, PAIR), BF16),
        pltpu.VMEM((2, PAIR, PAIR), BF16),
        pltpu.VMEM((NY, NZ, chp, LANES), BF16),
        pltpu.VMEM((NZ, chp, LANES), BF16),
        pltpu.VMEM((2, NY, NZ, chp, LANES), BF16),
        pltpu.VMEM((chp, LANES), BF16),
        pltpu.VMEM((chp, LANES), BF16),
        pltpu.VMEM((2, chp, LANES), BF16),
        pltpu.VMEM((2, chp, LANES), BF16),
        pltpu.VMEM((2 * ffp, PAIR), BF16),
        pltpu.VMEM((2, 2, ffp, PAIR), F32),
        pltpu.VMEM((2, 2, ffp, PAIR), F32),
        pltpu.VMEM((2, 3, 2, ffp, PAIR), F32),
        pltpu.VMEM((2, ffp, PAIR), BF16),
        pltpu.VMEM((2, ffp, PAIR), BF16),
        pltpu.VMEM((2, ffp, PAIR), BF16),
        pltpu.VMEM((2, ffp, PAIR), BF16),
        pltpu.VMEM((ffp, PAIR), BF16),
        pltpu.VMEM((ffp, PAIR), BF16),
        pltpu.VMEM((2, NZ, NY, chp, PAIR), F32),
        pltpu.VMEM((2, FAR, NY, chp, LANES), BF16),
        pltpu.VMEM((2, FAR, NY, chp, LANES), BF16),
        pltpu.VMEM((2, FAR, chp, LANES), BF16),
        pltpu.VMEM((2, FAR, chp, LANES), BF16),
        pltpu.VMEM((2, chp, LANES), BF16),
        pltpu.VMEM((2, 2, FAR, chp, LANES), BF16),
        pltpu.VMEM((2, 2, FAR, chp, LANES), BF16),
        pltpu.VMEM((2, NZ, chp, LANES), BF16),
        pltpu.VMEM((2, NZ, chp, LANES), BF16),
        pltpu.VMEM((2, chp, LANES), BF16),
        pltpu.VMEM((2, chp, LANES), BF16),
        pltpu.SemaphoreType.DMA((2,)),
        pltpu.SemaphoreType.DMA((128,)),
        pltpu.SemaphoreType.DMA((128,)),
    ]
    return pl.pallas_call(
        functools.partial(kernel, row_devices),
        out_shape=jax.ShapeDtypeStruct(latents.shape, BF16),
        in_specs=[vmem, smem, smem, hbm, vmem, vmem, vmem, hbm],
        out_specs=vmem,
        scratch_shapes=scratch,
        compiler_params=pltpu.CompilerParams(
            collective_id=0, has_side_effects=True, vmem_limit_bytes=60 * 1024 * 1024
        ),
    )(
        latents,
        clip_height,
        clip_width,
        expand_weight.transpose(2, 0, 1),
        expand_bias,
        depth_weight,
        depth_bias,
        project_weight,
    )


def solution(mesh):
    in_specs = (
        P(None, "row", None, "tensor"),
        P(),
        P(),
        P(None, None, "tensor"),
        P(None, "tensor"),
        P(None, None, None, "tensor"),
        P(None, "tensor"),
        P("tensor", None),
    )
    return jax.shard_map(
        functools.partial(on_device, mesh.shape["row"]),
        mesh=mesh,
        in_specs=in_specs,
        out_specs=P(None, "row", None, "tensor"),
        check_vma=False,
    )
```

```python
import functools

import jax
import jax.numpy as jnp
from jax import lax
from jax.experimental import pallas as pl
from jax.experimental.pallas import tpu as pltpu
from jax.sharding import PartitionSpec as P

MESH = pl.DeviceIdType.MESH
NY, NZ = 2, 8
FAR = NZ // 2
LANES = 128
HALF = LANES // 2
PAIR = 2 * LANES
BF16 = jnp.bfloat16
F32 = jnp.float32
NEAR_ORDER = (3, -3, 4, 2, -2, 1, -1, 0)
STEPS = FAR - 1


def ceil_to(n, m):
    return -(-n // m) * m


def silu(v):
    h = 0.5 * v
    return h + h * jnp.tanh(h)


def iota(shape, dim):
    return lax.broadcasted_iota(jnp.int32, shape, dim)


def one_hot(cond):
    return jnp.where(cond, 1.0, 0.0).astype(BF16)


def across(a, b):
    return lax.dot_general(a, b, (((1,), (1,)), ((), ())), preferred_element_type=F32)


def kernel(
    rows,
    x_ref,
    height_ref,
    width_ref,
    w_hbm,
    bias_ref,
    taps_ref,
    shift_ref,
    p_hbm,
    out_ref,
    w_raw,
    w_flat,
    w_ref,
    p_raw,
    p_ref,
    rows_s,
    cols_s,
    taps_s,
    place,
    spot,
    xp_full,
    xp_half,
    xq,
    hx_out,
    hx_in,
    hx_own,
    hx_diag,
    ec,
    ex,
    turned,
    sums,
    dn_out,
    up_out,
    dn_in,
    up_in,
    hid,
    hc,
    part,
    pf_out,
    pf_in,
    ph_out,
    ph_in,
    ph_diag,
    qz_out,
    qz_in,
    qy_out,
    qy_in,
    py_out,
    py_in,
    load,
    send,
    recv,
):
    r = lax.axis_index("row")
    t = lax.axis_index("tensor")
    y, z = t // NZ, t % NZ
    clips, row_count, col_count, ch = x_ref.shape
    ff, ffp, chp = bias_ref.shape[1], ex.shape[2], xq.shape[3]
    wide, spread = NY * NZ * ch, NY * NZ * chp
    cut = ceil_to(chp // 2, 16)

    def tz(step):
        return (z + NZ + step) % NZ

    ring = ({"tensor": y * NZ + tz(1)}, {"tensor": y * NZ + tz(-1)})
    ring2 = ({"tensor": y * NZ + tz(2)}, {"tensor": y * NZ + tz(-2)})
    other = {"tensor": (1 - y) * NZ + z}
    diag = ({"tensor": (1 - y) * NZ + tz(1)}, {"tensor": (1 - y) * NZ + tz(-1)})
    above = {"row": (r + rows - 1) % rows}
    below = {"row": (r + 1) % rows}

    w_load = pltpu.make_async_copy(w_hbm, w_raw.at[pl.ds(0, ff)], load.at[0])
    p_load = pltpu.make_async_copy(p_hbm, p_raw, load.at[1])
    w_load.start()
    p_load.start()

    barrier = pltpu.get_barrier_semaphore()
    for target in ring + ring2 + diag + (other, above, below):
        pl.semaphore_signal(barrier, inc=1, device_id=target, device_id_type=MESH)

    pending = {}

    def start(key, src, dst, target):
        n = len(pending)
        c = pltpu.make_async_remote_copy(
            src_ref=src,
            dst_ref=dst,
            send_sem=send.at[n],
            recv_sem=recv.at[n],
            device_id=target,
            device_id_type=MESH,
        )
        c.start()
        pending[key] = c

    def same(key, ref, target):
        start(key, ref, ref, target)

    def arrived(*key):
        pending[key].wait_recv()

    widths = [width_ref[b] for b in range(clips)]
    heights = [height_ref[b] for b in range(clips)]
    narrow = jnp.int32(clips - 1)
    for b in reversed(range(clips - 1)):
        narrow = jnp.where(widths[b] == col_count // 2, b, narrow)
    slots = [jnp.where(narrow == b, clips - 1, jnp.where(narrow < b, b - 1, b)) for b in range(clips)]

    def of_slot(s, values):
        total = jnp.int32(0)
        for b in range(clips):
            total = total + jnp.where(slots[b] == s, values[b], 0)
        return total

    slot_w = [of_slot(s, widths) for s in range(clips)]
    slot_h = [of_slot(s, heights) for s in range(clips)]

    sub, lane2 = iota((LANES, PAIR), 0), iota((LANES, PAIR), 1)
    sub_row, sub_col = sub // HALF, sub % HALF
    canvas_row = row_count * r + sub_row

    def make_place(g):
        for b in range(clips):
            limit = jnp.where(slots[b] // 2 == g, widths[b], 0)
            first_slot = jnp.where(slots[b] == 2 * g + 1, 2 * slot_w[2 * g], 0)
            a = first_slot + sub_row * widths[b] + sub_col
            if g == 1:
                a = jnp.where(a < HALF, a + HALF * y, a + HALF)
            ok = (sub_col < limit) & (canvas_row < heights[b])
            place[g, b * LANES : (b + 1) * LANES] = one_hot(ok & (lane2 == a))

    def make_spot():
        for g in range(2):
            for s in range(2):
                w, h = slot_w[2 * g + s], slot_h[2 * g + s]
                a = s * 2 * slot_w[2 * g] + sub_row * w + sub_col
                ok = (sub_col < w) & (canvas_row < h)
                if g == 0:
                    hit = lane2 == a
                else:
                    hit = (lane2 == a + HALF) | ((a < HALF) & (lane2 == a))
                spot[g, s * LANES : (s + 1) * LANES] = one_hot(ok & hit)

    tokens = x_ref[...].reshape(clips * LANES, ch).T

    def make_block(g):
        make_place(g)
        block = jnp.dot(tokens, place[g], preferred_element_type=F32).astype(BF16)
        empty = jnp.zeros((chp - ch, LANES), BF16)
        if g == 0:
            xp_full[y, z, 0:ch] = block[:, :LANES]
            xp_full[y, z, ch:chp] = empty
        else:
            hx_out[0:ch] = block[:, :LANES]
            hx_out[ch:chp] = empty
        xq[g, y, z, 0:ch] = block[:, LANES:]
        xq[g, y, z, ch:chp] = empty

    make_block(0)
    pl.semaphore_wait(barrier, 9)

    def gather_begin(g):
        for d in range(2):
            if g == 0:
                same((g, "own", d), xp_full.at[y, z], ring[d])
            else:
                start((g, "own", d), hx_out, hx_own.at[d], ring[d])
        for d in range(2):
            if g == 0:
                same((g, "p", d, 0), xp_full.at[y, z], diag[d])
            else:
                start((g, "p", d, 0), hx_out, hx_diag.at[d], diag[d])
        for d in range(2):
            same((g, "q", d, 0), xq.at[g, y, z], ring[d])

    def gather_own(g):
        if g == 0:
            same((g, "y"), xp_full.at[y, z], other)
        else:
            start((g, "y"), hx_out, hx_in, other)
        same((g, "qy", 0), xq.at[g, y, z], other)

    def gather_pair(g):
        arrived(g, "y")
        if g == 1:
            xp_half[z] = hx_out[...] + hx_in[...]

    def cut_at(d):
        return pl.ds(0, cut) if d == 0 else pl.ds(cut, chp - cut)

    def gather_step(g, s):
        for d in range(2):
            zz = tz(-s if d == 0 else s)
            arrived(g, "p", d, s - 1)
            if s == 1:
                arrived(g, "own", d)
                if g == 1:
                    xp_half[zz] = hx_own[d] + hx_diag[d]
            if s < STEPS:
                src = xp_full.at[:, zz] if g == 0 else xp_half.at[zz]
                same((g, "p", d, s), src, ring[d])
            if s == 2:
                src = xp_full.at[d, zz] if g == 0 else xp_half.at[zz, cut_at(d)]
                same((g, "pf", d), src, ring2[d])
        for d in range(2):
            zz = tz(-s if d == 0 else s)
            arrived(g, "q", d, s - 1)
            if s < STEPS:
                same((g, "q", d, s), xq.at[g, y, zz], ring[d])
            if s == 2:
                same((g, "qf", d), xq.at[g, y, zz, cut_at(d)], ring2[d])
            same((g, "qy", -s if d == 0 else s), xq.at[g, y, zz], other)
        if s == STEPS:
            for d in range(2):
                arrived(g, "qf", d)
            same((g, "qy", FAR), xq.at[g, y, tz(FAR)], other)
            for d in range(2):
                arrived(g, "pf", d)

    def flatten_w():
        w_flat[:, wide:] = jnp.zeros((2 * ffp, w_flat.shape[1] - wide), BF16)
        w_load.wait()
        w_raw[ff:ffp] = jnp.zeros((ffp - ff, 2, wide), BF16)

        def body(i, _):
            dst = pl.ds(pl.multiple_of(i * 32, 32), 32)
            w_flat[dst, 0:wide] = w_raw[pl.ds(i * 16, 16)].reshape(32, wide)
            return 0

        lax.fori_loop(0, ffp // 16, body, 0)

    def spread_w():
        for j in range(spread // LANES):
            c = LANES * j + iota((PAIR, LANES), 1)
            begin = LANES * j - (chp - ch) * (LANES * j // chp)
            base = begin // LANES * LANES
            p = base + iota((PAIR, LANES), 0)
            owner = c // chp
            pick = one_hot((p == c - (chp - ch) * owner) & (c - chp * owner < ch))
            moved = jnp.dot(w_flat[:, base : base + PAIR], pick, preferred_element_type=F32)
            w_ref[:, LANES * j : LANES * (j + 1)] = moved.astype(BF16)

    def split_w():
        to, at = iota((2 * ffp, 2 * ffp), 0), iota((2 * ffp, 2 * ffp), 1)
        pick = one_hot(at == jnp.where(to < ffp, 2 * to, 2 * (to - ffp) + 1))
        for n in range(spread // PAIR):
            sl = slice(PAIR * n, PAIR * (n + 1))
            w_ref[:, sl] = jnp.dot(pick, w_ref[:, sl], preferred_element_type=F32).astype(BF16)

    def turn_p():
        p_ref[...] = jnp.zeros_like(p_ref)
        p_load.wait()
        for zz in range(NZ):
            for yy in range(NY):
                o = yy * NZ + zz
                p_ref[zz, yy, 0:ch, 0:ff] = p_raw[:, ch * o : ch * (o + 1)].T

    def turn_columns():
        rows_s[...] = jnp.zeros_like(rows_s)
        rows_s[0:2, 0:ff] = bias_ref[...]
        rows_s[2:4, 0:ff] = shift_ref[...]
        for i in range(3):
            for j in range(3):
                n = 4 + 2 * (3 * i + j)
                rows_s[n : n + 2, 0:ff] = taps_ref[i, j]
        cols_s[...] = rows_s[...].T[:ffp]

        def wide_col(n):
            return jnp.broadcast_to(cols_s[:, n : n + 1], (ffp, LANES))

        for n in range(4):
            taps_s[n] = wide_col(n)
        for m in range(6):
            above_tap, below_tap = wide_col(4 + m), wide_col(16 + m)
            taps_s[4 + m] = wide_col(10 + m)
            taps_s[10 + m] = jnp.where(first, below_tap, above_tap)
            taps_s[16 + m] = jnp.where(first, above_tap, below_tap)

    lane = iota((1, LANES), 1)
    first = lane < HALF
    col = lane % HALF
    left_ok = col > 0
    right_ok = col < HALF - 1
    edge_row = row_count * r + jnp.where(first, -1, row_count)
    edge_ok = (edge_row >= 0) & (edge_row < rows * row_count)

    def expand_p(g):
        if g == 0:
            x = xp_full[...].reshape(spread, LANES)
            pre = jnp.dot(w_ref[...], x, preferred_element_type=F32)
        else:
            x = xp_half[...].reshape(spread // 2, LANES)
            pre = jnp.dot(w_ref[:, : spread // 2], x, preferred_element_type=F32)
            more = jnp.dot(w_ref[:, spread // 2 :], x, preferred_element_type=F32)
            pre = jnp.where(first, pre + pltpu.roll(more, HALF, 1), 0.0)
        for k in range(2):
            value = silu(pre[k * ffp : (k + 1) * ffp] + taps_s[k])
            if g == 1:
                value = jnp.where(first, value, 0.0)
            ec[k * ffp : (k + 1) * ffp, :LANES] = value.astype(BF16)

    def expand_q(g):
        x = xq[g].reshape(spread, LANES)
        pre = jnp.dot(w_ref[...], x, preferred_element_type=F32)
        for k in range(2):
            value = silu(pre[k * ffp : (k + 1) * ffp] + taps_s[k])
            ec[k * ffp : (k + 1) * ffp, LANES:] = value.astype(BF16)

    def restore(g):
        for k in range(2):
            ex[g, k] = across(ec[k * ffp : (k + 1) * ffp], spot[g])

        def body(i, _):
            at = pl.ds(pl.multiple_of(i * 16, 16), 16)
            for s in range(2):
                sl = slice(s * LANES, (s + 1) * LANES)
                e0, e1 = ex[g, 0, at, sl], ex[g, 1, at, sl]
                t0, t1 = pltpu.roll(e0, HALF, 1), pltpu.roll(e1, HALF, 1)
                turned[g, 0, at, sl] = t0
                turned[g, 1, at, sl] = t1
                dn_out[g, at, sl] = jnp.where(first, t0, e1).astype(BF16)
                up_out[g, at, sl] = jnp.where(first, e0, t1).astype(BF16)
            return 0

        lax.fori_loop(0, ffp // 16, body, 0, unroll=11)
        start((g, "dn"), dn_out.at[g], dn_in.at[g], below)
        start((g, "up"), up_out.at[g], up_in.at[g], above)

    def convolve(g):
        def body(i, _):
            at = pl.ds(pl.multiple_of(i * 16, 16), 16)
            for k in range(2):
                for s in range(2):
                    sl = slice(s * LANES, (s + 1) * LANES)
                    mid, swap = ex[g, k, at, sl], turned[g, k, at, sl]
                    for j in range(3):
                        n = 2 * j + k
                        total = taps_s[4 + n, at] * mid + taps_s[10 + n, at] * swap
                        sums[g, j, k, at, sl] = total
            return 0

        lax.fori_loop(0, ffp // 16, body, 0, unroll=2)

    def complete(g):
        arrived(g, "dn")
        arrived(g, "up")

        def body(i, _):
            at = pl.ds(pl.multiple_of(i * 16, 16), 16)
            for s in range(2):
                sl = slice(s * LANES, (s + 1) * LANES)
                dn, up = dn_in[g, at, sl].astype(F32), up_in[g, at, sl].astype(F32)
                edges = (
                    jnp.where(first, dn, pltpu.roll(up, HALF, 1)),
                    jnp.where(first, pltpu.roll(dn, HALF, 1), up),
                )
                outs = []
                for k in range(2):
                    edge = jnp.where(edge_ok, edges[k], 0.0)
                    got = [sums[g, j, k, at, sl] + taps_s[16 + 2 * j + k, at] * edge for j in range(3)]
                    res = got[1] + taps_s[2 + k, at]
                    res = res + jnp.where(left_ok, pltpu.roll(got[0], 1, 1), 0.0)
                    res = res + jnp.where(right_ok, pltpu.roll(got[2], LANES - 1, 1), 0.0)
                    outs.append(res)
                hid[at, sl] = (outs[0] * silu(outs[1])).astype(BF16)
            return 0

        lax.fori_loop(0, ffp // 16, body, 0, unroll=4)

    def project(g):
        hc[...] = jnp.dot(hid[...], spot[g], preferred_element_type=F32).astype(BF16)
        p = p_ref[...].reshape(spread, ffp)
        part[g] = jnp.dot(p, hc[...], preferred_element_type=F32).reshape(NZ, NY, chp, PAIR)

    def scatter_y(g, *steps):
        for d in steps:
            n = NEAR_ORDER.index(d)
            qy_out[g, n] = part[g, tz(d), 1 - y, :, LANES:].astype(BF16)
            start((g, "ry", d), qy_out.at[g, n], qy_in.at[g, n], other)

    last = STEPS - 1

    def cut_of(d):
        return slice(0, cut) if d == 0 else slice(cut, chp)

    def half_block(zz, at):
        return jnp.where(first, part[1, zz, 0, at, :LANES], part[1, zz, 1, at, :LANES])

    def scatter_p(g, s):
        for d in range(2):
            zz = tz(STEPS - s if d == 0 else s - STEPS)
            near = cut_of(d)
            if s == 0:
                if g == 0:
                    pf_out[d, STEPS, d] = part[0, tz(FAR), d, :, :LANES].astype(BF16)
                    src, dst = pf_out.at[d, STEPS, d], pf_in.at[d, STEPS, d]
                else:
                    ph_out[d, STEPS, near] = half_block(tz(FAR), near).astype(BF16)
                    src, dst = ph_out.at[d, STEPS, near], ph_in.at[d, STEPS, near]
                start((g, "rpf", d), src, dst, ring2[d])
            if s > 0:
                arrived(g, "rp", d, s - 1)
            if s == 1:
                arrived(g, "rpf", d)
            if g == 0:
                for yy in range(NY):
                    total = part[0, zz, yy, :, :LANES]
                    if s > 0:
                        total = total + pf_in[d, s - 1, yy].astype(F32)
                    if s == 1 and yy == d:
                        total = total + pf_in[d, STEPS, yy].astype(F32)
                    pf_out[d, s, yy] = total.astype(BF16)
                if s < last:
                    src, dst = pf_out.at[d, s], pf_in.at[d, s]
                else:
                    src, dst = pf_out.at[d, s, 1 - y], pf_in.at[d, s, 1]
                    start((g, "rpd", d), src, dst, diag[d])
                    src, dst = pf_out.at[d, s, y], pf_in.at[d, s, 0]
            else:
                for e in range(2):
                    at = cut_of(e)
                    total = half_block(zz, at)
                    if s > 0:
                        total = total + ph_in[d, s - 1, at].astype(F32)
                    if s == 1 and e == d:
                        total = total + ph_in[d, STEPS, at].astype(F32)
                    ph_out[d, s, at] = total.astype(BF16)
                src, dst = ph_out.at[d, s], ph_in.at[d, s]
                if s == last:
                    start((g, "rpd", d), src, ph_diag.at[d], diag[d])
            start((g, "rp", d, s), src, dst, ring[d])

    def q_block(g, step, at):
        n = NEAR_ORDER.index(step)
        return part[g, tz(step), y, at, LANES:] + qy_in[g, n, at].astype(F32)

    def scatter_q(g, s):
        for d in range(2):
            step = STEPS - s if d == 0 else s - STEPS
            arrived(g, "ry", step)
            if s > 0:
                arrived(g, "rq", d, s - 1)
            if s == 1:
                arrived(g, "rqf", d)
            for e in range(2):
                at = cut_of(e)
                total = q_block(g, step, at)
                if s > 0:
                    total = total + qz_in[g, d, s - 1, at].astype(F32)
                if s == 1 and e == d:
                    total = total + qz_in[g, d, STEPS, at].astype(F32)
                qz_out[g, d, s, at] = total.astype(BF16)
            start((g, "rq", d, s), qz_out.at[g, d, s], qz_in.at[g, d, s], ring[d])
        if s == 0:
            arrived(g, "ry", FAR)
            for d in range(2):
                at = cut_of(d)
                qz_out[g, d, STEPS, at] = q_block(g, FAR, at).astype(BF16)
                src, dst = qz_out.at[g, d, STEPS, at], qz_in.at[g, d, STEPS, at]
                start((g, "rqf", d), src, dst, ring2[d])

    def scatter_own(g):
        if g == 0:
            py_out[g] = part[g, z, 1 - y, :, :LANES].astype(BF16)
        else:
            py_out[g] = half_block(z, slice(0, chp)).astype(BF16)
        start((g, "py"), py_out.at[g], py_in.at[g], other)

    def finish_q(g):
        for d in range(2):
            arrived(g, "rq", d, last)
        arrived(g, "ry", 0)
        n = NEAR_ORDER.index(0)
        total = part[g, z, y, :, LANES:] + qy_in[g, n].astype(F32)
        return total + qz_in[g, 0, last].astype(F32) + qz_in[g, 1, last].astype(F32)

    def finish_p(g):
        arrived(g, "py")
        if g == 0:
            total = part[g, z, y, :, :LANES]
        else:
            total = half_block(z, slice(0, chp))
        total = total + py_in[g].astype(F32)
        for d in range(2):
            arrived(g, "rp", d, last)
            arrived(g, "rpd", d)
            if g == 0:
                total = total + pf_in[d, last, 0].astype(F32) + pf_in[d, last, 1].astype(F32)
            else:
                total = total + ph_in[d, last].astype(F32) + ph_diag[d].astype(F32)
        return total

    def restored(g):
        q = finish_q(g).astype(BF16)
        p = finish_p(g).astype(BF16)
        return across(place[g, :, :LANES], p) + across(place[g, :, LANES:], q)

    gather_begin(0)
    gather_own(0)
    make_block(1)
    gather_begin(1)
    gather_own(1)
    turn_columns()
    flatten_w()
    gather_step(0, 1)
    gather_step(1, 1)
    gather_pair(0)
    gather_pair(1)
    spread_w()
    gather_step(0, 2)
    gather_step(1, 2)
    split_w()
    make_spot()
    turn_p()
    gather_step(0, 3)
    expand_p(0)
    gather_step(1, 3)
    for d in NEAR_ORDER:
        arrived(0, "qy", d)
    expand_q(0)
    restore(0)
    expand_p(1)
    for d in NEAR_ORDER:
        arrived(1, "qy", d)
    expand_q(1)
    restore(1)
    convolve(0)
    convolve(1)
    complete(0)
    project(0)
    scatter_p(0, 0)
    scatter_y(0, 3, -3, 4)
    complete(1)
    project(1)
    scatter_p(1, 0)
    scatter_y(1, 3, -3, 4)
    scatter_y(0, 2, -2)
    scatter_q(0, 0)
    scatter_y(1, 2, -2)
    scatter_q(1, 0)
    scatter_p(0, 1)
    scatter_y(0, 1, -1)
    scatter_q(0, 1)
    scatter_p(1, 1)
    scatter_y(1, 1, -1)
    scatter_q(1, 1)
    scatter_y(0, 0)
    scatter_y(1, 0)
    scatter_own(0)
    scatter_own(1)
    for g in range(2):
        scatter_p(g, 2)
        scatter_q(g, 2)
    acc = restored(0)
    acc = acc + restored(1)
    out_ref[...] = acc[:, :ch].astype(BF16).reshape(out_ref.shape)
    for c in pending.values():
        c.wait_send()


def on_device(
    row_devices,
    latents,
    clip_height,
    clip_width,
    expand_weight,
    expand_bias,
    depth_weight,
    depth_bias,
    project_weight,
):
    batch, row_count, col_count, ch = latents.shape
    ff = expand_bias.shape[1]
    assert batch == 4 and row_count == 2 and col_count == HALF
    chp, ffp = ceil_to(ch, 16), ceil_to(ff, 16)
    spread = NY * NZ * chp

    vmem = pl.BlockSpec(memory_space=pltpu.VMEM)
    smem = pl.BlockSpec(memory_space=pltpu.SMEM)
    hbm = pl.BlockSpec(memory_space=pl.ANY)
    scratch = [
        pltpu.VMEM((ffp, 2, NY * NZ * ch), BF16),
        pltpu.VMEM((2 * ffp, spread + LANES), BF16),
        pltpu.VMEM((2 * ffp, spread), BF16),
        pltpu.VMEM((ff, NY * NZ * ch), BF16),
        pltpu.VMEM((NZ, NY, chp, ffp), BF16),
        pltpu.VMEM((LANES, ceil_to(ffp, LANES)), F32),
        pltpu.VMEM((ffp, LANES), F32),
        pltpu.VMEM((22, ffp, LANES), F32),
        pltpu.VMEM((2, batch * LANES, PAIR), BF16),
        pltpu.VMEM((2, PAIR, PAIR), BF16),
        pltpu.VMEM((NY, NZ, chp, LANES), BF16),
        pltpu.VMEM((NZ, chp, LANES), BF16),
        pltpu.VMEM((2, NY, NZ, chp, LANES), BF16),
        pltpu.VMEM((chp, LANES), BF16),
        pltpu.VMEM((chp, LANES), BF16),
        pltpu.VMEM((2, chp, LANES), BF16),
        pltpu.VMEM((2, chp, LANES), BF16),
        pltpu.VMEM((2 * ffp, PAIR), BF16),
        pltpu.VMEM((2, 2, ffp, PAIR), F32),
        pltpu.VMEM((2, 2, ffp, PAIR), F32),
        pltpu.VMEM((2, 3, 2, ffp, PAIR), F32),
        pltpu.VMEM((2, ffp, PAIR), BF16),
        pltpu.VMEM((2, ffp, PAIR), BF16),
        pltpu.VMEM((2, ffp, PAIR), BF16),
        pltpu.VMEM((2, ffp, PAIR), BF16),
        pltpu.VMEM((ffp, PAIR), BF16),
        pltpu.VMEM((ffp, PAIR), BF16),
        pltpu.VMEM((2, NZ, NY, chp, PAIR), F32),
        pltpu.VMEM((2, FAR, NY, chp, LANES), BF16),
        pltpu.VMEM((2, FAR, NY, chp, LANES), BF16),
        pltpu.VMEM((2, FAR, chp, LANES), BF16),
        pltpu.VMEM((2, FAR, chp, LANES), BF16),
        pltpu.VMEM((2, chp, LANES), BF16),
        pltpu.VMEM((2, 2, FAR, chp, LANES), BF16),
        pltpu.VMEM((2, 2, FAR, chp, LANES), BF16),
        pltpu.VMEM((2, NZ, chp, LANES), BF16),
        pltpu.VMEM((2, NZ, chp, LANES), BF16),
        pltpu.VMEM((2, chp, LANES), BF16),
        pltpu.VMEM((2, chp, LANES), BF16),
        pltpu.SemaphoreType.DMA((2,)),
        pltpu.SemaphoreType.DMA((128,)),
        pltpu.SemaphoreType.DMA((128,)),
    ]
    return pl.pallas_call(
        functools.partial(kernel, row_devices),
        out_shape=jax.ShapeDtypeStruct(latents.shape, BF16),
        in_specs=[vmem, smem, smem, hbm, vmem, vmem, vmem, hbm],
        out_specs=vmem,
        scratch_shapes=scratch,
        compiler_params=pltpu.CompilerParams(
            collective_id=0, has_side_effects=True, vmem_limit_bytes=60 * 1024 * 1024
        ),
    )(
        latents,
        clip_height,
        clip_width,
        expand_weight.transpose(2, 0, 1),
        expand_bias,
        depth_weight,
        depth_bias,
        project_weight,
    )


def solution(mesh):
    in_specs = (
        P(None, "row", None, "tensor"),
        P(),
        P(),
        P(None, None, "tensor"),
        P(None, "tensor"),
        P(None, None, None, "tensor"),
        P(None, "tensor"),
        P("tensor", None),
    )
    return jax.shard_map(
        functools.partial(on_device, mesh.shape["row"]),
        mesh=mesh,
        in_specs=in_specs,
        out_specs=P(None, "row", None, "tensor"),
        check_vma=False,
    )
```
